128 devices in a mesh: atom: 16 (over x_hi, y, core), mode: 8 (over x_lo, z).
Axes of the slice: x: 4 (x_hi: 2, x_lo: 2; x = x_hi * 2 + x_lo), y: 4, z: 4, core: 2. Of those that a mesh axis runs over, the one named last changes fastest.
Arguments:
- features: float32 [128, 16384], P(None, 'atom'), may hold values from -6 to 6
- positions: float32 [3, 16384], P(None, 'atom'), may hold values from 0 to 1, as said below
- wavevectors: int32 [3, 8192], P(None, 'mode'), may hold values from -768 to 768, as said below
- mode_filter: float32 [128, 8192], P(None, 'mode'), may hold values from -12 to 12
- radial_mix: float32 [4, 128, 128], replicated, may hold values from -0.03125 to 0.03125
- radial_rates: float32 [4], replicated, may hold values from 0.2 to 3
- neighbour_ids: int32 [128, 5], P(('atom', 'mode')), may hold values from 0 to 127, as said below
- live_counts: int32 [128], P(('atom', 'mode')), may hold values from 1 to 5, as said below
- cotangent: float32 [128, 16384], P(None, ('atom', 'mode')), may hold values from -6 to 6
Outputs:
- layer_out: float32 [128, 16384], P(None, ('atom', 'mode'))
- grad_features: float32 [128, 16384], P(None, ('atom', 'mode'))
- grad_filter: float32 [128, 8192], P(None, 'mode')
The draws below stay inside these ranges and needn't reach their ends.
Inputs may be any that keep to these rules, and one draw needn't show every extreme that they name: `positions`: row 0 of atom i lies between b / 128 and (b + 1) / 128, with b = i // 128; rows 1 and 2 lie anywhere in the range. `wavevectors`: row 0 lies between -768 and 768; rows 1 and 2 lie between -12 and 12. `neighbour_ids`: row b lists the 5 blocks (b + o) mod 128, o from -2 to 2, each once, in some order; only the first live_counts[b] slots are live. `live_counts`: some block has all 5 slots live.
All inputs are finite; a program needn't handle non-finite values.
Results may differ from the reference program's by a relative error of at most 0.00035.
Values sent between devices are 32-bit elements; how exact they have to be, the bound alone decides.
No kernel may reach another device: no remote copies, remote signals or barrier semaphores. Data moves between devices by JAX's collectives and lax.ppermute only.
A program may use at most 64 MiB of HBM per device.

```python
import math
import jax
import jax.numpy as jnp
from jax import lax

C = 128
MODES = 8192
RADIAL = 4
BLOCK = 128
REACH = 2
ATOM_DEV = 1024
SLOTS = 5
ATOMS = 16384
NBLK = 128


def neighbour_plan(key):
    order_key = jax.random.fold_in(key, 11)
    first_key = jax.random.fold_in(key, 12)
    second_key = jax.random.fold_in(key, 13)
    shift_key = jax.random.fold_in(key, 14)
    scores = jax.random.randint(order_key, (NBLK, SLOTS), 0, 1000) * SLOTS + jnp.arange(SLOTS, dtype=jnp.int32)[None, :]
    ordering = jnp.argsort(scores, axis=1, stable=True).astype(jnp.int32)
    block_numbers = jnp.arange(NBLK, dtype=jnp.int32)
    neighbours = jnp.mod(block_numbers[:, None] + ordering - REACH, NBLK).astype(jnp.int32)
    first_draw = jax.random.randint(first_key, (NBLK,), 0, SLOTS)
    second_draw = jax.random.randint(second_key, (NBLK,), 0, SLOTS)
    shifted = jax.random.randint(shift_key, (), 0, NBLK)
    dense = jnp.mod(block_numbers + shifted, NBLK) < NBLK // 2
    counted = 1 + jnp.where(dense, jnp.maximum(first_draw, second_draw), jnp.minimum(first_draw, second_draw))
    counted = jnp.where(jnp.mod(block_numbers + shifted, NBLK) == 0, SLOTS, counted).astype(jnp.int32)
    return (neighbours, counted)


def draw_neighbour_ids(key, part):
    neighbours, counted = neighbour_plan(key)
    return neighbours


def draw_live_counts(key, part):
    neighbours, counted = neighbour_plan(key)
    return counted


def draw_wavevectors(key, part):
    long_key = jax.random.fold_in(key, 31)
    cross_key = jax.random.fold_in(key, 32)
    along = jax.random.randint(long_key, (1, MODES), -6 * NBLK, 6 * NBLK + 1)
    across = jax.random.randint(cross_key, (2, MODES), -12, 13)
    return jnp.concatenate([along, across], axis=0).astype(jnp.int32)


def draw_positions(key, part):
    inside_key = jax.random.fold_in(key, 21)
    cross_key = jax.random.fold_in(key, 22)
    inside = jax.random.uniform(inside_key, (ATOMS,), jnp.float32)
    cross = jax.random.uniform(cross_key, (2, ATOMS), jnp.float32)
    block_of = (jnp.arange(ATOMS, dtype=jnp.int32) // BLOCK).astype(jnp.float32)
    first_row = jnp.minimum((block_of + inside) / NBLK, 0.9999999)
    return jnp.concatenate([first_row[None, :], cross], axis=0).astype(jnp.float32)


def level_of(stream_key, dims, pieces, least, largest):
    factor_of = 1.0
    for dim, blocks in pieces:
        heights = jax.random.uniform(jax.random.fold_in(jax.random.fold_in(stream_key, 6), dim), (blocks,), jnp.float32, least / len(pieces), largest / len(pieces))
        factor_of = factor_of * jnp.repeat(jnp.exp(heights), dims[dim] // blocks).reshape((-1,) + (1,) * (len(dims) - 1 - dim))
    return factor_of


def bell_draw(key, dims, scale, bound, cuts=(), held_as=jnp.bfloat16):
    array = scale * jax.random.normal(key, dims, jnp.float32)
    if cuts:
        array = array * level_of(key, dims, cuts, -0.22, 0.18)
    return jnp.clip(array, -bound, bound).astype(held_as)


def setup_inputs(seed: int = 0) -> dict:
    key_list = jax.random.split(jax.random.key(seed), 10)
    return {
        "features": bell_draw(key_list[0], (C, ATOMS), 1.0, 6.0, ((1, 16),), jnp.float32),
        "positions": draw_positions(jax.random.fold_in(key_list[9], 71), 0),
        "wavevectors": draw_wavevectors(jax.random.fold_in(key_list[9], 71), 0),
        "mode_filter": bell_draw(key_list[3], (C, MODES), 2.0, 12.0, ((1, 8),), jnp.float32),
        "radial_mix": bell_draw(key_list[4], (RADIAL, C, C), (RADIAL * C * 64) ** -0.5, 0.03125, (), jnp.float32),
        "radial_rates": jnp.clip(jnp.exp(jax.random.uniform(key_list[5], (RADIAL,), jnp.float32, math.log(0.2), math.log(3.0))), 0.2, 3.0),
        "neighbour_ids": draw_neighbour_ids(jax.random.fold_in(key_list[9], 71), 0),
        "live_counts": draw_live_counts(jax.random.fold_in(key_list[9], 71), 0),
        "cotangent": bell_draw(key_list[8], (C, ATOMS), 1.0, 6.0, ((1, 128),), jnp.float32),
    }


def wave_tables(coords, wavevectors):
    wave_float = wavevectors.astype(jnp.float32)
    phases = 2.0 * jnp.pi * (coords[0][:, None] * wave_float[0][None, :] + coords[1][:, None] * wave_float[1][None, :] + coords[2][:, None] * wave_float[2][None, :])
    return jnp.cos(phases), jnp.sin(phases)


def pair_weights(own_coords, other_coords, radial_rates, total_blocks, live_mask):
    lengths = (total_blocks / jnp.pi, 2.0 / jnp.pi, 2.0 / jnp.pi)
    squared = None
    for axis_number in range(3):
        difference = own_coords[axis_number][:, None, :, None] - other_coords[axis_number][:, :, None, :]
        term = (lengths[axis_number] * jnp.sin(jnp.pi * difference)) ** 2
        squared = term if squared is None else squared + term
    return jnp.exp(-radial_rates[:, None, None, None, None] * squared[None]) * live_mask[None, :, :, None, None]


def matmul_exact(left, right):
    return jnp.dot(left, right, precision=lax.Precision.HIGHEST, preferred_element_type=jnp.float32)


def general_exact(left, right):
    return lax.dot_general(left, right, (((1,), (1,)), ((), ())), precision=lax.Precision.HIGHEST, preferred_element_type=jnp.float32)


def reference(features, positions, wavevectors, mode_filter, radial_mix, radial_rates, neighbour_ids, live_counts, cotangent):
    channels, atoms_total = features.shape
    inverse_count = 1.0 / atoms_total
    group_rows = ATOM_DEV
    group_count = atoms_total // group_rows
    feat_groups = features.reshape(channels, group_count, group_rows).transpose(1, 0, 2)
    cot_groups = cotangent.reshape(channels, group_count, group_rows).transpose(1, 0, 2)
    pos_groups = positions.reshape(3, group_count, group_rows).transpose(1, 0, 2)

    def accumulate(totals, inputs):
        feat_part, cot_part, pos_part = inputs
        cosines, sines = wave_tables(pos_part, wavevectors)
        return (totals[0] + matmul_exact(feat_part, cosines), totals[1] + matmul_exact(feat_part, sines), totals[2] + matmul_exact(cot_part, cosines), totals[3] + matmul_exact(cot_part, sines)), None

    zero_sums = jnp.zeros((channels, MODES), jnp.float32)
    sums, _ = lax.scan(accumulate, (zero_sums, zero_sums, zero_sums, zero_sums), (feat_groups, cot_groups, pos_groups))
    cos_sums, sin_sums, cot_cos, cot_sin = sums
    filt_cos = mode_filter * cos_sums * inverse_count
    filt_sin = mode_filter * sin_sums * inverse_count
    back_cos = mode_filter * cot_cos * inverse_count
    back_sin = mode_filter * cot_sin * inverse_count
    grad_filter = (cos_sums * cot_cos + sin_sums * cot_sin) * inverse_count

    def give_back(pos_part):
        cosines, sines = wave_tables(pos_part, wavevectors)
        return (general_exact(filt_cos, cosines) + general_exact(filt_sin, sines), general_exact(back_cos, cosines) + general_exact(back_sin, sines))

    long_groups, back_groups = lax.map(give_back, pos_groups)
    long_range = long_groups.transpose(1, 0, 2).reshape(channels, atoms_total)
    back_long = back_groups.transpose(1, 0, 2).reshape(channels, atoms_total)

    block_count = atoms_total // BLOCK
    blocks = features.reshape(channels, block_count, BLOCK)
    coord_blocks = positions.reshape(3, block_count, BLOCK)
    flat_ids = neighbour_ids.reshape(-1).astype(jnp.int32)
    nearby_feat = jnp.take(blocks, flat_ids, axis=1).reshape(channels, block_count, SLOTS, BLOCK)
    nearby_coord = jnp.take(coord_blocks, flat_ids, axis=1).reshape(3, block_count, SLOTS, BLOCK)
    live_mask = (jnp.arange(SLOTS, dtype=jnp.int32)[None, :] < live_counts[:, None]).astype(jnp.float32)
    weights = pair_weights(coord_blocks, nearby_coord, radial_rates, block_count, live_mask)
    gathered = jnp.einsum('cosj,rosij->rcoi', nearby_feat, weights, precision=lax.Precision.HIGHEST)
    short_range = jnp.einsum('rdc,rdoi->coi', radial_mix, gathered, precision=lax.Precision.HIGHEST).reshape(channels, atoms_total)
    layer_out = features + long_range + short_range
    back_mix = jnp.einsum('rdc,coi->rdoi', radial_mix, cotangent.reshape(channels, block_count, BLOCK), precision=lax.Precision.HIGHEST)
    contribution = jnp.einsum('rosij,rdoi->dosj', weights, back_mix, precision=lax.Precision.HIGHEST)
    back_short = jnp.zeros((channels, block_count, BLOCK), jnp.float32).at[:, flat_ids, :].add(contribution.reshape(channels, block_count * SLOTS, BLOCK))
    grad_features = cotangent + back_long + back_short.reshape(channels, atoms_total)
    return layer_out, grad_features, grad_filter
```

```python
import jax
import jax.numpy as jnp
from jax import lax
from jax.experimental import pallas as pl
from jax.experimental.pallas import tpu as pltpu
from jax.sharding import PartitionSpec as P

BLOCK = 128
REACH = 2
SLOTS = 5
C = 128
ATOMS = 1024
MODES = 1024
HALF = 512
SHARE = 64
RADIAL = 4
ATOM_DEV = 16
MODE_DEV = 8
HALO_ROWS = 272

F32 = jnp.float32
BF16 = jnp.bfloat16
MAGIC = 12582912.0
VMEM = pltpu.VMEM

NT = (((1,), (1,)), ((), ()))
NN = (((1,), (0,)), ((), ()))


def dot(a, b, dims):
    return lax.dot_general(a, b, dims, preferred_element_type=F32)


def pieces(x):
    high = x.astype(BF16)
    low = (x - high.astype(F32)).astype(BF16)
    return high, low


def cos_sin_turns(t):
    r = t - ((t + MAGIC) - MAGIC)
    y = r * r
    s = r * (4.44287957 + y * (-7.30781668 + y * (3.59777418 + y * -0.79119939)))
    c = 1.4142135 + y * (
        -6.97885095 + y * (5.73946038 + y * (-1.88355791 + y * 0.31068803))
    )
    return 1.0 - s * s, s * c


ROWS = 32
TILE = 256


def tables_tile(pos_ref, wave_ref, tab_ref, first, tile):
    shard = lax.axis_index("atom")
    mid = (2 * shard + 1).astype(F32) * (1.0 / 32.0)
    for chunk in range(TILE // ROWS):
        at = tile * TILE + chunk * ROWS
        w = wave_ref[pl.ds(pl.multiple_of(first + at, ROWS), ROWS), :]
        start = ((w[:, 0:1] * (2 * shard + 1)) & 31).astype(F32) * (1.0 / 32.0)
        wf = w.astype(F32)
        w0 = jnp.broadcast_to(wf[:, 0:1], (ROWS, BLOCK))
        w1 = jnp.broadcast_to(wf[:, 1:2], (ROWS, BLOCK))
        w2 = jnp.broadcast_to(wf[:, 2:3], (ROWS, BLOCK))
        c0 = jnp.broadcast_to(start, (ROWS, BLOCK))
        for k in range(ATOMS // BLOCK):
            lanes = pl.ds(k * BLOCK, BLOCK)
            p0 = pos_ref[0:1, lanes] - mid
            p1 = pos_ref[1:2, lanes]
            p2 = pos_ref[2:3, lanes]
            t = w0 * p0 + (w1 * p1 + (w2 * p2 + c0))
            cos, sin = cos_sin_turns(t)
            ch, cl = pieces(cos)
            sh, sl = pieces(sin)
            tab_ref[at : at + ROWS, lanes] = ch
            tab_ref[HALF + at : HALF + at + ROWS, lanes] = sh
            tab_ref[2 * HALF + at : 2 * HALF + at + ROWS, lanes] = cl
            tab_ref[3 * HALF + at : 3 * HALF + at + ROWS, lanes] = sl


def sums_tile(tab_ref, rhs_ref, out_ref, tile):
    for trig in range(2):
        at = trig * HALF + tile * TILE
        both = dot(tab_ref[at : at + TILE, :], rhs_ref[...], NT)
        at = at + 2 * HALF
        rest = dot(tab_ref[at : at + TILE, :], rhs_ref[0:C, :], NT)
        out_ref[tile * TILE : (tile + 1) * TILE, trig * C : (trig + 1) * C] = (
            both[:, :C] + both[:, C:] + rest
        )


def tables_kernel(own, feat_ref, pos_ref, wave_ref, out_ref, tab_ref, rhs_ref):
    core = lax.axis_index("atom") % 2
    first = HALF * (core if own else 1 - core)
    high, low = pieces(feat_ref[...])
    rhs_ref[0:C, :] = high
    rhs_ref[C:, :] = low
    for tile in range(HALF // TILE):
        tables_tile(pos_ref, wave_ref, tab_ref, first, tile)
        sums_tile(tab_ref, rhs_ref, out_ref, tile)


def spec():
    return pl.BlockSpec(memory_space=VMEM)


def tables_call(own, feat, pos, wave):
    def body(*refs):
        tables_kernel(own, *refs)

    return pl.pallas_call(
        body,
        out_shape=(
            jax.ShapeDtypeStruct((HALF, 2 * C), F32),
            jax.ShapeDtypeStruct((4 * HALF, ATOMS), BF16),
        ),
        in_specs=[spec()] * 3,
        out_specs=(spec(), spec()),
        scratch_shapes=[VMEM((2 * C, ATOMS), BF16)],
        cost_estimate=pl.CostEstimate(
            flops=3 * 10**9, bytes_accessed=5 * 10**6, transcendentals=0
        ),
        name="tables_own" if own else "tables_other",
    )(feat, pos, wave)


def cot_kernel(cot_ref, tab_ref, out_ref, rhs_ref):
    for k in range(MODE_DEV):
        high, low = pieces(cot_ref[k, 0:C, :])
        rhs_ref[0:C, k * BLOCK : (k + 1) * BLOCK] = high
        rhs_ref[C:, k * BLOCK : (k + 1) * BLOCK] = low
    for tile in range(HALF // TILE):
        sums_tile(tab_ref, rhs_ref, out_ref, tile)


def cot_call(cot, tab):
    return pl.pallas_call(
        cot_kernel,
        out_shape=jax.ShapeDtypeStruct((HALF, 2 * C), F32),
        in_specs=[spec()] * 2,
        out_specs=spec(),
        scratch_shapes=[VMEM((2 * C, ATOMS), BF16)],
        cost_estimate=pl.CostEstimate(
            flops=2 * 10**9, bytes_accessed=5 * 10**6, transcendentals=0
        ),
        name="cot_sums",
    )(cot, tab)


def turned(sums_ref, trig):
    return jnp.concatenate(
        [
            sums_ref[k * C : (k + 1) * C, trig * C : (trig + 1) * C].T
            for k in range(HALF // C)
        ],
        axis=1,
    )


def give_back_kernel(
    with_grad, own_ref, oth_ref, filt_ref, tab_own_ref, tab_oth_ref, *rest
):
    if with_grad:
        fown_ref, foth_ref, out_ref, grad_ref, lhs_ref = rest
    else:
        out_ref, lhs_ref = rest
    core = lax.axis_index("atom") % 2
    scale = 1.0 / (ATOM_DEV * ATOMS)
    for half in range(2):
        ref = (own_ref, oth_ref)[half]
        at = pl.multiple_of(HALF * (core if half == 0 else 1 - core), HALF)
        filt = filt_ref[:, pl.ds(at, HALF)] * scale
        grad = None
        for trig in range(2):
            sums = turned(ref, trig)
            if with_grad:
                term = turned((fown_ref, foth_ref)[half], trig) * sums
                grad = term if grad is None else grad + term
            high, low = pieces(filt * sums)
            lanes = pl.ds((2 * half + trig) * HALF, HALF)
            lhs_ref[0:C, lanes] = high
            lhs_ref[C:, lanes] = low
        if with_grad:
            grad_ref[:, pl.ds(at, HALF)] = grad * scale
    width = 2 * BLOCK
    for k in range(ATOMS // width):
        lanes = slice(k * width, (k + 1) * width)
        total = None
        for half in range(2):
            tab = (tab_own_ref, tab_oth_ref)[half]
            at = slice(2 * half * HALF, 2 * (half + 1) * HALF)
            both = dot(lhs_ref[:, at], tab[0 : 2 * HALF, lanes], NN)
            more = dot(lhs_ref[0:C, at], tab[2 * HALF :, lanes], NN)
            part = both[:C] + both[C:] + more
            total = part if total is None else total + part
        out_ref[2 * k] = total[:, :BLOCK]
        out_ref[2 * k + 1] = total[:, BLOCK:]


def give_back_call(own, oth, filt, tab_own, tab_oth, fsums=None):
    with_grad = fsums is not None

    def body(*refs):
        give_back_kernel(with_grad, *refs)

    out_shape = [jax.ShapeDtypeStruct((MODE_DEV, C, BLOCK), F32)]
    args = [own, oth, filt, tab_own, tab_oth]
    if with_grad:
        out_shape.append(jax.ShapeDtypeStruct((C, MODES), F32))
        args.extend(fsums)
    return pl.pallas_call(
        body,
        out_shape=tuple(out_shape),
        in_specs=[spec()] * len(args),
        out_specs=tuple(spec() for _ in out_shape),
        scratch_shapes=[VMEM((2 * C, 4 * HALF), BF16)],
        cost_estimate=pl.CostEstimate(
            flops=2 * 10**9, bytes_accessed=10**7, transcendentals=0
        ),
        name="give_back_cot" if with_grad else "give_back_feat",
    )(*args)


def near_kernel(
    left_ref,
    right_ref,
    feat_ref,
    pos_ref,
    cot_ref,
    mix_ref,
    rate_ref,
    live_ref,
    out_ref,
    back_ref,
    ext_ref,
    rhs_ref,
):
    own = lax.axis_index("mode")
    pad = REACH * BLOCK
    ext_ref[:, 0:pad] = left_ref[...]
    ext_ref[:, pad + ATOMS :] = right_ref[...]
    ext_ref[0:C, pad : pad + ATOMS] = feat_ref[...]
    ext_ref[C : C + 3, pad : pad + ATOMS] = pos_ref[...]
    for k in range(MODE_DEV):
        ext_ref[136:272, pad + k * BLOCK : pad + (k + 1) * BLOCK] = cot_ref[k]
    shard = lax.axis_index("atom")
    total_blocks = ATOM_DEV * MODE_DEV

    def unit(block, row):
        return row * float(total_blocks) - block.astype(F32)

    def halves(row):
        q = row - 0.5
        y = q * q
        s = q * (
            3.14159265
            + y
            * (-5.16771276 + y * (2.55016332 + y * (-0.5992522 + y * (0.0820504 - 0.00702839 * y))))
        )
        c = 1.0 + y * (
            -4.93480214
            + y * (4.05870916 + y * (-1.335212 + y * (0.23493731 - 0.02439632 * y)))
        )
        return -s, c

    me = shard * MODE_DEV + own
    here = ext_ref[C : C + 8, pl.ds(pl.multiple_of(pad + own * BLOCK, BLOCK), BLOCK)]
    u_own = unit(me, here[0:1])
    c1, s1 = halves(here[1:2])
    c2, s2 = halves(here[2:3])
    rows = jnp.concatenate([u_own, c1, s1, c2, s2, u_own, u_own, u_own], axis=0)
    columns = jnp.concatenate([rows] * (BLOCK // 8), axis=0).T
    wide = [jnp.broadcast_to(columns[:, k : k + 1], (BLOCK, BLOCK)) for k in range(5)]
    span = 2 * REACH + 1
    dist = []
    live = live_ref[0:1, :]
    for o in range(span):
        at = pl.ds(pl.multiple_of((own + o) * BLOCK, BLOCK), BLOCK)
        block = ext_ref[:, at]
        there = lax.rem(me + o - REACH + total_blocks, total_blocks)
        near = block[C : C + 8]
        x = wide[0] - (unit(there, near[0:1]) + float(o - REACH))
        d1c, d1s = halves(near[1:2])
        d2c, d2s = halves(near[2:3])
        y = x * x
        z = y * (3.14159265 / total_blocks) ** 2
        d = y * (1.0 + z * (-1.0 / 3.0 + z * (2.0 / 45.0)))
        e1 = wide[2] * d1c - wide[1] * d1s
        e2 = wide[4] * d2c - wide[3] * d2s
        d = d + (e1 * e1 + e2 * e2) * (2.0 / 3.14159265) ** 2
        dist.append(d)
        lanes = slice(o * BLOCK, (o + 1) * BLOCK)
        high, low = pieces(block[0:C] * live[0:1, o : o + 1])
        rhs_ref[0:C, lanes] = high
        rhs_ref[2 * C : 3 * C, lanes] = low
        lists_me = block[264:265, span - 1 - o : span - o]
        high, low = pieces(block[136 : 136 + C] * lists_me)
        rhs_ref[C : 2 * C, lanes] = high
        rhs_ref[3 * C :, lanes] = low
    out = ext_ref[0:C, pl.ds(pl.multiple_of(pad + own * BLOCK, BLOCK), BLOCK)]
    back = ext_ref[136 : 136 + C, pl.ds(pl.multiple_of(pad + own * BLOCK, BLOCK), BLOCK)]
    for r in range(RADIAL):
        rate = rate_ref[r]
        highs, lows = [], []
        for o in range(span):
            high, low = pieces(jnp.exp(dist[o] * -rate))
            highs.append(high)
            lows.append(low)
        weights_high = jnp.concatenate(highs, axis=1)
        weights_low = jnp.concatenate(lows, axis=1)
        both = dot(rhs_ref[...], weights_high, NT)
        got = (
            both[: 2 * C]
            + both[2 * C :]
            + dot(rhs_ref[0 : 2 * C, :], weights_low, NT)
        )
        high, low = pieces(got)
        mix = mix_ref[r]
        mh, ml = pieces(mix)
        th, tl = pieces(mix.T)
        out = out + (
            dot(th, high[:C], NN) + dot(th, low[:C], NN) + dot(tl, high[:C], NN)
        )
        back = back + (
            dot(mh, high[C:], NN) + dot(mh, low[C:], NN) + dot(ml, high[C:], NN)
        )
    out_ref[...] = out
    back_ref[...] = back


def near_call(left, right, feat, pos, cot, mix, rates, live):
    return pl.pallas_call(
        near_kernel,
        out_shape=(
            jax.ShapeDtypeStruct((C, BLOCK), F32),
            jax.ShapeDtypeStruct((C, BLOCK), F32),
        ),
        in_specs=[spec()] * 6 + [pl.BlockSpec(memory_space=pltpu.SMEM)] + [spec()],
        out_specs=(spec(), spec()),
        scratch_shapes=[
            VMEM((HALO_ROWS, ATOMS + 2 * REACH * BLOCK), F32),
            VMEM((4 * C, (2 * REACH + 1) * BLOCK), BF16),
        ],
        cost_estimate=pl.CostEstimate(
            flops=2 * 10**9, bytes_accessed=2 * 10**6, transcendentals=3 * 10**5
        ),
        name="near_blocks",
    )(left, right, feat, pos, cot, mix, rates, live)


def per_device(
    features,
    positions,
    wavevectors,
    mode_filter,
    radial_mix,
    radial_rates,
    neighbour_ids,
    live_counts,
    cotangent,
):
    core_swap = [(i, i ^ 1) for i in range(ATOM_DEV)]
    chips = [[c + 2 * i for i in range(ATOM_DEV // 2)] for c in range(2)]
    up = [(i, (i + 1) % ATOM_DEV) for i in range(ATOM_DEV)]
    down = [((i + 1) % ATOM_DEV, i) for i in range(ATOM_DEV)]

    def exchange(x):
        return lax.all_to_all(x, "atom", 0, 0, axis_index_groups=chips, tiled=True)

    me = lax.axis_index("atom") * MODE_DEV + lax.axis_index("mode")
    offset = jnp.mod(neighbour_ids[0] - me + REACH, ATOM_DEV * MODE_DEV)
    slots = jnp.arange(SLOTS, dtype=jnp.int32)
    hit = (offset[:, None] == jnp.arange(BLOCK, dtype=jnp.int32)[None, :]) & (
        slots[:, None] < live_counts[0]
    )
    live = jnp.broadcast_to(jnp.sum(hit.astype(F32), axis=0)[None, :], (8, BLOCK))
    packed = jnp.concatenate([cotangent, live], axis=0)
    cot = lax.all_to_all(
        jnp.broadcast_to(packed[None], (MODE_DEV, *packed.shape)), "mode", 0, 0, tiled=True
    )

    wave = wavevectors.T
    f_oth, tab_oth = tables_call(False, features, positions, wave)
    f_got = lax.ppermute(f_oth, "atom", core_swap)
    f_own, tab_own = tables_call(True, features, positions, wave)
    f_parts = exchange((f_own + f_got).reshape(8, SHARE, 2 * C))
    c_oth = cot_call(cot, tab_oth)
    c_got = lax.ppermute(c_oth, "atom", core_swap)
    c_own = cot_call(cot, tab_own)
    c_parts = exchange((c_own + c_got).reshape(8, SHARE, 2 * C))

    def halo(first):
        blocks = slice(first // BLOCK, first // BLOCK + REACH)
        ours = cot[blocks].transpose(1, 0, 2).reshape(C + 8, REACH * BLOCK)
        lanes = slice(first, first + REACH * BLOCK)
        return jnp.concatenate(
            [
                features[:, lanes],
                positions[:, lanes],
                jnp.zeros((5, REACH * BLOCK), F32),
                ours,
            ],
            axis=0,
        )

    left = lax.ppermute(halo(ATOMS - REACH * BLOCK), "atom", up)
    right = lax.ppermute(halo(0), "atom", down)
    near_out, near_back = near_call(
        left, right, features, positions, cot, radial_mix, radial_rates, live
    )

    def spread(parts):
        share = jnp.sum(parts, axis=0)
        own = exchange(jnp.broadcast_to(share[None], (8, *share.shape))).reshape(HALF, 2 * C)
        return own, lax.ppermute(own, "atom", core_swap)

    fs_own, fs_oth = spread(f_parts)
    (long_part,) = give_back_call(fs_own, fs_oth, mode_filter, tab_own, tab_oth)
    long_parts = lax.all_to_all(long_part, "mode", 0, 0, tiled=True)
    cs_own, cs_oth = spread(c_parts)
    back_part, grad_filter = give_back_call(
        cs_own, cs_oth, mode_filter, tab_own, tab_oth, (fs_own, fs_oth)
    )
    back_parts = lax.all_to_all(back_part, "mode", 0, 0, tiled=True)
    layer_out = near_out + jnp.sum(long_parts, axis=0)
    grad_features = near_back + jnp.sum(back_parts, axis=0)
    return (layer_out, grad_features, grad_filter)


def solution(mesh):
    in_specs = (
        P(None, "atom"),
        P(None, "atom"),
        P(None, "mode"),
        P(None, "mode"),
        P(),
        P(),
        P(("atom", "mode"), None),
        P(("atom", "mode")),
        P(None, ("atom", "mode")),
    )
    out_specs = (P(None, ("atom", "mode")), P(None, ("atom", "mode")), P(None, "mode"))
    return jax.shard_map(
        per_device, mesh=mesh, in_specs=in_specs, out_specs=out_specs, check_vma=False
    )
```

```python
import jax
import jax.numpy as jnp
from jax import lax
from jax.experimental import pallas as pl
from jax.experimental.pallas import tpu as pltpu
from jax.sharding import PartitionSpec as P

BLOCK = 128
REACH = 2
SLOTS = 5
C = 128
ATOMS = 1024
MODES = 1024
HALF = 512
SHARE = 64
RADIAL = 4
ATOM_DEV = 16
MODE_DEV = 8
HALO_ROWS = 272

F32 = jnp.float32
BF16 = jnp.bfloat16
MAGIC = 12582912.0
LIMIT = 24 * 1024 * 1024
VMEM = pltpu.VMEM

NT = (((1,), (1,)), ((), ()))
NN = (((1,), (0,)), ((), ()))


def dot(a, b, dims):
    return lax.dot_general(a, b, dims, preferred_element_type=F32)


def pieces(x):
    high = x.astype(BF16)
    low = (x - high.astype(F32)).astype(BF16)
    return high, low


def cos_sin_turns(t):
    r = t - ((t + MAGIC) - MAGIC)
    y = r * r
    s = r * (4.44287957 + y * (-7.30781668 + y * (3.59777418 + y * -0.79119939)))
    c = 1.4142135 + y * (
        -6.97885095 + y * (5.73946038 + y * (-1.88355791 + y * 0.31068803))
    )
    return 1.0 - s * s, s * c


ROWS = 32
TILE = 256
CHUNK = 4 * TILE
TILES = HALF // TILE


def columns_of(rows):
    rows = list(rows)
    rows = rows + [rows[0]] * (8 - len(rows))
    eight = jnp.concatenate(rows, axis=0)
    return jnp.concatenate([eight] * (BLOCK // 8), axis=0).T


def tables_tile(pos_ref, wave_ref, tab_ref, first, tile):
    shard = lax.axis_index("atom")
    mid = (2 * shard + 1).astype(F32) * (1.0 / 32.0)
    for group in range(TILE // BLOCK):
        at = tile * TILE + group * BLOCK
        w = wave_ref[:, pl.ds(pl.multiple_of(first + at, BLOCK), BLOCK)]
        start = ((w[0:1] * (2 * shard + 1)) & 31).astype(F32) * (1.0 / 32.0)
        wf = w.astype(F32)
        columns = columns_of((wf[0:1], wf[1:2], wf[2:3], start))
        for chunk in range(BLOCK // ROWS):
            part = columns[chunk * ROWS : (chunk + 1) * ROWS]
            w0, w1, w2, c0 = (
                jnp.broadcast_to(part[:, d : d + 1], (ROWS, BLOCK)) for d in range(4)
            )
            row = tile * CHUNK + group * BLOCK + chunk * ROWS
            for k in range(ATOMS // BLOCK):
                lanes = pl.ds(k * BLOCK, BLOCK)
                p0 = pos_ref[0:1, lanes] - mid
                p1 = pos_ref[1:2, lanes]
                p2 = pos_ref[2:3, lanes]
                t = w0 * p0 + (w1 * p1 + (w2 * p2 + c0))
                cos, sin = cos_sin_turns(t)
                ch, cl = pieces(cos)
                sh, sl = pieces(sin)
                tab_ref[row : row + ROWS, lanes] = ch
                tab_ref[TILE + row : TILE + row + ROWS, lanes] = sh
                tab_ref[2 * TILE + row : 2 * TILE + row + ROWS, lanes] = cl
                tab_ref[3 * TILE + row : 3 * TILE + row + ROWS, lanes] = sl


def sums_tile(tab_ref, rhs_ref, out_ref, tile, wide):
    at = tile * CHUNK
    both = dot(tab_ref[at : at + 2 * TILE, :], rhs_ref[...], NT)
    rest = dot(tab_ref[at + 2 * TILE : at + CHUNK, :], rhs_ref[0:wide, :], NT)
    total = both[:, :wide] + both[:, wide:] + rest
    for trig in range(2):
        out_ref[tile * TILE : (tile + 1) * TILE, trig * wide : (trig + 1) * wide] = (
            total[trig * TILE : (trig + 1) * TILE]
        )


def cot_rows(cot_ref, rhs_ref, high_at, low_at):
    for k in range(MODE_DEV):
        high, low = pieces(cot_ref[k, 0:C, :])
        rhs_ref[high_at : high_at + C, k * BLOCK : (k + 1) * BLOCK] = high
        rhs_ref[low_at : low_at + C, k * BLOCK : (k + 1) * BLOCK] = low


def tables_kernel(own, feat_hbm, pos_hbm, wave_hbm, extra_ref, *rest):
    out_ref, tab_hbm, rhs_ref, tab_ref, feat_ref, pos_ref, wave_ref, sems = rest
    fetches = [
        pltpu.make_async_copy(src, dst, sems.at[TILES + k])
        for k, (src, dst) in enumerate(
            ((pos_hbm, pos_ref), (wave_hbm, wave_ref), (feat_hbm, feat_ref))
        )
    ]
    for fetch in fetches:
        fetch.start()
    core = lax.axis_index("atom") % 2
    first = HALF * (core if own else 1 - core)
    wide = 2 * C if own else C
    if own:
        cot_rows(extra_ref, rhs_ref, C, wide + C)
    fetches[0].wait()
    fetches[1].wait()
    copies = []
    for tile in range(TILES):
        tables_tile(pos_ref, wave_ref, tab_ref, first, tile)
        rows = pl.ds(tile * CHUNK, CHUNK)
        copies.append(
            pltpu.make_async_copy(tab_ref.at[rows], tab_hbm.at[rows], sems.at[tile])
        )
        copies[-1].start()
        if tile == 0:
            fetches[2].wait()
            high, low = pieces(feat_ref[...])
            rhs_ref[0:C, :] = high
            rhs_ref[wide : wide + C, :] = low
        sums_tile(tab_ref, rhs_ref, out_ref, tile, wide)
    for copy in copies:
        copy.wait()


def spec():
    return pl.BlockSpec(memory_space=VMEM)


def call(body, name, ins, outs, scratch=(), flops=10**8, smem=(), far=(), far_outs=(), plain=(), args_in=()):
    args, in_specs = [], []
    for k, x in enumerate(ins):
        if k in smem:
            in_specs.append(pl.BlockSpec(memory_space=pltpu.SMEM))
        elif k in far:
            in_specs.append(pl.BlockSpec(memory_space=pltpu.HBM))
            x = pltpu.with_memory_space_constraint(x, pltpu.HBM)
        else:
            in_specs.append(spec())
            if k not in args_in:
                x = pltpu.with_memory_space_constraint(x, VMEM)
        args.append(x)
    size = sum(x.size * x.dtype.itemsize for x in ins)
    return pl.pallas_call(
        body,
        out_shape=tuple(
            pltpu.HBM(shape, kind)
            if k in far_outs
            else (jax.ShapeDtypeStruct if k in plain else VMEM)(shape, kind)
            for k, (shape, kind) in enumerate(outs)
        ),
        in_specs=in_specs,
        out_specs=tuple(
            pl.BlockSpec(memory_space=pltpu.HBM) if k in far_outs else spec()
            for k in range(len(outs))
        ),
        scratch_shapes=list(scratch),
        compiler_params=pltpu.CompilerParams(vmem_limit_bytes=LIMIT),
        cost_estimate=pl.CostEstimate(
            flops=flops, bytes_accessed=size, transcendentals=0
        ),
        name=name,
    )(*args)


def tables_call(own, feat, pos, wave, extra):
    def body(*refs):
        tables_kernel(own, *refs)

    wide = 2 * C if own else C
    return call(
        body,
        "tables_own" if own else "tables_other",
        (feat, pos, wave, extra),
        (((HALF, 2 * wide), F32), ((4 * HALF, ATOMS), BF16)),
        [
            VMEM((2 * wide, ATOMS), BF16),
            VMEM((4 * HALF, ATOMS), BF16),
            VMEM((C, ATOMS), F32),
            VMEM((3, ATOMS), F32),
            VMEM((3, MODES), jnp.int32),
            pltpu.SemaphoreType.DMA((TILES + 3,)),
        ],
        4 * 10**9,
        far=(0, 1, 2) if own else (0, 1, 2, 3),
        far_outs=(1,),
    )


def fetched(tab_hbm, tab_ref, sems):
    copies = []
    for tile in range(TILES):
        rows = pl.ds(tile * CHUNK, CHUNK)
        copy = pltpu.make_async_copy(tab_hbm.at[rows], tab_ref.at[rows], sems.at[tile])
        copy.start()
        copies.append(copy)
    return copies


def cot_kernel(cot_ref, tab_hbm, out_ref, rhs_ref, tab_ref, sems):
    copies = fetched(tab_hbm, tab_ref, sems)
    cot_rows(cot_ref, rhs_ref, 0, C)
    for tile in range(TILES):
        copies[tile].wait()
        sums_tile(tab_ref, rhs_ref, out_ref, tile, C)


def cot_call(cot, tab):
    (out,) = call(
        cot_kernel,
        "cot_sums",
        (cot, tab),
        (((HALF, 2 * C), F32),),
        [
            VMEM((2 * C, ATOMS), BF16),
            VMEM((4 * HALF, ATOMS), BF16),
            pltpu.SemaphoreType.DMA((TILES,)),
        ],
        2 * 10**9,
        far=(1,),
    )
    return out


def merge_kernel(own_ref, feat_ref, cot_ref, out_ref):
    for k in range(8):
        rows = slice(k * SHARE, (k + 1) * SHARE)
        for trig in range(2):
            for part in range(2):
                lanes = slice((2 * trig + part) * C, (2 * trig + part + 1) * C)
                got = (feat_ref, cot_ref)[part]
                out_ref[k, :, lanes] = (
                    own_ref[rows, lanes] + got[rows, trig * C : (trig + 1) * C]
                )


def give_back_kernel(own, sums_ref, filt_ref, tab_hbm, *rest):
    if own:
        acc_ref, lhs_ref, tab_ref, sems = rest
    else:
        acc_ref, out_ref, lhs_ref, tab_ref, sems = rest
    copies = fetched(tab_hbm, tab_ref, sems)
    core = lax.axis_index("atom") % 2
    at = pl.multiple_of(HALF * (core if own else 1 - core), HALF)
    scale = 1.0 / (ATOM_DEV * ATOMS)
    for k in range(HALF // C):
        filt = filt_ref[:, pl.ds(pl.multiple_of(at + k * C, C), C)] * scale
        tile, part = divmod(k * C, TILE)
        for trig in range(2):
            lanes = pl.ds((tile * 2 + trig) * TILE + part, C)
            for row in range(2):
                sums = sums_ref[k * C : (k + 1) * C, pl.ds((2 * trig + row) * C, C)]
                high, low = pieces(filt * sums.T)
                lhs_ref[row * C : (row + 1) * C, lanes] = high
                lhs_ref[(2 + row) * C : (3 + row) * C, lanes] = low
    width = 2 * BLOCK
    for n in range(TILES):
        copies[n].wait()
        depth = slice(n * 2 * TILE, (n + 1) * 2 * TILE)
        for k in range(ATOMS // width):
            lanes = slice(k * width, (k + 1) * width)
            top = n * CHUNK
            both = dot(lhs_ref[:, depth], tab_ref[top : top + 2 * TILE, lanes], NN)
            more = dot(
                lhs_ref[0 : 2 * C, depth],
                tab_ref[top + 2 * TILE : top + CHUNK, lanes],
                NN,
            )
            part = both[: 2 * C] + both[2 * C :] + more
            if not own and n == 0:
                part = part + acc_ref[:, lanes]
            if own and n == 0:
                acc_ref[:, lanes] = part
            elif own:
                acc_ref[:, lanes] = acc_ref[:, lanes] + part
            else:
                for side in range(2):
                    half = part[:, side * BLOCK : (side + 1) * BLOCK]
                    if n:
                        half = half + out_ref[2 * k + side]
                    out_ref[2 * k + side] = half


def give_back_call(own, sums, filt, tab, acc=None):
    def body(*refs):
        give_back_kernel(own, *refs)

    args = (sums, filt, tab) if own else (sums, filt, tab, acc)
    shape = (2 * C, ATOMS) if own else (MODE_DEV, 2 * C, BLOCK)
    (out,) = call(
        body,
        "give_back_own" if own else "give_back_other",
        args,
        ((shape, F32),),
        [
            VMEM((4 * C, 2 * HALF), BF16),
            VMEM((4 * HALF, ATOMS), BF16),
            pltpu.SemaphoreType.DMA((TILES,)),
        ],
        4 * 10**9,
        far=(2,),
        args_in=(1,),
    )
    return out


def grad_kernel(own_ref, oth_ref, grad_ref):
    core = lax.axis_index("atom") % 2
    scale = 1.0 / (ATOM_DEV * ATOMS)
    for half in range(2):
        ref = (own_ref, oth_ref)[half]
        at = pl.multiple_of(HALF * (core if half == 0 else 1 - core), HALF)
        for k in range(HALF // C):
            rows = slice(k * C, (k + 1) * C)
            grad = (
                ref[rows, 0:C] * ref[rows, C : 2 * C]
                + ref[rows, 2 * C : 3 * C] * ref[rows, 3 * C :]
            )
            grad_ref[:, pl.ds(pl.multiple_of(at + k * C, C), C)] = grad.T * scale


def near_kernel(
    left_ref,
    right_ref,
    feat_ref,
    pos_ref,
    cot_ref,
    mix_ref,
    rate_ref,
    out_ref,
    back_ref,
    ext_ref,
    rhs_ref,
):
    own = lax.axis_index("mode")
    pad = REACH * BLOCK
    ext_ref[:, 0:pad] = left_ref[...]
    ext_ref[:, pad + ATOMS :] = right_ref[...]
    ext_ref[0:C, pad : pad + ATOMS] = feat_ref[...]
    ext_ref[C : C + 3, pad : pad + ATOMS] = pos_ref[...]
    for k in range(MODE_DEV):
        ext_ref[136:272, pad + k * BLOCK : pad + (k + 1) * BLOCK] = cot_ref[k]
    shard = lax.axis_index("atom")
    total_blocks = ATOM_DEV * MODE_DEV

    def unit(block, row):
        return row * float(total_blocks) - block.astype(F32)

    def halves(row):
        q = row - 0.5
        y = q * q
        s = q * (
            3.14159265
            + y
            * (-5.16771276 + y * (2.55016332 + y * (-0.5992522 + y * (0.0820504 - 0.00702839 * y))))
        )
        c = 1.0 + y * (
            -4.93480214
            + y * (4.05870916 + y * (-1.335212 + y * (0.23493731 - 0.02439632 * y)))
        )
        return -s, c

    me = shard * MODE_DEV + own
    here = ext_ref[C : C + 8, pl.ds(pl.multiple_of(pad + own * BLOCK, BLOCK), BLOCK)]
    u_own = unit(me, here[0:1])
    c1, s1 = halves(here[1:2])
    c2, s2 = halves(here[2:3])
    columns = columns_of((u_own, c1, s1, c2, s2))
    wide = [jnp.broadcast_to(columns[:, k : k + 1], (BLOCK, BLOCK)) for k in range(5)]
    span = 2 * REACH + 1
    dist = []
    live = ext_ref[264:265, pl.ds(pl.multiple_of(pad + own * BLOCK, BLOCK), BLOCK)]
    for o in range(span):
        at = pl.ds(pl.multiple_of((own + o) * BLOCK, BLOCK), BLOCK)
        block = ext_ref[:, at]
        there = lax.rem(me + o - REACH + total_blocks, total_blocks)
        near = block[C : C + 8]
        x = wide[0] - (unit(there, near[0:1]) + float(o - REACH))
        d1c, d1s = halves(near[1:2])
        d2c, d2s = halves(near[2:3])
        y = x * x
        z = y * (3.14159265 / total_blocks) ** 2
        d = y * (1.0 + z * (-1.0 / 3.0 + z * (2.0 / 45.0)))
        e1 = wide[2] * d1c - wide[1] * d1s
        e2 = wide[4] * d2c - wide[3] * d2s
        d = d + (e1 * e1 + e2 * e2) * (2.0 / 3.14159265) ** 2
        dist.append(d)
        lanes = slice(o * BLOCK, (o + 1) * BLOCK)
        high, low = pieces(block[0:C] * live[0:1, o : o + 1])
        rhs_ref[0:C, lanes] = high
        rhs_ref[2 * C : 3 * C, lanes] = low
        lists_me = block[264:265, span - 1 - o : span - o]
        high, low = pieces(block[136 : 136 + C] * lists_me)
        rhs_ref[C : 2 * C, lanes] = high
        rhs_ref[3 * C :, lanes] = low
    out = ext_ref[0:C, pl.ds(pl.multiple_of(pad + own * BLOCK, BLOCK), BLOCK)]
    back = ext_ref[136 : 136 + C, pl.ds(pl.multiple_of(pad + own * BLOCK, BLOCK), BLOCK)]
    for r in range(RADIAL):
        rate = rate_ref[r]
        highs, lows = [], []
        for o in range(span):
            high, low = pieces(jnp.exp(dist[o] * -rate))
            highs.append(high)
            lows.append(low)
        weights_high = jnp.concatenate(highs, axis=1)
        weights_low = jnp.concatenate(lows, axis=1)
        both = dot(rhs_ref[...], weights_high, NT)
        got = (
            both[: 2 * C]
            + both[2 * C :]
            + dot(rhs_ref[0 : 2 * C, :], weights_low, NT)
        )
        high, low = pieces(got)
        mix = mix_ref[r]
        mh, ml = pieces(mix)
        th, tl = pieces(mix.T)
        out = out + (
            dot(th, high[:C], NN) + dot(th, low[:C], NN) + dot(tl, high[:C], NN)
        )
        back = back + (
            dot(mh, high[C:], NN) + dot(mh, low[C:], NN) + dot(ml, high[C:], NN)
        )
    out_ref[...] = out
    back_ref[...] = back


def near_call(left, right, feat, pos, cot, mix, rates):
    return call(
        near_kernel,
        "near_blocks",
        (left, right, feat, pos, cot, mix, rates),
        (((C, BLOCK), F32), ((C, BLOCK), F32)),
        [
            VMEM((HALO_ROWS, ATOMS + 2 * REACH * BLOCK), F32),
            VMEM((4 * C, (2 * REACH + 1) * BLOCK), BF16),
        ],
        2 * 10**9,
        smem=(6,),
        args_in=(2, 3, 5),
    )


def pack_kernel(ids_ref, live_ref, cot_ref, out_ref):
    total_blocks = ATOM_DEV * MODE_DEV
    me = lax.axis_index("atom") * MODE_DEV + lax.axis_index("mode")
    lane = lax.broadcasted_iota(jnp.int32, (8, BLOCK), 1)
    live = jnp.zeros((8, BLOCK), F32)
    for slot in range(SLOTS):
        offset = lax.rem(ids_ref[0, slot] - me + REACH + total_blocks, total_blocks)
        offset = jnp.where(slot < live_ref[0], offset, BLOCK)
        live = jnp.where(lane == offset, 1.0, live)
    for k in range(MODE_DEV):
        out_ref[k, 0:C, :] = cot_ref[...]
        out_ref[k, C:, :] = live


def halo_kernel(feat_hbm, pos_hbm, cot_ref, tail_ref, head_ref, pos_ref, sems):
    pad = REACH * BLOCK
    copies = []
    for k, (ref, first) in enumerate(((tail_ref, ATOMS - pad), (head_ref, 0))):
        lanes = pl.ds(first, pad)
        copies.append(
            pltpu.make_async_copy(
                feat_hbm.at[:, lanes], ref.at[pl.ds(0, C)], sems.at[k]
            )
        )
    copies.append(pltpu.make_async_copy(pos_hbm, pos_ref, sems.at[2]))
    for copy in copies:
        copy.start()
    for copy in copies:
        copy.wait()
    for ref, first in ((tail_ref, ATOMS - pad), (head_ref, 0)):
        ref[C : C + 8, :] = jnp.zeros((8, pad), F32)
        ref[C : C + 3, :] = pos_ref[:, first : first + pad]
        for k in range(REACH):
            lanes = slice(k * BLOCK, (k + 1) * BLOCK)
            ref[C + 8 :, lanes] = cot_ref[first // BLOCK + k]


def share_kernel(parts_ref, out_ref):
    share = parts_ref[0]
    for k in range(1, ATOM_DEV // 2):
        share = share + parts_ref[k]
    for k in range(ATOM_DEV // 2):
        out_ref[k] = share


def finish_kernel(near_ref, back_ref, parts_ref, out_ref, grad_ref):
    out = near_ref[...]
    grad = back_ref[...]
    for k in range(MODE_DEV):
        out = out + parts_ref[k, 0:C]
        grad = grad + parts_ref[k, C:]
    out_ref[...] = out
    grad_ref[...] = grad


def per_device(
    features,
    positions,
    wavevectors,
    mode_filter,
    radial_mix,
    radial_rates,
    neighbour_ids,
    live_counts,
    cotangent,
):
    core_swap = [(i, i ^ 1) for i in range(ATOM_DEV)]
    chips = [[c + 2 * i for i in range(ATOM_DEV // 2)] for c in range(2)]
    up = [(i, (i + 1) % ATOM_DEV) for i in range(ATOM_DEV)]
    down = [((i + 1) % ATOM_DEV, i) for i in range(ATOM_DEV)]

    def exchange(x):
        return lax.all_to_all(x, "atom", 0, 0, axis_index_groups=chips, tiled=True)

    (packed,) = call(
        pack_kernel,
        "pack_cot",
        (neighbour_ids, live_counts, cotangent),
        (((MODE_DEV, C + 8, BLOCK), F32),),
        smem=(0, 1),
        args_in=(2,),
        plain=(0,),
    )
    cot = lax.all_to_all(packed, "mode", 0, 0, tiled=True)

    f_oth, tab_oth = tables_call(False, features, positions, wavevectors, packed)
    f_got = lax.ppermute(f_oth, "atom", core_swap)
    c_got = lax.ppermute(cot_call(cot, tab_oth), "atom", core_swap)
    sums, tab_own = tables_call(True, features, positions, wavevectors, cot)
    tail, head = call(
        halo_kernel,
        "halo",
        (features, positions, cot),
        (((HALO_ROWS, REACH * BLOCK), F32), ((HALO_ROWS, REACH * BLOCK), F32)),
        [VMEM((3, ATOMS), F32), pltpu.SemaphoreType.DMA((3,))],
        far=(0, 1),
    )
    left = lax.ppermute(tail, "atom", up)
    right = lax.ppermute(head, "atom", down)
    sums, left, right = lax.optimization_barrier((sums, left, right))
    (parts,) = call(
        merge_kernel, "merge", (sums, f_got, c_got), (((8, SHARE, 4 * C), F32),)
    )
    parts = exchange(parts)
    near_out, near_back = near_call(
        left, right, features, positions, cot, radial_mix, radial_rates
    )

    parts, near_out, near_back = lax.optimization_barrier((parts, near_out, near_back))
    (share,) = call(share_kernel, "share", (parts,), ((parts.shape, F32),))
    own = exchange(share).reshape(HALF, 4 * C)
    oth = lax.ppermute(own, "atom", core_swap)
    acc = give_back_call(True, own, mode_filter, tab_own)
    back = give_back_call(False, oth, mode_filter, tab_oth, acc)
    back = lax.all_to_all(back, "mode", 0, 0, tiled=True)
    (grad_filter,) = call(
        grad_kernel, "grad_filter", (own, oth), (((C, MODES), F32),), plain=(0,), args_in=(0, 1)
    )
    layer_out, grad_features = call(
        finish_kernel,
        "finish",
        (near_out, near_back, back),
        (((C, BLOCK), F32), ((C, BLOCK), F32)),
        plain=(0, 1),
        args_in=(0, 1),
    )
    return (layer_out, grad_features, grad_filter)


def solution(mesh):
    in_specs = (
        P(None, "atom"),
        P(None, "atom"),
        P(None, "mode"),
        P(None, "mode"),
        P(),
        P(),
        P(("atom", "mode"), None),
        P(("atom", "mode")),
        P(None, ("atom", "mode")),
    )
    out_specs = (P(None, ("atom", "mode")), P(None, ("atom", "mode")), P(None, "mode"))
    return jax.shard_map(
        per_device, mesh=mesh, in_specs=in_specs, out_specs=out_specs, check_vma=False
    )
```

```python
import jax
import jax.numpy as jnp
from jax import lax
from jax.experimental import pallas as pl
from jax.experimental.pallas import tpu as pltpu
from jax.sharding import PartitionSpec as P


BLOCK = 128
REACH = 2
SLOTS = 5
C = 128
ATOMS = 1024
MODES = 1024
HALF = 512
SHARE = 64
RADIAL = 4
ATOM_DEV = 16
MODE_DEV = 8
HALO_ROWS = 272

F32 = jnp.float32
BF16 = jnp.bfloat16
MAGIC = 12582912.0
LIMIT = 24 * 1024 * 1024
VMEM = pltpu.VMEM

NT = (((1,), (1,)), ((), ()))
NN = (((1,), (0,)), ((), ()))


def dot(a, b, dims):
    return lax.dot_general(a, b, dims, preferred_element_type=F32)


def pieces(x):
    high = x.astype(BF16)
    low = (x - high.astype(F32)).astype(BF16)
    return high, low


def cos_sin_turns(t):
    r = t - ((t + MAGIC) - MAGIC)
    y = r * r
    s = r * (4.44287957 + y * (-7.30781668 + y * (3.59777418 + y * -0.79119939)))
    c = 1.4142135 + y * (
        -6.97885095 + y * (5.73946038 + y * (-1.88355791 + y * 0.31068803))
    )
    return 1.0 - s * s, s * c


ROWS = 32
TILE = 256
CHUNK = 4 * TILE
TILES = HALF // TILE


def columns_of(rows):
    rows = list(rows)
    rows = rows + [rows[0]] * (8 - len(rows))
    eight = jnp.concatenate(rows, axis=0)
    return jnp.concatenate([eight] * (BLOCK // 8), axis=0).T


def tables_tile(pos_ref, wave_ref, tab_ref, first, tile):
    shard = lax.axis_index("atom")
    mid = (2 * shard + 1).astype(F32) * (1.0 / 32.0)
    for group in range(TILE // BLOCK):
        at = tile * TILE + group * BLOCK
        w = wave_ref[:, pl.ds(pl.multiple_of(first + at, BLOCK), BLOCK)]
        start = ((w[0:1] * (2 * shard + 1)) & 31).astype(F32) * (1.0 / 32.0)
        wf = w.astype(F32)
        columns = columns_of((wf[0:1], wf[1:2], wf[2:3], start))
        for chunk in range(BLOCK // ROWS):
            part = columns[chunk * ROWS : (chunk + 1) * ROWS]
            w0, w1, w2, c0 = (
                jnp.broadcast_to(part[:, d : d + 1], (ROWS, BLOCK)) for d in range(4)
            )
            row = tile * CHUNK + group * BLOCK + chunk * ROWS
            for k in range(ATOMS // BLOCK):
                lanes = pl.ds(k * BLOCK, BLOCK)
                p0 = pos_ref[0:1, lanes] - mid
                p1 = pos_ref[1:2, lanes]
                p2 = pos_ref[2:3, lanes]
                t = w0 * p0 + (w1 * p1 + (w2 * p2 + c0))
                cos, sin = cos_sin_turns(t)
                ch, cl = pieces(cos)
                sh, sl = pieces(sin)
                tab_ref[row : row + ROWS, lanes] = ch
                tab_ref[TILE + row : TILE + row + ROWS, lanes] = sh
                tab_ref[2 * TILE + row : 2 * TILE + row + ROWS, lanes] = cl
                tab_ref[3 * TILE + row : 3 * TILE + row + ROWS, lanes] = sl


def sums_tile(tab_ref, rhs_ref, out_ref, tile, wide, copies=()):
    at = tile * CHUNK
    if copies:
        copies[0].wait()
    both = dot(tab_ref[at : at + 2 * TILE, :], rhs_ref[...], NT)
    if copies:
        copies[1].wait()
    rest = dot(tab_ref[at + 2 * TILE : at + CHUNK, :], rhs_ref[0:wide, :], NT)
    total = both[:, :wide] + both[:, wide:] + rest
    for trig in range(2):
        out_ref[tile * TILE : (tile + 1) * TILE, trig * wide : (trig + 1) * wide] = (
            total[trig * TILE : (trig + 1) * TILE]
        )


def cot_rows(cot_ref, rhs_ref, high_at, low_at):
    for k in range(MODE_DEV):
        high, low = pieces(cot_ref[k, 0:C, :])
        rhs_ref[high_at : high_at + C, k * BLOCK : (k + 1) * BLOCK] = high
        rhs_ref[low_at : low_at + C, k * BLOCK : (k + 1) * BLOCK] = low


def tables_kernel(own, feat_hbm, pos_hbm, wave_hbm, extra_ref, *rest):
    out_ref, tab_hbm, rhs_ref, tab_ref, feat_ref, pos_ref, wave_ref, sems = rest
    fetches = [
        pltpu.make_async_copy(src, dst, sems.at[TILES + k])
        for k, (src, dst) in enumerate(
            ((pos_hbm, pos_ref), (wave_hbm, wave_ref), (feat_hbm, feat_ref))
        )
    ]
    for fetch in fetches:
        fetch.start()
    core = lax.axis_index("atom") % 2
    first = HALF * (core if own else 1 - core)
    wide = C if own else 2 * C
    if not own:
        cot_rows(extra_ref, rhs_ref, C, wide + C)
    fetches[0].wait()
    fetches[1].wait()
    copies = []
    for tile in range(TILES):
        tables_tile(pos_ref, wave_ref, tab_ref, first, tile)
        rows = pl.ds(tile * CHUNK, CHUNK)
        copies.append(
            pltpu.make_async_copy(tab_ref.at[rows], tab_hbm.at[rows], sems.at[tile])
        )
        copies[-1].start()
        if tile == 0:
            fetches[2].wait()
            high, low = pieces(feat_ref[...])
            rhs_ref[0:C, :] = high
            rhs_ref[wide : wide + C, :] = low
        sums_tile(tab_ref, rhs_ref, out_ref, tile, wide)
    for copy in copies:
        copy.wait()


def spec():
    return pl.BlockSpec(memory_space=VMEM)


def call(body, name, ins, outs, scratch=(), flops=10**8, smem=(), far=(), far_outs=(), plain=(), args_in=(), any_in=()):
    args, in_specs = [], []
    for k, x in enumerate(ins):
        if k in smem:
            in_specs.append(pl.BlockSpec(memory_space=pltpu.SMEM))
        elif k in any_in:
            in_specs.append(pl.BlockSpec(memory_space=pl.ANY))
        elif k in far:
            in_specs.append(pl.BlockSpec(memory_space=pltpu.HBM))
            x = pltpu.with_memory_space_constraint(x, pltpu.HBM)
        else:
            in_specs.append(spec())
            if k not in args_in:
                x = pltpu.with_memory_space_constraint(x, VMEM)
        args.append(x)
    size = sum(x.size * x.dtype.itemsize for x in ins)
    return pl.pallas_call(
        body,
        out_shape=tuple(
            pltpu.HBM(shape, kind)
            if k in far_outs
            else (jax.ShapeDtypeStruct if k in plain else VMEM)(shape, kind)
            for k, (shape, kind) in enumerate(outs)
        ),
        in_specs=in_specs,
        out_specs=tuple(
            pl.BlockSpec(memory_space=pltpu.HBM) if k in far_outs else spec()
            for k in range(len(outs))
        ),
        scratch_shapes=list(scratch),
        compiler_params=pltpu.CompilerParams(vmem_limit_bytes=LIMIT),
        cost_estimate=pl.CostEstimate(
            flops=flops, bytes_accessed=size, transcendentals=0
        ),
        name=name,
    )(*args)


def tables_call(own, feat, pos, wave, extra):
    def body(*refs):
        tables_kernel(own, *refs)

    wide = C if own else 2 * C
    return call(
        body,
        "tables_own" if own else "tables_other",
        (feat, pos, wave, extra),
        (((HALF, 2 * wide), F32), ((4 * HALF, ATOMS), BF16)),
        [
            VMEM((2 * wide, ATOMS), BF16),
            VMEM((4 * HALF, ATOMS), BF16),
            VMEM((C, ATOMS), F32),
            VMEM((3, ATOMS), F32),
            VMEM((3, MODES), jnp.int32),
            pltpu.SemaphoreType.DMA((TILES + 3,)),
        ],
        4 * 10**9,
        far=(0, 1, 2, 3) if own else (0, 1, 2),
        far_outs=(1,),
    )


def fetched(tab_hbm, tab_ref, sems):
    copies = []
    for k in range(2 * TILES):
        rows = pl.ds(k * 2 * TILE, 2 * TILE)
        copy = pltpu.make_async_copy(tab_hbm.at[rows], tab_ref.at[rows], sems.at[k])
        copy.start()
        copies.append(copy)
    return copies


def cot_kernel(cot_ref, tab_hbm, out_ref, rhs_ref, tab_ref, sems):
    copies = fetched(tab_hbm, tab_ref, sems)
    cot_rows(cot_ref, rhs_ref, 0, C)
    for tile in range(TILES):
        sums_tile(tab_ref, rhs_ref, out_ref, tile, C, copies[2 * tile : 2 * tile + 2])


def cot_call(cot, tab):
    (out,) = call(
        cot_kernel,
        "cot_sums",
        (cot, tab),
        (((HALF, 2 * C), F32),),
        [
            VMEM((2 * C, ATOMS), BF16),
            VMEM((4 * HALF, ATOMS), BF16),
            pltpu.SemaphoreType.DMA((2 * TILES,)),
        ],
        2 * 10**9,
        far=(1,),
    )
    return out


def merge_kernel(feat_ref, cot_ref, got_ref, out_ref):
    for k in range(8):
        rows = slice(k * SHARE, (k + 1) * SHARE)
        for trig in range(2):
            for part in range(2):
                lanes = slice((2 * trig + part) * C, (2 * trig + part + 1) * C)
                own = (feat_ref, cot_ref)[part]
                out_ref[k, :, lanes] = (
                    got_ref[rows, lanes] + own[rows, trig * C : (trig + 1) * C]
                )


def give_back_kernel(own, sums_ref, filt_hbm, tab_hbm, *rest):
    if own:
        acc_ref, lhs_ref, tab_ref, filt_ref, sems = rest
    else:
        acc_ref, out_hbm, lhs_ref, tab_ref, filt_ref, sems, out_ref = rest
    core = lax.axis_index("atom") % 2
    at = pl.multiple_of(HALF * (core if own else 1 - core), HALF)
    fetch = pltpu.make_async_copy(
        filt_hbm.at[:, pl.ds(at, HALF)], filt_ref, sems.at[2 * TILES]
    )
    fetch.start()
    copies = fetched(tab_hbm, tab_ref, sems)
    fetch.wait()
    scale = 1.0 / (ATOM_DEV * ATOMS)
    for k in range(HALF // C):
        filt = filt_ref[:, k * C : (k + 1) * C] * scale
        tile, part = divmod(k * C, TILE)
        for trig in range(2):
            lanes = pl.ds((tile * 2 + trig) * TILE + part, C)
            for row in range(2):
                sums = sums_ref[k * C : (k + 1) * C, pl.ds((2 * trig + row) * C, C)]
                high, low = pieces(filt * sums.T)
                lhs_ref[row * C : (row + 1) * C, lanes] = high
                lhs_ref[(2 + row) * C : (3 + row) * C, lanes] = low
    width = 2 * BLOCK
    stores = []
    for n in range(TILES):
        copies[2 * n].wait()
        copies[2 * n + 1].wait()
        depth = slice(n * 2 * TILE, (n + 1) * 2 * TILE)
        for k in range(ATOMS // width):
            lanes = slice(k * width, (k + 1) * width)
            top = n * CHUNK
            both = dot(lhs_ref[:, depth], tab_ref[top : top + 2 * TILE, lanes], NN)
            more = dot(
                lhs_ref[0 : 2 * C, depth],
                tab_ref[top + 2 * TILE : top + CHUNK, lanes],
                NN,
            )
            part = both[: 2 * C] + both[2 * C :] + more
            if not own and n == 0:
                part = part + acc_ref[:, lanes]
            if own and n == 0:
                acc_ref[:, lanes] = part
            elif own:
                acc_ref[:, lanes] = acc_ref[:, lanes] + part
            else:
                for side in range(2):
                    half = part[:, side * BLOCK : (side + 1) * BLOCK]
                    if n:
                        half = half + out_ref[2 * k + side]
                    out_ref[2 * k + side] = half
                if n == TILES - 1:
                    pair = pl.ds(2 * k, 2)
                    stores.append(
                        pltpu.make_async_copy(
                            out_ref.at[pair], out_hbm.at[pair], sems.at[2 * TILES + 1 + k]
                        )
                    )
                    stores[-1].start()
    for store in stores:
        store.wait()


def give_back_call(own, sums, filt, tab, acc=None):
    def body(*refs):
        give_back_kernel(own, *refs)

    args = (sums, filt, tab) if own else (sums, filt, tab, acc)
    shape = (2 * C, ATOMS) if own else (MODE_DEV, 2 * C, BLOCK)
    (out,) = call(
        body,
        "give_back_own" if own else "give_back_other",
        args,
        ((shape, F32),),
        [
            VMEM((4 * C, 2 * HALF), BF16),
            VMEM((4 * HALF, ATOMS), BF16),
            VMEM((C, HALF), F32),
            pltpu.SemaphoreType.DMA((2 * TILES + 1 + ATOMS // (2 * BLOCK),)),
        ]
        + ([] if own else [VMEM(shape, F32)]),
        4 * 10**9,
        far=(1, 2),
        far_outs=() if own else (0,),
    )
    return out


def grad_kernel(own_ref, oth_ref, grad_ref):
    core = lax.axis_index("atom") % 2
    scale = 1.0 / (ATOM_DEV * ATOMS)
    for half in range(2):
        ref = (own_ref, oth_ref)[half]
        at = pl.multiple_of(HALF * (core if half == 0 else 1 - core), HALF)
        for k in range(HALF // C):
            rows = slice(k * C, (k + 1) * C)
            grad = (
                ref[rows, 0:C] * ref[rows, C : 2 * C]
                + ref[rows, 2 * C : 3 * C] * ref[rows, 3 * C :]
            )
            grad_ref[:, pl.ds(pl.multiple_of(at + k * C, C), C)] = grad.T * scale


def near_kernel(
    rim_ref,
    feat_ref,
    pos_ref,
    cot_ref,
    mix_hbm,
    rate_ref,
    out_ref,
    back_ref,
    ext_ref,
    rhs_ref,
    mix_ref,
    pos_vmem,
    sems,
):
    own = lax.axis_index("mode")
    pad = REACH * BLOCK
    middle = pl.ds(pad, ATOMS)
    rim_at = jnp.where(own < MODE_DEV // 2, 0, pad + ATOMS)
    moves = [
        (pos_ref, pos_vmem),
        (rim_ref, ext_ref.at[:, pl.ds(pl.multiple_of(rim_at, BLOCK), pad)]),
        (feat_ref, ext_ref.at[pl.ds(0, C), middle]),
        (mix_hbm, mix_ref),
    ]
    for k in range(MODE_DEV):
        lanes = pl.ds(pad + k * BLOCK, BLOCK)
        moves.append((cot_ref.at[k], ext_ref.at[pl.ds(C + 8, C + 8), lanes]))
    copies = [
        pltpu.make_async_copy(src, dst, sems.at[k]) for k, (src, dst) in enumerate(moves)
    ]
    for copy in copies:
        copy.start()
    for copy in copies:
        copy.wait()
    ext_ref[C : C + 3, pad : pad + ATOMS] = pos_vmem[...]
    shard = lax.axis_index("atom")
    total_blocks = ATOM_DEV * MODE_DEV

    def unit(block, row):
        return row * float(total_blocks) - block.astype(F32)

    def halves(row):
        q = row - 0.5
        y = q * q
        s = q * (
            3.14159265
            + y
            * (-5.16771276 + y * (2.55016332 + y * (-0.5992522 + y * (0.0820504 - 0.00702839 * y))))
        )
        c = 1.0 + y * (
            -4.93480214
            + y * (4.05870916 + y * (-1.335212 + y * (0.23493731 - 0.02439632 * y)))
        )
        return -s, c

    me = shard * MODE_DEV + own
    here = ext_ref[C : C + 8, pl.ds(pl.multiple_of(pad + own * BLOCK, BLOCK), BLOCK)]
    u_own = unit(me, here[0:1])
    c1, s1 = halves(here[1:2])
    c2, s2 = halves(here[2:3])
    columns = columns_of((u_own, c1, s1, c2, s2))
    wide = [jnp.broadcast_to(columns[:, k : k + 1], (BLOCK, BLOCK)) for k in range(5)]
    span = 2 * REACH + 1
    dist = []
    live = ext_ref[264:265, pl.ds(pl.multiple_of(pad + own * BLOCK, BLOCK), BLOCK)]
    for o in range(span):
        at = pl.ds(pl.multiple_of((own + o) * BLOCK, BLOCK), BLOCK)
        block = ext_ref[:, at]
        there = lax.rem(me + o - REACH + total_blocks, total_blocks)
        near = block[C : C + 8]
        x = wide[0] - (unit(there, near[0:1]) + float(o - REACH))
        d1c, d1s = halves(near[1:2])
        d2c, d2s = halves(near[2:3])
        y = x * x
        z = y * (3.14159265 / total_blocks) ** 2
        d = y * (1.0 + z * (-1.0 / 3.0 + z * (2.0 / 45.0)))
        e1 = wide[2] * d1c - wide[1] * d1s
        e2 = wide[4] * d2c - wide[3] * d2s
        d = d + (e1 * e1 + e2 * e2) * (2.0 / 3.14159265) ** 2
        dist.append(d)
        lanes = slice(o * BLOCK, (o + 1) * BLOCK)
        high, low = pieces(block[0:C] * live[0:1, o : o + 1])
        rhs_ref[0:C, lanes] = high
        rhs_ref[2 * C : 3 * C, lanes] = low
        lists_me = block[264:265, span - 1 - o : span - o]
        high, low = pieces(block[136 : 136 + C] * lists_me)
        rhs_ref[C : 2 * C, lanes] = high
        rhs_ref[3 * C :, lanes] = low
    out = ext_ref[0:C, pl.ds(pl.multiple_of(pad + own * BLOCK, BLOCK), BLOCK)]
    back = ext_ref[136 : 136 + C, pl.ds(pl.multiple_of(pad + own * BLOCK, BLOCK), BLOCK)]
    for r in range(RADIAL):
        rate = rate_ref[r]
        highs, lows = [], []
        for o in range(span):
            high, low = pieces(jnp.exp(dist[o] * -rate))
            highs.append(high)
            lows.append(low)
        weights_high = jnp.concatenate(highs, axis=1)
        weights_low = jnp.concatenate(lows, axis=1)
        both = dot(rhs_ref[...], weights_high, NT)
        got = (
            both[: 2 * C]
            + both[2 * C :]
            + dot(rhs_ref[0 : 2 * C, :], weights_low, NT)
        )
        high, low = pieces(got)
        mix = mix_ref[r]
        mh, ml = pieces(mix)
        th, tl = pieces(mix.T)
        out = out + (
            dot(th, high[:C], NN) + dot(th, low[:C], NN) + dot(tl, high[:C], NN)
        )
        back = back + (
            dot(mh, high[C:], NN) + dot(mh, low[C:], NN) + dot(ml, high[C:], NN)
        )
    out_ref[...] = out
    back_ref[...] = back


def near_call(rim, feat, pos, cot, mix, rates):
    return call(
        near_kernel,
        "near_blocks",
        (rim, feat, pos, cot, mix, rates),
        (((C, BLOCK), F32), ((C, BLOCK), F32)),
        [
            VMEM((HALO_ROWS, ATOMS + 2 * REACH * BLOCK), F32),
            VMEM((4 * C, (2 * REACH + 1) * BLOCK), BF16),
            VMEM((RADIAL, C, C), F32),
            VMEM((3, ATOMS), F32),
            pltpu.SemaphoreType.DMA((4 + MODE_DEV,)),
        ],
        2 * 10**9,
        smem=(5,),
        any_in=(0, 1, 2, 3, 4),
    )


def pack_kernel(ids_hbm, live_ref, cot_hbm, out_hbm, ids_ref, pack_ref, sems):
    fetches = [
        pltpu.make_async_copy(cot_hbm, pack_ref.at[pl.ds(0, C)], sems.at[MODE_DEV]),
        pltpu.make_async_copy(ids_hbm, ids_ref, sems.at[MODE_DEV + 1]),
    ]
    for fetch in fetches:
        fetch.start()
    total_blocks = ATOM_DEV * MODE_DEV
    me = lax.axis_index("atom") * MODE_DEV + lax.axis_index("mode")
    lane = lax.broadcasted_iota(jnp.int32, (8, BLOCK), 1)
    live = jnp.zeros((8, BLOCK), F32)
    fetches[1].wait()
    for slot in range(SLOTS):
        offset = lax.rem(ids_ref[0, slot] - me + REACH + total_blocks, total_blocks)
        offset = jnp.where(slot < live_ref[0], offset, BLOCK)
        live = jnp.where(lane == offset, 1.0, live)
    pack_ref[C:, :] = live
    fetches[0].wait()
    copies = [
        pltpu.make_async_copy(pack_ref, out_hbm.at[k], sems.at[k]) for k in range(MODE_DEV)
    ]
    for copy in copies:
        copy.start()
    for copy in copies:
        copy.wait()


def halo_kernel(feat_hbm, pos_hbm, cot_ref, out_ref, pos_ref, sems):
    pad = REACH * BLOCK
    tail = lax.axis_index("mode") < MODE_DEV // 2
    block = jnp.where(tail, MODE_DEV - REACH, 0)
    lanes = pl.ds(pl.multiple_of(block * BLOCK, BLOCK), pad)
    copies = [
        pltpu.make_async_copy(feat_hbm.at[:, lanes], out_ref.at[pl.ds(0, C)], sems.at[0]),
        pltpu.make_async_copy(pos_hbm, pos_ref, sems.at[1]),
    ]
    for copy in copies:
        copy.start()
    for k in range(REACH):
        out_ref[C + 8 :, k * BLOCK : (k + 1) * BLOCK] = cot_ref[block + k]
    out_ref[C : C + 8, :] = jnp.zeros((8, pad), F32)
    for copy in copies:
        copy.wait()
    out_ref[C : C + 3, :] = pos_ref[:, lanes]


def share_kernel(parts_ref, out_ref):
    share = parts_ref[0]
    for k in range(1, ATOM_DEV // 2):
        share = share + parts_ref[k]
    for k in range(ATOM_DEV // 2):
        out_ref[k] = share


def finish_kernel(near_ref, back_ref, parts_ref, out_ref, grad_ref):
    out = near_ref[...]
    grad = back_ref[...]
    for k in range(MODE_DEV):
        out = out + parts_ref[k, 0:C]
        grad = grad + parts_ref[k, C:]
    out_ref[...] = out
    grad_ref[...] = grad


def per_device(
    features,
    positions,
    wavevectors,
    mode_filter,
    radial_mix,
    radial_rates,
    neighbour_ids,
    live_counts,
    cotangent,
):
    core_swap = [(i, i ^ 1) for i in range(ATOM_DEV)]
    chips = [[c + 2 * i for i in range(ATOM_DEV // 2)] for c in range(2)]
    rims = []
    for i in range(ATOM_DEV):
        for m in range(REACH):
            after = (i + 1) % ATOM_DEV
            rims.append((i * MODE_DEV + m, after * MODE_DEV + m))
            last = MODE_DEV - 1 - m
            rims.append((after * MODE_DEV + last, i * MODE_DEV + last))

    def exchange(x):
        return lax.all_to_all(x, "atom", 0, 0, axis_index_groups=chips, tiled=True)

    (packed,) = call(
        pack_kernel,
        "pack_cot",
        (neighbour_ids, live_counts, cotangent),
        (((MODE_DEV, C + 8, BLOCK), F32),),
        [
            pltpu.SMEM((1, SLOTS), jnp.int32),
            VMEM((C + 8, BLOCK), F32),
            pltpu.SemaphoreType.DMA((MODE_DEV + 2,)),
        ],
        smem=(1,),
        far=(0, 2),
        far_outs=(0,),
    )
    cot = lax.all_to_all(packed, "mode", 0, 0, tiled=True)

    f_own, tab_own = tables_call(True, features, positions, wavevectors, packed)
    cot, f_own, tab_own = lax.optimization_barrier((cot, f_own, tab_own))
    oth, tab_oth = tables_call(False, features, positions, wavevectors, cot)
    got = lax.ppermute(oth, "atom", core_swap)
    c_own = cot_call(cot, tab_own)
    (rim,) = call(
        halo_kernel,
        "halo",
        (features, positions, cot),
        (((HALO_ROWS, REACH * BLOCK), F32),),
        [VMEM((3, ATOMS), F32), pltpu.SemaphoreType.DMA((2,))],
        far=(0, 1),
    )
    (parts,) = call(
        merge_kernel, "merge", (f_own, c_own, got), (((8, SHARE, 4 * C), F32),)
    )
    parts, rim = lax.optimization_barrier((parts, rim))
    parts = exchange(parts)
    rim = lax.ppermute(rim, ("atom", "mode"), rims)
    parts, rim = lax.optimization_barrier((parts, rim))
    near_out, near_back = near_call(
        rim, features, positions, cot, radial_mix, radial_rates
    )
    (share,) = call(share_kernel, "share", (parts,), ((parts.shape, F32),))
    own = exchange(share).reshape(HALF, 4 * C)
    own, near_out, near_back = lax.optimization_barrier((own, near_out, near_back))
    oth = lax.ppermute(own, "atom", core_swap)
    acc = give_back_call(True, own, mode_filter, tab_own)
    back = give_back_call(False, oth, mode_filter, tab_oth, acc)
    back = lax.all_to_all(back, "mode", 0, 0, tiled=True)
    (grad_filter,) = call(
        grad_kernel, "grad_filter", (own, oth), (((C, MODES), F32),), plain=(0,), args_in=(0, 1)
    )
    layer_out, grad_features = call(
        finish_kernel,
        "finish",
        (near_out, near_back, back),
        (((C, BLOCK), F32), ((C, BLOCK), F32)),
        plain=(0, 1),
        args_in=(0, 1),
    )
    return (layer_out, grad_features, grad_filter)


def solution(mesh):
    in_specs = (
        P(None, "atom"),
        P(None, "atom"),
        P(None, "mode"),
        P(None, "mode"),
        P(),
        P(),
        P(("atom", "mode"), None),
        P(("atom", "mode")),
        P(None, ("atom", "mode")),
    )
    out_specs = (P(None, ("atom", "mode")), P(None, ("atom", "mode")), P(None, "mode"))
    return jax.shard_map(
        per_device, mesh=mesh, in_specs=in_specs, out_specs=out_specs, check_vma=False
    )
```

```python
import jax
import jax.numpy as jnp
from jax import lax
from jax.experimental import pallas as pl
from jax.experimental.pallas import tpu as pltpu
from jax.sharding import PartitionSpec as P


BLOCK = 128
REACH = 2
SLOTS = 5
C = 128
ATOMS = 1024
MODES = 1024
HALF = 512
SHARE = 64
RADIAL = 4
ATOM_DEV = 16
MODE_DEV = 8
HALO_ROWS = 272

F32 = jnp.float32
BF16 = jnp.bfloat16
MAGIC = 12582912.0
LIMIT = 24 * 1024 * 1024
VMEM = pltpu.VMEM

NT = (((1,), (1,)), ((), ()))
NN = (((1,), (0,)), ((), ()))


def dot(a, b, dims):
    return lax.dot_general(a, b, dims, preferred_element_type=F32)


def pieces(x):
    high = x.astype(BF16)
    low = (x - high.astype(F32)).astype(BF16)
    return high, low


def cos_sin_turns(t):
    r = t - ((t + MAGIC) - MAGIC)
    y = r * r
    s = r * (4.44287957 + y * (-7.30781668 + y * (3.59777418 + y * -0.79119939)))
    c = 1.4142135 + y * (
        -6.97885095 + y * (5.73946038 + y * (-1.88355791 + y * 0.31068803))
    )
    return 1.0 - s * s, s * c


ROWS = 32
TILE = 256
CHUNK = 4 * TILE
TILES = HALF // TILE


def columns_of(rows):
    rows = list(rows)
    rows = rows + [rows[0]] * (8 - len(rows))
    eight = jnp.concatenate(rows, axis=0)
    return jnp.concatenate([eight] * (BLOCK // 8), axis=0).T


def tables_tile(pos_ref, wave_ref, tab_ref, first, tile, leave):
    shard = lax.axis_index("atom")
    mid = (2 * shard + 1).astype(F32) * (1.0 / 32.0)
    for group in range(TILE // BLOCK):
        at = tile * TILE + group * BLOCK
        w = wave_ref[:, pl.ds(pl.multiple_of(first + at, BLOCK), BLOCK)]
        start = ((w[0:1] * (2 * shard + 1)) & 31).astype(F32) * (1.0 / 32.0)
        wf = w.astype(F32)
        columns = columns_of((wf[0:1], wf[1:2], wf[2:3], start))
        for chunk in range(BLOCK // ROWS):
            part = columns[chunk * ROWS : (chunk + 1) * ROWS]
            w0, w1, w2, c0 = (
                jnp.broadcast_to(part[:, d : d + 1], (ROWS, BLOCK)) for d in range(4)
            )
            row = tile * CHUNK + group * BLOCK + chunk * ROWS
            for k in range(ATOMS // BLOCK):
                lanes = pl.ds(k * BLOCK, BLOCK)
                p0 = pos_ref[0:1, lanes] - mid
                p1 = pos_ref[1:2, lanes]
                p2 = pos_ref[2:3, lanes]
                t = w0 * p0 + (w1 * p1 + (w2 * p2 + c0))
                cos, sin = cos_sin_turns(t)
                ch, cl = pieces(cos)
                sh, sl = pieces(sin)
                tab_ref[row : row + ROWS, lanes] = ch
                tab_ref[TILE + row : TILE + row + ROWS, lanes] = sh
                tab_ref[2 * TILE + row : 2 * TILE + row + ROWS, lanes] = cl
                tab_ref[3 * TILE + row : 3 * TILE + row + ROWS, lanes] = sl
        leave(tile * CHUNK + group * BLOCK)


def sums_tile(tab_ref, rhs_ref, out_ref, tile, wide, copies=()):
    at = tile * CHUNK
    for copy in copies:
        copy.wait()
    both = dot(tab_ref[at : at + 2 * TILE, :], rhs_ref[...], NT)
    rest = dot(tab_ref[at + 2 * TILE : at + CHUNK, :], rhs_ref[0:wide, :], NT)
    total = both[:, :wide] + both[:, wide:] + rest
    for trig in range(2):
        out_ref[tile * TILE : (tile + 1) * TILE, trig * wide : (trig + 1) * wide] = (
            total[trig * TILE : (trig + 1) * TILE]
        )


def cot_rows(cot_ref, rhs_ref, high_at, low_at):
    for k in range(MODE_DEV):
        high, low = pieces(cot_ref[k, 0:C, :])
        rhs_ref[high_at : high_at + C, k * BLOCK : (k + 1) * BLOCK] = high
        rhs_ref[low_at : low_at + C, k * BLOCK : (k + 1) * BLOCK] = low


def tables_kernel(own, feat_hbm, pos_ref, wave_ref, dep_ref, *rest):
    out_ref, tab_hbm, rhs_ref, tab_ref, feat_ref, sems = rest
    fetch = pltpu.make_async_copy(feat_hbm, feat_ref, sems.at[0])
    fetch.start()
    core = lax.axis_index("atom") % 2
    first = HALF * (core if own else 1 - core)
    copies = []

    def leave(row):
        for kind in range(4):
            rows = pl.ds(row + kind * TILE, BLOCK)
            sem = sems.at[1 + len(copies)]
            copies.append(
                pltpu.make_async_copy(tab_ref.at[rows], tab_hbm.at[rows], sem)
            )
            copies[-1].start()

    for tile in range(TILES):
        tables_tile(pos_ref, wave_ref, tab_ref, first, tile, leave)
        if tile == 0:
            fetch.wait()
            high, low = pieces(feat_ref[...])
            rhs_ref[0:C, :] = high
            rhs_ref[C:, :] = low
        sums_tile(tab_ref, rhs_ref, out_ref, tile, C)
    for copy in copies:
        copy.wait()


def spec():
    return pl.BlockSpec(memory_space=VMEM)


def call(body, ins, outs, scratch=(), flops=10**8, smem=(), far=(), far_outs=(), plain=(), args_in=(), any_in=()):
    args, in_specs = [], []
    for k, x in enumerate(ins):
        if k in smem:
            in_specs.append(pl.BlockSpec(memory_space=pltpu.SMEM))
        elif k in any_in:
            in_specs.append(pl.BlockSpec(memory_space=pl.ANY))
        elif k in far:
            in_specs.append(pl.BlockSpec(memory_space=pltpu.HBM))
            x = pltpu.with_memory_space_constraint(x, pltpu.HBM)
        else:
            in_specs.append(spec())
            if k not in args_in:
                x = pltpu.with_memory_space_constraint(x, VMEM)
        args.append(x)
    size = sum(x.size * x.dtype.itemsize for x in ins)
    return pl.pallas_call(
        body,
        out_shape=tuple(
            pltpu.HBM(shape, kind)
            if k in far_outs
            else (jax.ShapeDtypeStruct if k in plain else VMEM)(shape, kind)
            for k, (shape, kind) in enumerate(outs)
        ),
        in_specs=in_specs,
        out_specs=tuple(
            pl.BlockSpec(memory_space=pltpu.HBM) if k in far_outs else spec()
            for k in range(len(outs))
        ),
        scratch_shapes=list(scratch),
        compiler_params=pltpu.CompilerParams(vmem_limit_bytes=LIMIT),
        cost_estimate=pl.CostEstimate(
            flops=flops, bytes_accessed=size, transcendentals=0
        ),
    )(*args)


def tables_call(own, feat, pos, wave, dep):
    def body(*refs):
        tables_kernel(own, *refs)

    return call(
        body,
        (feat, pos, wave, dep),
        (((HALF, 2 * C), F32), ((4 * HALF, ATOMS), BF16)),
        [
            VMEM((2 * C, ATOMS), BF16),
            VMEM((4 * HALF, ATOMS), BF16),
            VMEM((C, ATOMS), F32),
            pltpu.SemaphoreType.DMA((1 + 4 * HALF // BLOCK,)),
        ],
        4 * 10**9,
        far=(0, 3),
        far_outs=(1,),
    )


def fetched(tab_hbm, tab_ref, sems, tiles):
    copies = []
    for tile in tiles:
        rows = pl.ds(tile * CHUNK, CHUNK)
        copy = pltpu.make_async_copy(tab_hbm.at[rows], tab_ref.at[rows], sems.at[tile])
        copy.start()
        copies.append(copy)
    return copies


def ahead(next_hbm, next_ref, sem):
    copy = pltpu.make_async_copy(next_hbm.at[pl.ds(0, CHUNK)], next_ref, sem)
    copy.start()
    return copy


def cot_kernel(first, cot_ref, tab_hbm, other_ref, *rest):
    if first:
        feat_hbm, pos_hbm, out_ref, next_ref, rim_ref, rhs_ref, tab_ref, sems, pos_ref = rest
        copies = fetched(tab_hbm, tab_ref, sems, range(TILES))
        pad = REACH * BLOCK
        tail = lax.axis_index("mode") < MODE_DEV // 2
        block = jnp.where(tail, MODE_DEV - REACH, 0)
        lanes = pl.ds(pl.multiple_of(block * BLOCK, BLOCK), pad)
        later = [
            pltpu.make_async_copy(pos_hbm, pos_ref, sems.at[TILES + 1]),
            pltpu.make_async_copy(
                feat_hbm.at[:, lanes], rim_ref.at[pl.ds(0, C)], sems.at[TILES + 2]
            ),
        ]
        for copy in later:
            copy.start()
        later.append(ahead(other_ref, next_ref, sems.at[TILES]))
        for k in range(REACH):
            rim_ref[C + 8 :, k * BLOCK : (k + 1) * BLOCK] = cot_ref[block + k]
        rim_ref[C : C + 8, :] = jnp.zeros((8, pad), F32)
    else:
        out_ref, rhs_ref, tab_ref, sems = rest
        copies = [None] + fetched(tab_hbm, tab_ref, sems, range(1, TILES))
    cot_rows(cot_ref, rhs_ref, 0, C)
    for tile in range(TILES):
        if copies[tile] is None:
            sums_tile(other_ref, rhs_ref, out_ref, tile, C)
        else:
            copies[tile].wait()
            sums_tile(tab_ref, rhs_ref, out_ref, tile, C)
    if first:
        for copy in later:
            copy.wait()
        rim_ref[C : C + 3, :] = pos_ref[:, lanes]


def cot_call(first, cot, tab, other, *more):
    def body(*refs):
        cot_kernel(first, *refs)

    outs = [((HALF, 2 * C), F32)]
    scratch = [
        VMEM((2 * C, ATOMS), BF16),
        VMEM((4 * HALF, ATOMS), BF16),
        pltpu.SemaphoreType.DMA((TILES + 3,)),
    ]
    if first:
        outs += [((CHUNK, ATOMS), BF16), ((HALO_ROWS, REACH * BLOCK), F32)]
        scratch.append(VMEM((3, ATOMS), F32))
    return call(
        body,
        (cot, tab, other, *more),
        outs,
        scratch,
        2 * 10**9,
        far=(1, 2, 3, 4) if first else (1,),
    )


def merge_kernel(feat_ref, cot_ref, feat_got_ref, cot_got_ref, out_ref):
    for k in range(8):
        rows = slice(k * SHARE, (k + 1) * SHARE)
        for trig in range(2):
            for part in range(2):
                lanes = slice((2 * trig + part) * C, (2 * trig + part + 1) * C)
                here = slice(trig * C, (trig + 1) * C)
                own = (feat_ref, cot_ref)[part]
                got = (feat_got_ref, cot_got_ref)[part]
                out_ref[k, :, lanes] = own[rows, here] + got[rows, here]


def give_back_kernel(own, sums_ref, filt_hbm, tab_hbm, other_ref, *rest):
    if own:
        acc_ref, next_ref, lhs_ref, tab_ref, filt_ref, sems = rest
    else:
        acc_ref, out_hbm, lhs_ref, tab_ref, filt_ref, sems, out_ref = rest
    core = lax.axis_index("atom") % 2
    at = pl.multiple_of(HALF * (core if own else 1 - core), HALF)
    fetch = pltpu.make_async_copy(
        filt_hbm.at[:, pl.ds(at, HALF)], filt_ref, sems.at[TILES]
    )
    fetch.start()
    if own:
        copies = fetched(tab_hbm, tab_ref, sems, range(TILES))
        later = ahead(other_ref, next_ref, sems.at[TILES + 1])
    else:
        copies = [None] + fetched(tab_hbm, tab_ref, sems, range(1, TILES))
    fetch.wait()
    scale = 1.0 / (ATOM_DEV * ATOMS)
    for k in range(HALF // C):
        filt = filt_ref[:, k * C : (k + 1) * C] * scale
        tile, part = divmod(k * C, TILE)
        for trig in range(2):
            lanes = pl.ds((tile * 2 + trig) * TILE + part, C)
            for row in range(2):
                sums = sums_ref[k * C : (k + 1) * C, pl.ds((2 * trig + row) * C, C)]
                high, low = pieces(filt * sums.T)
                lhs_ref[row * C : (row + 1) * C, lanes] = high
                lhs_ref[(2 + row) * C : (3 + row) * C, lanes] = low
    width = 2 * BLOCK
    stores = []
    for n in range(TILES):
        if copies[n] is not None:
            copies[n].wait()
        table = other_ref if copies[n] is None else tab_ref
        depth = slice(n * 2 * TILE, (n + 1) * 2 * TILE)
        for k in range(ATOMS // width):
            lanes = slice(k * width, (k + 1) * width)
            top = n * CHUNK
            both = dot(lhs_ref[:, depth], table[top : top + 2 * TILE, lanes], NN)
            more = dot(
                lhs_ref[0 : 2 * C, depth],
                table[top + 2 * TILE : top + CHUNK, lanes],
                NN,
            )
            part = both[: 2 * C] + both[2 * C :] + more
            if not own and n == 0:
                part = part + acc_ref[:, lanes]
            if own and n == 0:
                acc_ref[:, lanes] = part
            elif own:
                acc_ref[:, lanes] = acc_ref[:, lanes] + part
            else:
                for side in range(2):
                    half = part[:, side * BLOCK : (side + 1) * BLOCK]
                    if n:
                        half = half + out_ref[2 * k + side]
                    out_ref[2 * k + side] = half
                if n == TILES - 1:
                    pair = pl.ds(2 * k, 2)
                    stores.append(
                        pltpu.make_async_copy(
                            out_ref.at[pair], out_hbm.at[pair], sems.at[TILES + 2 + k]
                        )
                    )
                    stores[-1].start()
    for store in stores:
        store.wait()
    if own:
        later.wait()


def give_back_call(own, sums, filt, tab, other, acc=None):
    def body(*refs):
        give_back_kernel(own, *refs)

    args = [sums, filt, tab, other]
    if own:
        outs = [((2 * C, ATOMS), F32), ((CHUNK, ATOMS), BF16)]
    else:
        args.append(acc)
        outs = [((MODE_DEV, 2 * C, BLOCK), F32)]
    return call(
        body,
        args,
        outs,
        [
            VMEM((4 * C, 2 * HALF), BF16),
            VMEM((4 * HALF, ATOMS), BF16),
            VMEM((C, HALF), F32),
            pltpu.SemaphoreType.DMA((TILES + 2 + ATOMS // (2 * BLOCK),)),
        ]
        + ([] if own else [VMEM(outs[0][0], F32)]),
        4 * 10**9,
        far=(1, 2, 3) if own else (1, 2),
        far_outs=() if own else (0,),
    )


def grad_kernel(own_ref, oth_ref, grad_ref):
    core = lax.axis_index("atom") % 2
    scale = 1.0 / (ATOM_DEV * ATOMS)
    for half in range(2):
        ref = (own_ref, oth_ref)[half]
        at = pl.multiple_of(HALF * (core if half == 0 else 1 - core), HALF)
        for k in range(HALF // C):
            rows = slice(k * C, (k + 1) * C)
            grad = (
                ref[rows, 0:C] * ref[rows, C : 2 * C]
                + ref[rows, 2 * C : 3 * C] * ref[rows, 3 * C :]
            )
            grad_ref[:, pl.ds(pl.multiple_of(at + k * C, C), C)] = grad.T * scale


def near_kernel(
    rim_ref,
    feat_ref,
    pos_ref,
    cot_ref,
    mix_hbm,
    rate_ref,
    out_ref,
    back_ref,
    ext_ref,
    rhs_ref,
    mix_ref,
    pos_vmem,
    sems,
):
    own = lax.axis_index("mode")
    pad = REACH * BLOCK
    middle = pl.ds(pad, ATOMS)
    rim_at = jnp.where(own < MODE_DEV // 2, 0, pad + ATOMS)
    moves = [
        (pos_ref, pos_vmem),
        (rim_ref, ext_ref.at[:, pl.ds(pl.multiple_of(rim_at, BLOCK), pad)]),
        (feat_ref, ext_ref.at[pl.ds(0, C), middle]),
        (mix_hbm, mix_ref),
    ]
    for k in range(MODE_DEV):
        lanes = pl.ds(pad + k * BLOCK, BLOCK)
        moves.append((cot_ref.at[k], ext_ref.at[pl.ds(C + 8, C + 8), lanes]))
    copies = [
        pltpu.make_async_copy(src, dst, sems.at[k]) for k, (src, dst) in enumerate(moves)
    ]
    for copy in copies:
        copy.start()
    for copy in copies:
        copy.wait()
    ext_ref[C : C + 3, pad : pad + ATOMS] = pos_vmem[...]
    shard = lax.axis_index("atom")
    total_blocks = ATOM_DEV * MODE_DEV

    def unit(block, row):
        return row * float(total_blocks) - block.astype(F32)

    def halves(row):
        q = row - 0.5
        y = q * q
        s = q * (
            3.14159265
            + y
            * (-5.16771276 + y * (2.55016332 + y * (-0.5992522 + y * (0.0820504 - 0.00702839 * y))))
        )
        c = 1.0 + y * (
            -4.93480214
            + y * (4.05870916 + y * (-1.335212 + y * (0.23493731 - 0.02439632 * y)))
        )
        return -s, c

    me = shard * MODE_DEV + own
    here = ext_ref[C : C + 8, pl.ds(pl.multiple_of(pad + own * BLOCK, BLOCK), BLOCK)]
    u_own = unit(me, here[0:1])
    c1, s1 = halves(here[1:2])
    c2, s2 = halves(here[2:3])
    columns = columns_of((u_own, c1, s1, c2, s2))
    wide = [jnp.broadcast_to(columns[:, k : k + 1], (BLOCK, BLOCK)) for k in range(5)]
    span = 2 * REACH + 1
    dist = []
    live = ext_ref[264:265, pl.ds(pl.multiple_of(pad + own * BLOCK, BLOCK), BLOCK)]
    for o in range(span):
        at = pl.ds(pl.multiple_of((own + o) * BLOCK, BLOCK), BLOCK)
        block = ext_ref[:, at]
        there = lax.rem(me + o - REACH + total_blocks, total_blocks)
        near = block[C : C + 8]
        x = wide[0] - (unit(there, near[0:1]) + float(o - REACH))
        d1c, d1s = halves(near[1:2])
        d2c, d2s = halves(near[2:3])
        y = x * x
        z = y * (3.14159265 / total_blocks) ** 2
        d = y * (1.0 + z * (-1.0 / 3.0 + z * (2.0 / 45.0)))
        e1 = wide[2] * d1c - wide[1] * d1s
        e2 = wide[4] * d2c - wide[3] * d2s
        d = d + (e1 * e1 + e2 * e2) * (2.0 / 3.14159265) ** 2
        dist.append(d)
        lanes = slice(o * BLOCK, (o + 1) * BLOCK)
        high, low = pieces(block[0:C] * live[0:1, o : o + 1])
        rhs_ref[0:C, lanes] = high
        rhs_ref[2 * C : 3 * C, lanes] = low
        lists_me = block[264:265, span - 1 - o : span - o]
        high, low = pieces(block[136 : 136 + C] * lists_me)
        rhs_ref[C : 2 * C, lanes] = high
        rhs_ref[3 * C :, lanes] = low
    out = ext_ref[0:C, pl.ds(pl.multiple_of(pad + own * BLOCK, BLOCK), BLOCK)]
    back = ext_ref[136 : 136 + C, pl.ds(pl.multiple_of(pad + own * BLOCK, BLOCK), BLOCK)]
    for r in range(RADIAL):
        rate = rate_ref[r]
        highs, lows = [], []
        for o in range(span):
            high, low = pieces(jnp.exp(dist[o] * -rate))
            highs.append(high)
            lows.append(low)
        weights_high = jnp.concatenate(highs, axis=1)
        weights_low = jnp.concatenate(lows, axis=1)
        both = dot(rhs_ref[...], weights_high, NT)
        got = (
            both[: 2 * C]
            + both[2 * C :]
            + dot(rhs_ref[0 : 2 * C, :], weights_low, NT)
        )
        high, low = pieces(got)
        mix = mix_ref[r]
        mh, ml = pieces(mix)
        th, tl = pieces(mix.T)
        out = out + (
            dot(th, high[:C], NN) + dot(th, low[:C], NN) + dot(tl, high[:C], NN)
        )
        back = back + (
            dot(mh, high[C:], NN) + dot(mh, low[C:], NN) + dot(ml, high[C:], NN)
        )
    out_ref[...] = out
    back_ref[...] = back


def near_call(rim, feat, pos, cot, mix, rates):
    return call(
        near_kernel,
        (rim, feat, pos, cot, mix, rates),
        (((C, BLOCK), F32), ((C, BLOCK), F32)),
        [
            VMEM((HALO_ROWS, ATOMS + 2 * REACH * BLOCK), F32),
            VMEM((4 * C, (2 * REACH + 1) * BLOCK), BF16),
            VMEM((RADIAL, C, C), F32),
            VMEM((3, ATOMS), F32),
            pltpu.SemaphoreType.DMA((4 + MODE_DEV,)),
        ],
        2 * 10**9,
        smem=(5,),
        any_in=(0, 1, 2, 3, 4),
    )


def pack_kernel(ids_hbm, live_ref, cot_hbm, pos_hbm, wave_hbm, *rest):
    out_hbm, pos_ref, wave_ref, ids_ref, pack_ref, sems = rest
    fetches = [
        pltpu.make_async_copy(cot_hbm, pack_ref.at[pl.ds(0, C)], sems.at[MODE_DEV]),
        pltpu.make_async_copy(ids_hbm, ids_ref, sems.at[MODE_DEV + 1]),
        pltpu.make_async_copy(pos_hbm, pos_ref, sems.at[MODE_DEV + 2]),
        pltpu.make_async_copy(wave_hbm, wave_ref, sems.at[MODE_DEV + 3]),
    ]
    for fetch in fetches:
        fetch.start()
    total_blocks = ATOM_DEV * MODE_DEV
    me = lax.axis_index("atom") * MODE_DEV + lax.axis_index("mode")
    lane = lax.broadcasted_iota(jnp.int32, (8, BLOCK), 1)
    live = jnp.zeros((8, BLOCK), F32)
    fetches[1].wait()
    for slot in range(SLOTS):
        offset = lax.rem(ids_ref[0, slot] - me + REACH + total_blocks, total_blocks)
        offset = jnp.where(slot < live_ref[0], offset, BLOCK)
        live = jnp.where(lane == offset, 1.0, live)
    pack_ref[C:, :] = live
    fetches[0].wait()
    copies = [
        pltpu.make_async_copy(pack_ref, out_hbm.at[k], sems.at[k]) for k in range(MODE_DEV)
    ]
    for copy in copies:
        copy.start()
    for copy in copies + fetches[2:]:
        copy.wait()


def share_kernel(parts_ref, out_ref):
    share = parts_ref[0]
    for k in range(1, ATOM_DEV // 2):
        share = share + parts_ref[k]
    for k in range(ATOM_DEV // 2):
        out_ref[k] = share


def finish_kernel(near_ref, back_ref, parts_ref, out_ref, grad_ref):
    out = near_ref[...]
    grad = back_ref[...]
    for k in range(MODE_DEV):
        out = out + parts_ref[k, 0:C]
        grad = grad + parts_ref[k, C:]
    out_ref[...] = out
    grad_ref[...] = grad


def per_device(
    features,
    positions,
    wavevectors,
    mode_filter,
    radial_mix,
    radial_rates,
    neighbour_ids,
    live_counts,
    cotangent,
):
    core_swap = [(i, i ^ 1) for i in range(ATOM_DEV)]
    chips = [[c + 2 * i for i in range(ATOM_DEV // 2)] for c in range(2)]
    rims = []
    for i in range(ATOM_DEV):
        for m in range(REACH):
            after = (i + 1) % ATOM_DEV
            rims.append((i * MODE_DEV + m, after * MODE_DEV + m))
            last = MODE_DEV - 1 - m
            rims.append((after * MODE_DEV + last, i * MODE_DEV + last))

    def exchange(x):
        return lax.all_to_all(x, "atom", 0, 0, axis_index_groups=chips, tiled=True)

    packed, pos_near, wave_near = call(
        pack_kernel,
        (neighbour_ids, live_counts, cotangent, positions, wavevectors),
        (
            ((MODE_DEV, C + 8, BLOCK), F32),
            (positions.shape, F32),
            (wavevectors.shape, jnp.int32),
        ),
        [
            pltpu.SMEM((1, SLOTS), jnp.int32),
            VMEM((C + 8, BLOCK), F32),
            pltpu.SemaphoreType.DMA((MODE_DEV + 4,)),
        ],
        smem=(1,),
        far=(0, 2, 3, 4),
        far_outs=(0,),
    )
    cot = lax.all_to_all(packed, "mode", 0, 0, tiled=True)

    f_own, tab_own = tables_call(True, features, pos_near, wave_near, packed)
    f_oth, tab_oth = tables_call(False, features, pos_near, wave_near, tab_own)
    f_got = lax.ppermute(f_oth, "atom", core_swap)
    cot, f_oth = lax.optimization_barrier((cot, f_oth))
    c_oth, tab_next, rim = cot_call(True, cot, tab_oth, tab_own, features, positions)
    rim = lax.ppermute(rim, ("atom", "mode"), rims)
    c_got = lax.ppermute(c_oth, "atom", core_swap)
    cot, c_oth = lax.optimization_barrier((cot, c_oth))
    (c_own,) = cot_call(False, cot, tab_own, tab_next)
    (parts,) = call(
        merge_kernel, (f_own, c_own, f_got, c_got), (((8, SHARE, 4 * C), F32),)
    )
    parts = exchange(parts)
    (share,) = call(share_kernel, (parts,), ((parts.shape, F32),))
    own = exchange(share).reshape(HALF, 4 * C)
    oth = lax.ppermute(own, "atom", core_swap)
    acc, tab_next = give_back_call(True, own, mode_filter, tab_own, tab_oth)
    (back,) = give_back_call(False, oth, mode_filter, tab_oth, tab_next, acc)
    back, cot, rim = lax.optimization_barrier((back, cot, rim))
    near_out, near_back = near_call(
        rim, features, positions, cot, radial_mix, radial_rates
    )
    back = lax.all_to_all(back, "mode", 0, 0, tiled=True)
    (grad_filter,) = call(
        grad_kernel, (own, oth), (((C, MODES), F32),), plain=(0,), args_in=(0, 1)
    )
    layer_out, grad_features = call(
        finish_kernel,
        (near_out, near_back, back),
        (((C, BLOCK), F32), ((C, BLOCK), F32)),
        plain=(0, 1),
        args_in=(0, 1),
    )
    return (layer_out, grad_features, grad_filter)


def solution(mesh):
    in_specs = (
        P(None, "atom"),
        P(None, "atom"),
        P(None, "mode"),
        P(None, "mode"),
        P(),
        P(),
        P(("atom", "mode"), None),
        P(("atom", "mode")),
        P(None, ("atom", "mode")),
    )
    out_specs = (P(None, ("atom", "mode")), P(None, ("atom", "mode")), P(None, "mode"))
    return jax.shard_map(
        per_device, mesh=mesh, in_specs=in_specs, out_specs=out_specs, check_vma=False
    )
```

```python
import jax
import jax.numpy as jnp
from jax import lax
from jax.experimental import pallas as pl
from jax.experimental.pallas import tpu as pltpu
from jax.sharding import PartitionSpec as P


BLOCK = 128
REACH = 2
SLOTS = 5
C = 128
ATOMS = 1024
MODES = 1024
HALF = 512
SHARE = 64
RADIAL = 4
ATOM_DEV = 16
MODE_DEV = 8
HALO_ROWS = 272

F32 = jnp.float32
BF16 = jnp.bfloat16
MAGIC = 12582912.0
LIMIT = 24 * 1024 * 1024
VMEM = pltpu.VMEM

NT = (((1,), (1,)), ((), ()))
NN = (((1,), (0,)), ((), ()))


def dot(a, b, dims):
    return lax.dot_general(a, b, dims, preferred_element_type=F32)


def pieces(x):
    high = x.astype(BF16)
    low = (x - high.astype(F32)).astype(BF16)
    return high, low


def cos_sin_turns(t):
    r = t - ((t + MAGIC) - MAGIC)
    y = r * r
    s = r * (4.44287957 + y * (-7.30781668 + y * (3.59777418 + y * -0.79119939)))
    c = 1.4142135 + y * (
        -6.97885095 + y * (5.73946038 + y * (-1.88355791 + y * 0.31068803))
    )
    return 1.0 - s * s, s * c


ROWS = 32
TILE = 256
CHUNK = 4 * TILE
TILES = HALF // TILE


def columns_of(rows):
    rows = list(rows)
    rows = rows + [rows[0]] * (8 - len(rows))
    eight = jnp.concatenate(rows, axis=0)
    return jnp.concatenate([eight] * (BLOCK // 8), axis=0).T


def tables_tile(pos_ref, wave_ref, tab_ref, first, tile, leave):
    shard = lax.axis_index("atom")
    mid = (2 * shard + 1).astype(F32) * (1.0 / 32.0)
    for group in range(TILE // BLOCK):
        at = tile * TILE + group * BLOCK
        w = wave_ref[:, pl.ds(pl.multiple_of(first + at, BLOCK), BLOCK)]
        start = ((w[0:1] * (2 * shard + 1)) & 31).astype(F32) * (1.0 / 32.0)
        wf = w.astype(F32)
        columns = columns_of((wf[0:1], wf[1:2], wf[2:3], start))
        for chunk in range(BLOCK // ROWS):
            part = columns[chunk * ROWS : (chunk + 1) * ROWS]
            w0, w1, w2, c0 = (
                jnp.broadcast_to(part[:, d : d + 1], (ROWS, BLOCK)) for d in range(4)
            )
            row = tile * CHUNK + group * BLOCK + chunk * ROWS
            for k in range(ATOMS // BLOCK):
                lanes = pl.ds(k * BLOCK, BLOCK)
                p0 = pos_ref[0:1, lanes] - mid
                p1 = pos_ref[1:2, lanes]
                p2 = pos_ref[2:3, lanes]
                t = w0 * p0 + (w1 * p1 + (w2 * p2 + c0))
                cos, sin = cos_sin_turns(t)
                ch, cl = pieces(cos)
                sh, sl = pieces(sin)
                tab_ref[row : row + ROWS, lanes] = ch
                tab_ref[TILE + row : TILE + row + ROWS, lanes] = sh
                tab_ref[2 * TILE + row : 2 * TILE + row + ROWS, lanes] = cl
                tab_ref[3 * TILE + row : 3 * TILE + row + ROWS, lanes] = sl
        leave(tile * CHUNK + group * BLOCK)


def sums_tile(tab_ref, rhs_ref, out_ref, tile, wide, copies=()):
    at = tile * CHUNK
    for copy in copies:
        copy.wait()
    both = dot(tab_ref[at : at + 2 * TILE, :], rhs_ref[...], NT)
    rest = dot(tab_ref[at + 2 * TILE : at + CHUNK, :], rhs_ref[0:wide, :], NT)
    total = both[:, :wide] + both[:, wide:] + rest
    for trig in range(2):
        out_ref[tile * TILE : (tile + 1) * TILE, trig * wide : (trig + 1) * wide] = (
            total[trig * TILE : (trig + 1) * TILE]
        )


def cot_rows(cot_ref, rhs_ref, high_at, low_at):
    for k in range(MODE_DEV):
        high, low = pieces(cot_ref[k, 0:C, :])
        rhs_ref[high_at : high_at + C, k * BLOCK : (k + 1) * BLOCK] = high
        rhs_ref[low_at : low_at + C, k * BLOCK : (k + 1) * BLOCK] = low


def tables_kernel(own, feat_hbm, pos_ref, wave_ref, dep_ref, *rest):
    out_ref, tab_hbm, rhs_ref, tab_ref, feat_ref, sems = rest
    fetch = pltpu.make_async_copy(feat_hbm, feat_ref, sems.at[0])
    fetch.start()
    core = lax.axis_index("atom") % 2
    first = HALF * (core if own else 1 - core)
    copies = []

    def leave(row):
        for kind in range(4):
            rows = pl.ds(row + kind * TILE, BLOCK)
            sem = sems.at[1 + len(copies)]
            copies.append(
                pltpu.make_async_copy(tab_ref.at[rows], tab_hbm.at[rows], sem)
            )
            copies[-1].start()

    for tile in range(TILES):
        tables_tile(pos_ref, wave_ref, tab_ref, first, tile, leave)
        if tile == 0:
            fetch.wait()
            high, low = pieces(feat_ref[...])
            rhs_ref[0:C, :] = high
            rhs_ref[C:, :] = low
        sums_tile(tab_ref, rhs_ref, out_ref, tile, C)
    for copy in copies:
        copy.wait()


def spec():
    return pl.BlockSpec(memory_space=VMEM)


def call(body, ins, outs, scratch=(), flops=10**8, smem=(), far=(), far_outs=(), plain=(), args_in=(), any_in=()):
    args, in_specs = [], []
    for k, x in enumerate(ins):
        if k in smem:
            in_specs.append(pl.BlockSpec(memory_space=pltpu.SMEM))
        elif k in any_in:
            in_specs.append(pl.BlockSpec(memory_space=pl.ANY))
        elif k in far:
            in_specs.append(pl.BlockSpec(memory_space=pltpu.HBM))
            x = pltpu.with_memory_space_constraint(x, pltpu.HBM)
        else:
            in_specs.append(spec())
            if k not in args_in:
                x = pltpu.with_memory_space_constraint(x, VMEM)
        args.append(x)
    size = sum(x.size * x.dtype.itemsize for x in ins)
    return pl.pallas_call(
        body,
        out_shape=tuple(
            pltpu.HBM(shape, kind)
            if k in far_outs
            else (jax.ShapeDtypeStruct if k in plain else VMEM)(shape, kind)
            for k, (shape, kind) in enumerate(outs)
        ),
        in_specs=in_specs,
        out_specs=tuple(
            pl.BlockSpec(memory_space=pltpu.HBM) if k in far_outs else spec()
            for k in range(len(outs))
        ),
        scratch_shapes=list(scratch),
        compiler_params=pltpu.CompilerParams(vmem_limit_bytes=LIMIT),
        cost_estimate=pl.CostEstimate(
            flops=flops, bytes_accessed=size, transcendentals=0
        ),
    )(*args)


def tables_call(own, feat, pos, wave, dep):
    def body(*refs):
        tables_kernel(own, *refs)

    return call(
        body,
        (feat, pos, wave, dep),
        (((HALF, 2 * C), F32), ((4 * HALF, ATOMS), BF16)),
        [
            VMEM((2 * C, ATOMS), BF16),
            VMEM((4 * HALF, ATOMS), BF16),
            VMEM((C, ATOMS), F32),
            pltpu.SemaphoreType.DMA((1 + 4 * HALF // BLOCK,)),
        ],
        4 * 10**9,
        far=(0, 3),
        far_outs=(1,),
    )


def fetched(tab_hbm, tab_ref, sems, tiles):
    copies = []
    for tile in tiles:
        rows = pl.ds(tile * CHUNK, CHUNK)
        copy = pltpu.make_async_copy(tab_hbm.at[rows], tab_ref.at[rows], sems.at[tile])
        copy.start()
        copies.append(copy)
    return copies


def ahead(next_hbm, next_ref, sem):
    copy = pltpu.make_async_copy(next_hbm.at[pl.ds(0, CHUNK)], next_ref, sem)
    copy.start()
    return copy


def cot_kernel(first, cot_ref, tab_hbm, other_ref, *rest):
    if first:
        feat_hbm, pos_hbm, out_ref, next_ref, rim_ref, rhs_ref, tab_ref, sems, pos_ref = rest
        copies = fetched(tab_hbm, tab_ref, sems, range(TILES))
        pad = REACH * BLOCK
        tail = lax.axis_index("mode") < MODE_DEV // 2
        block = jnp.where(tail, MODE_DEV - REACH, 0)
        lanes = pl.ds(pl.multiple_of(block * BLOCK, BLOCK), pad)
        later = [
            pltpu.make_async_copy(pos_hbm, pos_ref, sems.at[TILES + 1]),
            pltpu.make_async_copy(
                feat_hbm.at[:, lanes], rim_ref.at[pl.ds(0, C)], sems.at[TILES + 2]
            ),
        ]
        for copy in later:
            copy.start()
        later.append(ahead(other_ref, next_ref, sems.at[TILES]))
        for k in range(REACH):
            rim_ref[C + 8 :, k * BLOCK : (k + 1) * BLOCK] = cot_ref[block + k]
        rim_ref[C : C + 8, :] = jnp.zeros((8, pad), F32)
    else:
        out_ref, rhs_ref, tab_ref, sems = rest
        copies = [None] + fetched(tab_hbm, tab_ref, sems, range(1, TILES))
    cot_rows(cot_ref, rhs_ref, 0, C)
    for tile in range(TILES):
        if copies[tile] is None:
            sums_tile(other_ref, rhs_ref, out_ref, tile, C)
        else:
            copies[tile].wait()
            sums_tile(tab_ref, rhs_ref, out_ref, tile, C)
    if first:
        for copy in later:
            copy.wait()
        rim_ref[C : C + 3, :] = pos_ref[:, lanes]


def cot_call(first, cot, tab, other, *more):
    def body(*refs):
        cot_kernel(first, *refs)

    outs = [((HALF, 2 * C), F32)]
    scratch = [
        VMEM((2 * C, ATOMS), BF16),
        VMEM((4 * HALF, ATOMS), BF16),
        pltpu.SemaphoreType.DMA((TILES + 3,)),
    ]
    if first:
        outs += [((CHUNK, ATOMS), BF16), ((HALO_ROWS, REACH * BLOCK), F32)]
        scratch.append(VMEM((3, ATOMS), F32))
    return call(
        body,
        (cot, tab, other, *more),
        outs,
        scratch,
        2 * 10**9,
        far=(1, 2, 3, 4) if first else (1,),
    )


def merge_kernel(feat_ref, cot_ref, feat_got_ref, cot_got_ref, out_ref):
    for k in range(8):
        rows = slice(k * SHARE, (k + 1) * SHARE)
        for trig in range(2):
            for part in range(2):
                lanes = slice((2 * trig + part) * C, (2 * trig + part + 1) * C)
                here = slice(trig * C, (trig + 1) * C)
                own = (feat_ref, cot_ref)[part]
                got = (feat_got_ref, cot_got_ref)[part]
                out_ref[k, :, lanes] = own[rows, here] + got[rows, here]


def give_back_kernel(own, sums_ref, filt_hbm, tab_hbm, other_ref, *rest):
    if own:
        acc_ref, next_ref, filt_ref, lhs_ref, tab_ref, sems = rest
    else:
        acc_ref, out_hbm, lhs_ref, tab_ref, sems, out_ref = rest
        filt_ref = filt_hbm
    core = lax.axis_index("atom") % 2
    at = pl.multiple_of(HALF * (core if own else 1 - core), HALF)
    if own:
        fetch = pltpu.make_async_copy(filt_hbm, filt_ref, sems.at[TILES])
        fetch.start()
        copies = fetched(tab_hbm, tab_ref, sems, range(TILES))
        later = ahead(other_ref, next_ref, sems.at[TILES + 1])
    else:
        copies = [None] + fetched(tab_hbm, tab_ref, sems, range(1, TILES))
    if own:
        fetch.wait()
    scale = 1.0 / (ATOM_DEV * ATOMS)
    for k in range(HALF // C):
        filt = filt_ref[:, pl.ds(pl.multiple_of(at + k * C, C), C)] * scale
        tile, part = divmod(k * C, TILE)
        for trig in range(2):
            lanes = pl.ds((tile * 2 + trig) * TILE + part, C)
            for row in range(2):
                sums = sums_ref[k * C : (k + 1) * C, pl.ds((2 * trig + row) * C, C)]
                high, low = pieces(filt * sums.T)
                lhs_ref[row * C : (row + 1) * C, lanes] = high
                lhs_ref[(2 + row) * C : (3 + row) * C, lanes] = low
    width = 2 * BLOCK
    stores = []
    for n in range(TILES):
        if copies[n] is not None:
            copies[n].wait()
        table = other_ref if copies[n] is None else tab_ref
        depth = slice(n * 2 * TILE, (n + 1) * 2 * TILE)
        for k in range(ATOMS // width):
            lanes = slice(k * width, (k + 1) * width)
            top = n * CHUNK
            both = dot(lhs_ref[:, depth], table[top : top + 2 * TILE, lanes], NN)
            more = dot(
                lhs_ref[0 : 2 * C, depth],
                table[top + 2 * TILE : top + CHUNK, lanes],
                NN,
            )
            part = both[: 2 * C] + both[2 * C :] + more
            if not own and n == 0:
                part = part + acc_ref[:, lanes]
            if own and n == 0:
                acc_ref[:, lanes] = part
            elif own:
                acc_ref[:, lanes] = acc_ref[:, lanes] + part
            else:
                for side in range(2):
                    half = part[:, side * BLOCK : (side + 1) * BLOCK]
                    if n:
                        half = half + out_ref[2 * k + side]
                    out_ref[2 * k + side] = half
                if n == TILES - 1:
                    pair = pl.ds(2 * k, 2)
                    stores.append(
                        pltpu.make_async_copy(
                            out_ref.at[pair], out_hbm.at[pair], sems.at[TILES + 2 + k]
                        )
                    )
                    stores[-1].start()
    for store in stores:
        store.wait()
    if own:
        later.wait()


def give_back_call(own, sums, filt, tab, other, acc=None):
    def body(*refs):
        give_back_kernel(own, *refs)

    args = [sums, filt, tab, other]
    if own:
        outs = [((2 * C, ATOMS), F32), ((CHUNK, ATOMS), BF16), ((C, MODES), F32)]
    else:
        args.append(acc)
        outs = [((MODE_DEV, 2 * C, BLOCK), F32)]
    return call(
        body,
        args,
        outs,
        [
            VMEM((4 * C, 2 * HALF), BF16),
            VMEM((4 * HALF, ATOMS), BF16),
            pltpu.SemaphoreType.DMA((TILES + 2 + ATOMS // (2 * BLOCK),)),
        ]
        + ([] if own else [VMEM(outs[0][0], F32)]),
        4 * 10**9,
        far=(1, 2, 3) if own else (2,),
        far_outs=() if own else (0,),
    )


def grad_kernel(own_ref, oth_ref, grad_ref):
    core = lax.axis_index("atom") % 2
    scale = 1.0 / (ATOM_DEV * ATOMS)
    for half in range(2):
        ref = (own_ref, oth_ref)[half]
        at = pl.multiple_of(HALF * (core if half == 0 else 1 - core), HALF)
        for k in range(HALF // C):
            rows = slice(k * C, (k + 1) * C)
            grad = (
                ref[rows, 0:C] * ref[rows, C : 2 * C]
                + ref[rows, 2 * C : 3 * C] * ref[rows, 3 * C :]
            )
            grad_ref[:, pl.ds(pl.multiple_of(at + k * C, C), C)] = grad.T * scale


def near_kernel(
    rim_ref,
    feat_ref,
    pos_ref,
    cot_ref,
    mix_hbm,
    rate_ref,
    out_ref,
    back_ref,
    ext_ref,
    rhs_ref,
    mix_ref,
    pos_vmem,
    sems,
):
    own = lax.axis_index("mode")
    pad = REACH * BLOCK
    middle = pl.ds(pad, ATOMS)
    rim_at = jnp.where(own < MODE_DEV // 2, 0, pad + ATOMS)
    moves = [
        (pos_ref, pos_vmem),
        (rim_ref, ext_ref.at[:, pl.ds(pl.multiple_of(rim_at, BLOCK), pad)]),
        (feat_ref, ext_ref.at[pl.ds(0, C), middle]),
        (mix_hbm, mix_ref),
    ]
    for k in range(MODE_DEV):
        lanes = pl.ds(pad + k * BLOCK, BLOCK)
        moves.append((cot_ref.at[k], ext_ref.at[pl.ds(C + 8, C + 8), lanes]))
    copies = [
        pltpu.make_async_copy(src, dst, sems.at[k]) for k, (src, dst) in enumerate(moves)
    ]
    for copy in copies:
        copy.start()
    for copy in copies:
        copy.wait()
    ext_ref[C : C + 3, pad : pad + ATOMS] = pos_vmem[...]
    shard = lax.axis_index("atom")
    total_blocks = ATOM_DEV * MODE_DEV

    def unit(block, row):
        return row * float(total_blocks) - block.astype(F32)

    def halves(row):
        q = row - 0.5
        y = q * q
        s = q * (
            3.14159265
            + y
            * (-5.16771276 + y * (2.55016332 + y * (-0.5992522 + y * (0.0820504 - 0.00702839 * y))))
        )
        c = 1.0 + y * (
            -4.93480214
            + y * (4.05870916 + y * (-1.335212 + y * (0.23493731 - 0.02439632 * y)))
        )
        return -s, c

    me = shard * MODE_DEV + own
    here = ext_ref[C : C + 8, pl.ds(pl.multiple_of(pad + own * BLOCK, BLOCK), BLOCK)]
    u_own = unit(me, here[0:1])
    c1, s1 = halves(here[1:2])
    c2, s2 = halves(here[2:3])
    columns = columns_of((u_own, c1, s1, c2, s2))
    wide = [jnp.broadcast_to(columns[:, k : k + 1], (BLOCK, BLOCK)) for k in range(5)]
    span = 2 * REACH + 1
    dist = []
    live = ext_ref[264:265, pl.ds(pl.multiple_of(pad + own * BLOCK, BLOCK), BLOCK)]
    for o in range(span):
        at = pl.ds(pl.multiple_of((own + o) * BLOCK, BLOCK), BLOCK)
        block = ext_ref[:, at]
        there = lax.rem(me + o - REACH + total_blocks, total_blocks)
        near = block[C : C + 8]
        x = wide[0] - (unit(there, near[0:1]) + float(o - REACH))
        d1c, d1s = halves(near[1:2])
        d2c, d2s = halves(near[2:3])
        y = x * x
        z = y * (3.14159265 / total_blocks) ** 2
        d = y * (1.0 + z * (-1.0 / 3.0 + z * (2.0 / 45.0)))
        e1 = wide[2] * d1c - wide[1] * d1s
        e2 = wide[4] * d2c - wide[3] * d2s
        d = d + (e1 * e1 + e2 * e2) * (2.0 / 3.14159265) ** 2
        dist.append(d)
        lanes = slice(o * BLOCK, (o + 1) * BLOCK)
        high, low = pieces(block[0:C] * live[0:1, o : o + 1])
        rhs_ref[0:C, lanes] = high
        rhs_ref[2 * C : 3 * C, lanes] = low
        lists_me = block[264:265, span - 1 - o : span - o]
        high, low = pieces(block[136 : 136 + C] * lists_me)
        rhs_ref[C : 2 * C, lanes] = high
        rhs_ref[3 * C :, lanes] = low
    out = ext_ref[0:C, pl.ds(pl.multiple_of(pad + own * BLOCK, BLOCK), BLOCK)]
    back = ext_ref[136 : 136 + C, pl.ds(pl.multiple_of(pad + own * BLOCK, BLOCK), BLOCK)]
    for r in range(RADIAL):
        rate = rate_ref[r]
        highs, lows = [], []
        for o in range(span):
            high, low = pieces(jnp.exp(dist[o] * -rate))
            highs.append(high)
            lows.append(low)
        weights_high = jnp.concatenate(highs, axis=1)
        weights_low = jnp.concatenate(lows, axis=1)
        both = dot(rhs_ref[...], weights_high, NT)
        got = (
            both[: 2 * C]
            + both[2 * C :]
            + dot(rhs_ref[0 : 2 * C, :], weights_low, NT)
        )
        high, low = pieces(got)
        mix = mix_ref[r]
        mh, ml = pieces(mix)
        th, tl = pieces(mix.T)
        out = out + (
            dot(th, high[:C], NN) + dot(th, low[:C], NN) + dot(tl, high[:C], NN)
        )
        back = back + (
            dot(mh, high[C:], NN) + dot(mh, low[C:], NN) + dot(ml, high[C:], NN)
        )
    out_ref[...] = out
    back_ref[...] = back


def near_call(rim, feat, pos, cot, mix, rates):
    return call(
        near_kernel,
        (rim, feat, pos, cot, mix, rates),
        (((C, BLOCK), F32), ((C, BLOCK), F32)),
        [
            VMEM((HALO_ROWS, ATOMS + 2 * REACH * BLOCK), F32),
            VMEM((4 * C, (2 * REACH + 1) * BLOCK), BF16),
            VMEM((RADIAL, C, C), F32),
            VMEM((3, ATOMS), F32),
            pltpu.SemaphoreType.DMA((4 + MODE_DEV,)),
        ],
        2 * 10**9,
        smem=(5,),
        any_in=(0, 1, 2, 3, 4),
    )


def pack_kernel(ids_hbm, live_ref, cot_hbm, pos_hbm, wave_hbm, *rest):
    out_hbm, pos_ref, wave_ref, ids_ref, pack_ref, sems = rest
    fetches = [
        pltpu.make_async_copy(cot_hbm, pack_ref.at[pl.ds(0, C)], sems.at[MODE_DEV]),
        pltpu.make_async_copy(ids_hbm, ids_ref, sems.at[MODE_DEV + 1]),
        pltpu.make_async_copy(pos_hbm, pos_ref, sems.at[MODE_DEV + 2]),
        pltpu.make_async_copy(wave_hbm, wave_ref, sems.at[MODE_DEV + 3]),
    ]
    for fetch in fetches:
        fetch.start()
    total_blocks = ATOM_DEV * MODE_DEV
    me = lax.axis_index("atom") * MODE_DEV + lax.axis_index("mode")
    lane = lax.broadcasted_iota(jnp.int32, (8, BLOCK), 1)
    live = jnp.zeros((8, BLOCK), F32)
    fetches[1].wait()
    for slot in range(SLOTS):
        offset = lax.rem(ids_ref[0, slot] - me + REACH + total_blocks, total_blocks)
        offset = jnp.where(slot < live_ref[0], offset, BLOCK)
        live = jnp.where(lane == offset, 1.0, live)
    pack_ref[C:, :] = live
    fetches[0].wait()
    copies = [
        pltpu.make_async_copy(pack_ref, out_hbm.at[k], sems.at[k]) for k in range(MODE_DEV)
    ]
    for copy in copies:
        copy.start()
    for copy in copies + fetches[2:]:
        copy.wait()


def share_kernel(parts_ref, out_ref):
    share = parts_ref[0]
    for k in range(1, ATOM_DEV // 2):
        share = share + parts_ref[k]
    for k in range(ATOM_DEV // 2):
        out_ref[k] = share


def finish_kernel(near_ref, back_ref, parts_ref, out_ref, grad_ref):
    out = near_ref[...]
    grad = back_ref[...]
    for k in range(MODE_DEV):
        out = out + parts_ref[k, 0:C]
        grad = grad + parts_ref[k, C:]
    out_ref[...] = out
    grad_ref[...] = grad


def per_device(
    features,
    positions,
    wavevectors,
    mode_filter,
    radial_mix,
    radial_rates,
    neighbour_ids,
    live_counts,
    cotangent,
):
    core_swap = [(i, i ^ 1) for i in range(ATOM_DEV)]
    chips = [[c + 2 * i for i in range(ATOM_DEV // 2)] for c in range(2)]
    rims = []
    for i in range(ATOM_DEV):
        for m in range(REACH):
            after = (i + 1) % ATOM_DEV
            rims.append((i * MODE_DEV + m, after * MODE_DEV + m))
            last = MODE_DEV - 1 - m
            rims.append((after * MODE_DEV + last, i * MODE_DEV + last))

    def exchange(x):
        return lax.all_to_all(x, "atom", 0, 0, axis_index_groups=chips, tiled=True)

    packed, pos_near, wave_near = call(
        pack_kernel,
        (neighbour_ids, live_counts, cotangent, positions, wavevectors),
        (
            ((MODE_DEV, C + 8, BLOCK), F32),
            (positions.shape, F32),
            (wavevectors.shape, jnp.int32),
        ),
        [
            pltpu.SMEM((1, SLOTS), jnp.int32),
            VMEM((C + 8, BLOCK), F32),
            pltpu.SemaphoreType.DMA((MODE_DEV + 4,)),
        ],
        smem=(1,),
        far=(0, 2, 3, 4),
        far_outs=(0,),
    )
    cot = lax.all_to_all(packed, "mode", 0, 0, tiled=True)

    f_own, tab_own = tables_call(True, features, pos_near, wave_near, packed)
    f_oth, tab_oth = tables_call(False, features, pos_near, wave_near, tab_own)
    f_got = lax.ppermute(f_oth, "atom", core_swap)
    cot, f_oth = lax.optimization_barrier((cot, f_oth))
    c_oth, tab_next, rim = cot_call(True, cot, tab_oth, tab_own, features, positions)
    rim = lax.ppermute(rim, ("atom", "mode"), rims)
    c_got = lax.ppermute(c_oth, "atom", core_swap)
    cot, c_oth = lax.optimization_barrier((cot, c_oth))
    (c_own,) = cot_call(False, cot, tab_own, tab_next)
    (parts,) = call(
        merge_kernel, (f_own, c_own, f_got, c_got), (((8, SHARE, 4 * C), F32),)
    )
    parts = exchange(parts)
    (share,) = call(share_kernel, (parts,), ((parts.shape, F32),))
    own = exchange(share).reshape(HALF, 4 * C)
    oth = lax.ppermute(own, "atom", core_swap)
    acc, tab_next, filt = give_back_call(True, own, mode_filter, tab_own, tab_oth)
    (back,) = give_back_call(False, oth, filt, tab_oth, tab_next, acc)
    back, cot, rim = lax.optimization_barrier((back, cot, rim))
    near_out, near_back = near_call(
        rim, features, positions, cot, radial_mix, radial_rates
    )
    back = lax.all_to_all(back, "mode", 0, 0, tiled=True)
    (grad_filter,) = call(
        grad_kernel, (own, oth), (((C, MODES), F32),), plain=(0,), args_in=(0, 1)
    )
    layer_out, grad_features = call(
        finish_kernel,
        (near_out, near_back, back),
        (((C, BLOCK), F32), ((C, BLOCK), F32)),
        plain=(0, 1),
        args_in=(0, 1),
    )
    return (layer_out, grad_features, grad_filter)


def solution(mesh):
    in_specs = (
        P(None, "atom"),
        P(None, "atom"),
        P(None, "mode"),
        P(None, "mode"),
        P(),
        P(),
        P(("atom", "mode"), None),
        P(("atom", "mode")),
        P(None, ("atom", "mode")),
    )
    out_specs = (P(None, ("atom", "mode")), P(None, ("atom", "mode")), P(None, "mode"))
    return jax.shard_map(
        per_device, mesh=mesh, in_specs=in_specs, out_specs=out_specs, check_vma=False
    )
```

```python
import jax
import jax.numpy as jnp
from jax import lax
from jax.experimental import pallas as pl
from jax.experimental.pallas import tpu as pltpu
from jax.sharding import PartitionSpec as P


BLOCK = 128
REACH = 2
SLOTS = 5
C = 128
ATOMS = 1024
MODES = 1024
HALF = 512
SHARE = 64
RADIAL = 4
ATOM_DEV = 16
MODE_DEV = 8
HALO_ROWS = 272

F32 = jnp.float32
BF16 = jnp.bfloat16
MAGIC = 12582912.0
LIMIT = 24 * 1024 * 1024
VMEM = pltpu.VMEM

NT = (((1,), (1,)), ((), ()))
NN = (((1,), (0,)), ((), ()))


def dot(a, b, dims):
    return lax.dot_general(a, b, dims, preferred_element_type=F32)


def pieces(x):
    high = x.astype(BF16)
    low = (x - high.astype(F32)).astype(BF16)
    return high, low


def cos_sin_turns(t):
    r = t - ((t + MAGIC) - MAGIC)
    y = r * r
    s = r * (4.44287957 + y * (-7.30781668 + y * (3.59777418 + y * -0.79119939)))
    c = 1.4142135 + y * (
        -6.97885095 + y * (5.73946038 + y * (-1.88355791 + y * 0.31068803))
    )
    return 1.0 - s * s, s * c


ROWS = 32
TILE = 256
CHUNK = 4 * TILE
TILES = HALF // TILE
AHEAD = 2 * TILE


def columns_of(rows):
    rows = list(rows)
    rows = rows + [rows[0]] * (8 - len(rows))
    eight = jnp.concatenate(rows, axis=0)
    return jnp.concatenate([eight] * (BLOCK // 8), axis=0).T


def tables_tile(pos_ref, wave_ref, tab_ref, first, tile, leave):
    shard = lax.axis_index("atom")
    mid = (2 * shard + 1).astype(F32) * (1.0 / 32.0)
    for group in range(TILE // BLOCK):
        at = tile * TILE + group * BLOCK
        w = wave_ref[:, pl.ds(pl.multiple_of(first + at, BLOCK), BLOCK)]
        start = ((w[0:1] * (2 * shard + 1)) & 31).astype(F32) * (1.0 / 32.0)
        wf = w.astype(F32)
        columns = columns_of((wf[0:1], wf[1:2], wf[2:3], start))
        for chunk in range(BLOCK // ROWS):
            part = columns[chunk * ROWS : (chunk + 1) * ROWS]
            w0, w1, w2, c0 = (
                jnp.broadcast_to(part[:, d : d + 1], (ROWS, BLOCK)) for d in range(4)
            )
            row = tile * CHUNK + group * BLOCK + chunk * ROWS
            for k in range(ATOMS // BLOCK):
                lanes = pl.ds(k * BLOCK, BLOCK)
                p0 = pos_ref[0:1, lanes] - mid
                p1 = pos_ref[1:2, lanes]
                p2 = pos_ref[2:3, lanes]
                t = w0 * p0 + (w1 * p1 + (w2 * p2 + c0))
                cos, sin = cos_sin_turns(t)
                ch, cl = pieces(cos)
                sh, sl = pieces(sin)
                tab_ref[row : row + ROWS, lanes] = ch
                tab_ref[TILE + row : TILE + row + ROWS, lanes] = sh
                tab_ref[2 * TILE + row : 2 * TILE + row + ROWS, lanes] = cl
                tab_ref[3 * TILE + row : 3 * TILE + row + ROWS, lanes] = sl
        leave(tile * CHUNK + group * BLOCK)


def sums_tile(tab_ref, rhs_ref, out_ref, tile, wide, high_ref):
    at = tile * CHUNK
    both = dot(high_ref[at : at + 2 * TILE, :], rhs_ref[...], NT)
    rest = dot(tab_ref[at + 2 * TILE : at + CHUNK, :], rhs_ref[0:wide, :], NT)
    total = both[:, :wide] + both[:, wide:] + rest
    for trig in range(2):
        out_ref[tile * TILE : (tile + 1) * TILE, trig * wide : (trig + 1) * wide] = (
            total[trig * TILE : (trig + 1) * TILE]
        )


def cot_rows(cot_ref, rhs_ref, high_at, low_at):
    for k in range(MODE_DEV):
        high, low = pieces(cot_ref[k, 0:C, :])
        rhs_ref[high_at : high_at + C, k * BLOCK : (k + 1) * BLOCK] = high
        rhs_ref[low_at : low_at + C, k * BLOCK : (k + 1) * BLOCK] = low


def tables_kernel(own, feat_hbm, pos_ref, wave_ref, dep_ref, *rest):
    out_ref, tab_hbm, rhs_ref, tab_ref, feat_ref, sems = rest
    fetch = pltpu.make_async_copy(feat_hbm, feat_ref, sems.at[0])
    fetch.start()
    core = lax.axis_index("atom") % 2
    first = HALF * (core if own else 1 - core)
    copies = []

    def leave(row):
        for kind in range(4):
            rows = pl.ds(row + kind * TILE, BLOCK)
            sem = sems.at[1 + len(copies)]
            copies.append(
                pltpu.make_async_copy(tab_ref.at[rows], tab_hbm.at[rows], sem)
            )
            copies[-1].start()

    for tile in range(TILES):
        tables_tile(pos_ref, wave_ref, tab_ref, first, tile, leave)
        if tile == 0:
            fetch.wait()
            high, low = pieces(feat_ref[...])
            rhs_ref[0:C, :] = high
            rhs_ref[C:, :] = low
        sums_tile(tab_ref, rhs_ref, out_ref, tile, C, tab_ref)
    for copy in copies:
        copy.wait()


def spec():
    return pl.BlockSpec(memory_space=VMEM)


def call(body, ins, outs, scratch=(), flops=10**8, smem=(), far=(), far_outs=(), plain=(), args_in=(), any_in=()):
    args, in_specs = [], []
    for k, x in enumerate(ins):
        if k in smem:
            in_specs.append(pl.BlockSpec(memory_space=pltpu.SMEM))
        elif k in any_in:
            in_specs.append(pl.BlockSpec(memory_space=pl.ANY))
        elif k in far:
            in_specs.append(pl.BlockSpec(memory_space=pltpu.HBM))
            x = pltpu.with_memory_space_constraint(x, pltpu.HBM)
        else:
            in_specs.append(spec())
            if k not in args_in:
                x = pltpu.with_memory_space_constraint(x, VMEM)
        args.append(x)
    size = sum(x.size * x.dtype.itemsize for x in ins)
    return pl.pallas_call(
        body,
        out_shape=tuple(
            pltpu.HBM(shape, kind)
            if k in far_outs
            else (jax.ShapeDtypeStruct if k in plain else VMEM)(shape, kind)
            for k, (shape, kind) in enumerate(outs)
        ),
        in_specs=in_specs,
        out_specs=tuple(
            pl.BlockSpec(memory_space=pltpu.HBM) if k in far_outs else spec()
            for k in range(len(outs))
        ),
        scratch_shapes=list(scratch),
        compiler_params=pltpu.CompilerParams(vmem_limit_bytes=LIMIT),
        cost_estimate=pl.CostEstimate(
            flops=flops, bytes_accessed=size, transcendentals=0
        ),
    )(*args)


def tables_call(own, feat, pos, wave, dep):
    def body(*refs):
        tables_kernel(own, *refs)

    return call(
        body,
        (feat, pos, wave, dep),
        (((HALF, 2 * C), F32), ((4 * HALF, ATOMS), BF16)),
        [
            VMEM((2 * C, ATOMS), BF16),
            VMEM((4 * HALF, ATOMS), BF16),
            VMEM((C, ATOMS), F32),
            pltpu.SemaphoreType.DMA((1 + 4 * HALF // BLOCK,)),
        ],
        4 * 10**9,
        far=(0, 3),
        far_outs=(1,),
    )


def fetched(tab_hbm, tab_ref, sems, begun=False):
    copies = []
    for tile in range(TILES):
        skip = AHEAD if begun and tile == 0 else 0
        rows = pl.ds(tile * CHUNK + skip, CHUNK - skip)
        copy = pltpu.make_async_copy(tab_hbm.at[rows], tab_ref.at[rows], sems.at[tile])
        copy.start()
        copies.append(copy)
    return copies


def ahead(next_hbm, next_ref, sem):
    copy = pltpu.make_async_copy(next_hbm.at[pl.ds(0, AHEAD)], next_ref, sem)
    copy.start()
    return copy


def cot_kernel(first, cot_ref, tab_hbm, other_ref, *rest):
    if first:
        feat_hbm, pos_hbm, sums_ref, out_ref, next_ref, rim_ref = rest[:6]
        rhs_ref, tab_ref, sems, pos_ref = rest[6:]
        out_ref[:, 0 : 2 * C] = sums_ref[...]
        out_ref = out_ref.at[:, 2 * C :]
        copies = fetched(tab_hbm, tab_ref, sems)
        pad = REACH * BLOCK
        tail = lax.axis_index("mode") < MODE_DEV // 2
        block = jnp.where(tail, MODE_DEV - REACH, 0)
        lanes = pl.ds(pl.multiple_of(block * BLOCK, BLOCK), pad)
        later = [
            pltpu.make_async_copy(pos_hbm, pos_ref, sems.at[TILES + 1]),
            pltpu.make_async_copy(
                feat_hbm.at[:, lanes], rim_ref.at[pl.ds(0, C)], sems.at[TILES + 2]
            ),
        ]
        for copy in later:
            copy.start()
        later.append(ahead(other_ref, next_ref, sems.at[TILES]))
        for k in range(REACH):
            rim_ref[C + 8 :, k * BLOCK : (k + 1) * BLOCK] = cot_ref[block + k]
        rim_ref[C : C + 8, :] = jnp.zeros((8, pad), F32)
    else:
        out_ref, rhs_ref, tab_ref, sems = rest
        copies = fetched(tab_hbm, tab_ref, sems, begun=True)
    cot_rows(cot_ref, rhs_ref, 0, C)
    for tile in range(TILES):
        copies[tile].wait()
        high_ref = other_ref if tile == 0 and not first else tab_ref
        sums_tile(tab_ref, rhs_ref, out_ref, tile, C, high_ref)
    if first:
        for copy in later:
            copy.wait()
        rim_ref[C : C + 3, :] = pos_ref[:, lanes]


def cot_call(first, cot, tab, other, *more):
    def body(*refs):
        cot_kernel(first, *refs)

    outs = [((HALF, 4 * C if first else 2 * C), F32)]
    scratch = [
        VMEM((2 * C, ATOMS), BF16),
        VMEM((4 * HALF, ATOMS), BF16),
        pltpu.SemaphoreType.DMA((TILES + 3,)),
    ]
    if first:
        outs += [((AHEAD, ATOMS), BF16), ((HALO_ROWS, REACH * BLOCK), F32)]
        scratch.append(VMEM((3, ATOMS), F32))
    return call(
        body,
        (cot, tab, other, *more),
        outs,
        scratch,
        2 * 10**9,
        far=(1, 2, 3, 4) if first else (1,),
    )


def merge_kernel(feat_ref, cot_ref, got_ref, out_hbm, out_ref, sems):
    copies = []
    for k in range(8):
        rows = slice(k * SHARE, (k + 1) * SHARE)
        for trig in range(2):
            for part in range(2):
                lanes = slice((2 * trig + part) * C, (2 * trig + part + 1) * C)
                here = slice(trig * C, (trig + 1) * C)
                there = slice((2 * part + trig) * C, (2 * part + trig + 1) * C)
                own = (feat_ref, cot_ref)[part]
                out_ref[k, :, lanes] = own[rows, here] + got_ref[rows, there]
        copies.append(pltpu.make_async_copy(out_ref.at[k], out_hbm.at[k], sems.at[k]))
        copies[-1].start()
    for copy in copies:
        copy.wait()


def give_back_kernel(own, sums_ref, filt_hbm, tab_hbm, other_ref, *rest):
    if own:
        acc_ref, next_ref, filt_ref, lhs_ref, tab_ref, sems = rest
    else:
        acc_ref, out_hbm, lhs_ref, tab_ref, sems, out_ref = rest
        filt_ref = filt_hbm
    core = lax.axis_index("atom") % 2
    at = pl.multiple_of(HALF * (core if own else 1 - core), HALF)
    if own:
        fetch = pltpu.make_async_copy(filt_hbm, filt_ref, sems.at[TILES])
        fetch.start()
        copies = fetched(tab_hbm, tab_ref, sems)
        later = ahead(other_ref, next_ref, sems.at[TILES + 1])
    else:
        copies = fetched(tab_hbm, tab_ref, sems, begun=True)
    if own:
        fetch.wait()
    scale = 1.0 / (ATOM_DEV * ATOMS)
    for k in range(HALF // C):
        filt = filt_ref[:, pl.ds(pl.multiple_of(at + k * C, C), C)] * scale
        tile, part = divmod(k * C, TILE)
        for trig in range(2):
            lanes = pl.ds((tile * 2 + trig) * TILE + part, C)
            for row in range(2):
                sums = sums_ref[k * C : (k + 1) * C, pl.ds((2 * trig + row) * C, C)]
                high, low = pieces(filt * sums.T)
                lhs_ref[row * C : (row + 1) * C, lanes] = high
                lhs_ref[(2 + row) * C : (3 + row) * C, lanes] = low
    width = 2 * BLOCK
    stores = []
    for n in range(TILES):
        copies[n].wait()
        high_ref = other_ref if n == 0 and not own else tab_ref
        depth = slice(n * 2 * TILE, (n + 1) * 2 * TILE)
        for k in range(ATOMS // width):
            lanes = slice(k * width, (k + 1) * width)
            top = n * CHUNK
            both = dot(lhs_ref[:, depth], high_ref[top : top + 2 * TILE, lanes], NN)
            more = dot(
                lhs_ref[0 : 2 * C, depth],
                tab_ref[top + 2 * TILE : top + CHUNK, lanes],
                NN,
            )
            part = both[: 2 * C] + both[2 * C :] + more
            if not own and n == 0:
                part = part + acc_ref[:, lanes]
            if own and n == 0:
                acc_ref[:, lanes] = part
            elif own:
                acc_ref[:, lanes] = acc_ref[:, lanes] + part
            else:
                for side in range(2):
                    half = part[:, side * BLOCK : (side + 1) * BLOCK]
                    if n:
                        half = half + out_ref[2 * k + side]
                    out_ref[2 * k + side] = half
                if n == TILES - 1:
                    pair = pl.ds(2 * k, 2)
                    stores.append(
                        pltpu.make_async_copy(
                            out_ref.at[pair], out_hbm.at[pair], sems.at[TILES + 2 + k]
                        )
                    )
                    stores[-1].start()
    for store in stores:
        store.wait()
    if own:
        later.wait()


def give_back_call(own, sums, filt, tab, other, acc=None):
    def body(*refs):
        give_back_kernel(own, *refs)

    args = [sums, filt, tab, other]
    if own:
        outs = [((2 * C, ATOMS), F32), ((AHEAD, ATOMS), BF16), ((C, MODES), F32)]
    else:
        args.append(acc)
        outs = [((MODE_DEV, 2 * C, BLOCK), F32)]
    return call(
        body,
        args,
        outs,
        [
            VMEM((4 * C, 2 * HALF), BF16),
            VMEM((4 * HALF, ATOMS), BF16),
            pltpu.SemaphoreType.DMA((TILES + 2 + ATOMS // (2 * BLOCK),)),
        ]
        + ([] if own else [VMEM(outs[0][0], F32)]),
        4 * 10**9,
        far=(1, 2, 3) if own else (2,),
        far_outs=() if own else (0,),
    )


def grad_kernel(own_ref, oth_ref, grad_ref):
    core = lax.axis_index("atom") % 2
    scale = 1.0 / (ATOM_DEV * ATOMS)
    for half in range(2):
        ref = (own_ref, oth_ref)[half]
        at = pl.multiple_of(HALF * (core if half == 0 else 1 - core), HALF)
        for k in range(HALF // C):
            rows = slice(k * C, (k + 1) * C)
            grad = (
                ref[rows, 0:C] * ref[rows, C : 2 * C]
                + ref[rows, 2 * C : 3 * C] * ref[rows, 3 * C :]
            )
            grad_ref[:, pl.ds(pl.multiple_of(at + k * C, C), C)] = grad.T * scale


def near_kernel(
    rim_ref,
    feat_ref,
    pos_ref,
    cot_ref,
    mix_hbm,
    rate_ref,
    out_ref,
    back_ref,
    ext_ref,
    rhs_ref,
    mix_ref,
    pos_vmem,
    sems,
):
    own = lax.axis_index("mode")
    pad = REACH * BLOCK
    middle = pl.ds(pad, ATOMS)
    rim_at = jnp.where(own < MODE_DEV // 2, 0, pad + ATOMS)
    moves = [
        (pos_ref, pos_vmem),
        (rim_ref, ext_ref.at[:, pl.ds(pl.multiple_of(rim_at, BLOCK), pad)]),
        (feat_ref, ext_ref.at[pl.ds(0, C), middle]),
        (mix_hbm, mix_ref),
    ]
    for k in range(MODE_DEV):
        lanes = pl.ds(pad + k * BLOCK, BLOCK)
        moves.append((cot_ref.at[k], ext_ref.at[pl.ds(C + 8, C + 8), lanes]))
    copies = [
        pltpu.make_async_copy(src, dst, sems.at[k]) for k, (src, dst) in enumerate(moves)
    ]
    for copy in copies:
        copy.start()
    for copy in copies:
        copy.wait()
    ext_ref[C : C + 3, pad : pad + ATOMS] = pos_vmem[...]
    shard = lax.axis_index("atom")
    total_blocks = ATOM_DEV * MODE_DEV

    def unit(block, row):
        return row * float(total_blocks) - block.astype(F32)

    def halves(row):
        q = row - 0.5
        y = q * q
        s = q * (
            3.14159265
            + y
            * (-5.16771276 + y * (2.55016332 + y * (-0.5992522 + y * (0.0820504 - 0.00702839 * y))))
        )
        c = 1.0 + y * (
            -4.93480214
            + y * (4.05870916 + y * (-1.335212 + y * (0.23493731 - 0.02439632 * y)))
        )
        return -s, c

    me = shard * MODE_DEV + own
    here = ext_ref[C : C + 8, pl.ds(pl.multiple_of(pad + own * BLOCK, BLOCK), BLOCK)]
    u_own = unit(me, here[0:1])
    c1, s1 = halves(here[1:2])
    c2, s2 = halves(here[2:3])
    columns = columns_of((u_own, c1, s1, c2, s2))
    wide = [jnp.broadcast_to(columns[:, k : k + 1], (BLOCK, BLOCK)) for k in range(5)]
    span = 2 * REACH + 1
    dist = []
    live = ext_ref[264:265, pl.ds(pl.multiple_of(pad + own * BLOCK, BLOCK), BLOCK)]
    for o in range(span):
        at = pl.ds(pl.multiple_of((own + o) * BLOCK, BLOCK), BLOCK)
        block = ext_ref[:, at]
        there = lax.rem(me + o - REACH + total_blocks, total_blocks)
        near = block[C : C + 8]
        x = wide[0] - (unit(there, near[0:1]) + float(o - REACH))
        d1c, d1s = halves(near[1:2])
        d2c, d2s = halves(near[2:3])
        y = x * x
        z = y * (3.14159265 / total_blocks) ** 2
        d = y * (1.0 + z * (-1.0 / 3.0 + z * (2.0 / 45.0)))
        e1 = wide[2] * d1c - wide[1] * d1s
        e2 = wide[4] * d2c - wide[3] * d2s
        d = d + (e1 * e1 + e2 * e2) * (2.0 / 3.14159265) ** 2
        dist.append(d)
        lanes = slice(o * BLOCK, (o + 1) * BLOCK)
        high, low = pieces(block[0:C] * live[0:1, o : o + 1])
        rhs_ref[0:C, lanes] = high
        rhs_ref[2 * C : 3 * C, lanes] = low
        lists_me = block[264:265, span - 1 - o : span - o]
        high, low = pieces(block[136 : 136 + C] * lists_me)
        rhs_ref[C : 2 * C, lanes] = high
        rhs_ref[3 * C :, lanes] = low
    out = ext_ref[0:C, pl.ds(pl.multiple_of(pad + own * BLOCK, BLOCK), BLOCK)]
    back = ext_ref[136 : 136 + C, pl.ds(pl.multiple_of(pad + own * BLOCK, BLOCK), BLOCK)]
    for r in range(RADIAL):
        rate = rate_ref[r]
        highs, lows = [], []
        for o in range(span):
            high, low = pieces(jnp.exp(dist[o] * -rate))
            highs.append(high)
            lows.append(low)
        weights_high = jnp.concatenate(highs, axis=1)
        weights_low = jnp.concatenate(lows, axis=1)
        both = dot(rhs_ref[...], weights_high, NT)
        got = (
            both[: 2 * C]
            + both[2 * C :]
            + dot(rhs_ref[0 : 2 * C, :], weights_low, NT)
        )
        high, low = pieces(got)
        mix = mix_ref[r]
        mh, ml = pieces(mix)
        th, tl = pieces(mix.T)
        out = out + (
            dot(th, high[:C], NN) + dot(th, low[:C], NN) + dot(tl, high[:C], NN)
        )
        back = back + (
            dot(mh, high[C:], NN) + dot(mh, low[C:], NN) + dot(ml, high[C:], NN)
        )
    out_ref[...] = out
    back_ref[...] = back


def near_call(rim, feat, pos, cot, mix, rates):
    return call(
        near_kernel,
        (rim, feat, pos, cot, mix, rates),
        (((C, BLOCK), F32), ((C, BLOCK), F32)),
        [
            VMEM((HALO_ROWS, ATOMS + 2 * REACH * BLOCK), F32),
            VMEM((4 * C, (2 * REACH + 1) * BLOCK), BF16),
            VMEM((RADIAL, C, C), F32),
            VMEM((3, ATOMS), F32),
            pltpu.SemaphoreType.DMA((4 + MODE_DEV,)),
        ],
        2 * 10**9,
        smem=(5,),
        any_in=(0, 1, 2, 3, 4),
    )


def pack_kernel(ids_hbm, live_ref, cot_hbm, pos_hbm, wave_hbm, *rest):
    out_hbm, pos_ref, wave_ref, ids_ref, pack_ref, sems = rest
    fetches = [
        pltpu.make_async_copy(cot_hbm, pack_ref.at[pl.ds(0, C)], sems.at[MODE_DEV]),
        pltpu.make_async_copy(ids_hbm, ids_ref, sems.at[MODE_DEV + 1]),
        pltpu.make_async_copy(pos_hbm, pos_ref, sems.at[MODE_DEV + 2]),
        pltpu.make_async_copy(wave_hbm, wave_ref, sems.at[MODE_DEV + 3]),
    ]
    for fetch in fetches:
        fetch.start()
    total_blocks = ATOM_DEV * MODE_DEV
    me = lax.axis_index("atom") * MODE_DEV + lax.axis_index("mode")
    lane = lax.broadcasted_iota(jnp.int32, (8, BLOCK), 1)
    live = jnp.zeros((8, BLOCK), F32)
    fetches[1].wait()
    for slot in range(SLOTS):
        offset = lax.rem(ids_ref[0, slot] - me + REACH + total_blocks, total_blocks)
        offset = jnp.where(slot < live_ref[0], offset, BLOCK)
        live = jnp.where(lane == offset, 1.0, live)
    pack_ref[C:, :] = live
    fetches[0].wait()
    copies = [
        pltpu.make_async_copy(pack_ref, out_hbm.at[k], sems.at[k]) for k in range(MODE_DEV)
    ]
    for copy in copies:
        copy.start()
    for copy in copies + fetches[2:]:
        copy.wait()


def share_kernel(parts_ref, out_ref):
    share = parts_ref[0]
    for k in range(1, ATOM_DEV // 2):
        share = share + parts_ref[k]
    for k in range(ATOM_DEV // 2):
        out_ref[k] = share


def finish_kernel(near_ref, back_ref, parts_ref, out_ref, grad_ref):
    out = near_ref[...]
    grad = back_ref[...]
    for k in range(MODE_DEV):
        out = out + parts_ref[k, 0:C]
        grad = grad + parts_ref[k, C:]
    out_ref[...] = out
    grad_ref[...] = grad


def per_device(
    features,
    positions,
    wavevectors,
    mode_filter,
    radial_mix,
    radial_rates,
    neighbour_ids,
    live_counts,
    cotangent,
):
    core_swap = [(i, i ^ 1) for i in range(ATOM_DEV)]
    chips = [[c + 2 * i for i in range(ATOM_DEV // 2)] for c in range(2)]
    rims = []
    for i in range(ATOM_DEV):
        for m in range(REACH):
            after = (i + 1) % ATOM_DEV
            rims.append((i * MODE_DEV + m, after * MODE_DEV + m))
            last = MODE_DEV - 1 - m
            rims.append((after * MODE_DEV + last, i * MODE_DEV + last))

    def exchange(x):
        return lax.all_to_all(x, "atom", 0, 0, axis_index_groups=chips, tiled=True)

    packed, pos_near, wave_near = call(
        pack_kernel,
        (neighbour_ids, live_counts, cotangent, positions, wavevectors),
        (
            ((MODE_DEV, C + 8, BLOCK), F32),
            (positions.shape, F32),
            (wavevectors.shape, jnp.int32),
        ),
        [
            pltpu.SMEM((1, SLOTS), jnp.int32),
            VMEM((C + 8, BLOCK), F32),
            pltpu.SemaphoreType.DMA((MODE_DEV + 4,)),
        ],
        smem=(1,),
        far=(0, 2, 3, 4),
        far_outs=(0,),
    )
    cot = lax.all_to_all(packed, "mode", 0, 0, tiled=True)

    f_own, tab_own = tables_call(True, features, pos_near, wave_near, packed)
    f_oth, tab_oth = tables_call(False, features, pos_near, wave_near, tab_own)
    cot, f_oth = lax.optimization_barrier((cot, f_oth))
    oth, tab_next, rim = cot_call(
        True, cot, tab_oth, tab_own, features, positions, f_oth
    )
    rim = lax.ppermute(rim, ("atom", "mode"), rims)
    got = lax.ppermute(oth, "atom", core_swap)
    cot, oth = lax.optimization_barrier((cot, oth))
    (c_own,) = cot_call(False, cot, tab_own, tab_next)
    (parts,) = call(
        merge_kernel,
        (f_own, c_own, got),
        (((8, SHARE, 4 * C), F32),),
        [VMEM((8, SHARE, 4 * C), F32), pltpu.SemaphoreType.DMA((8,))],
        far_outs=(0,),
    )
    parts = exchange(parts)
    (share,) = call(share_kernel, (parts,), ((parts.shape, F32),))
    own = exchange(share).reshape(HALF, 4 * C)
    oth = lax.ppermute(own, "atom", core_swap)
    acc, tab_next, filt = give_back_call(True, own, mode_filter, tab_own, tab_oth)
    (back,) = give_back_call(False, oth, filt, tab_oth, tab_next, acc)
    back, cot, rim = lax.optimization_barrier((back, cot, rim))
    near_out, near_back = near_call(
        rim, features, positions, cot, radial_mix, radial_rates
    )
    back = lax.all_to_all(back, "mode", 0, 0, tiled=True)
    (grad_filter,) = call(
        grad_kernel, (own, oth), (((C, MODES), F32),), plain=(0,), args_in=(0, 1)
    )
    layer_out, grad_features = call(
        finish_kernel,
        (near_out, near_back, back),
        (((C, BLOCK), F32), ((C, BLOCK), F32)),
        plain=(0, 1),
        args_in=(0, 1),
    )
    return (layer_out, grad_features, grad_filter)


def solution(mesh):
    in_specs = (
        P(None, "atom"),
        P(None, "atom"),
        P(None, "mode"),
        P(None, "mode"),
        P(),
        P(),
        P(("atom", "mode"), None),
        P(("atom", "mode")),
        P(None, ("atom", "mode")),
    )
    out_specs = (P(None, ("atom", "mode")), P(None, ("atom", "mode")), P(None, "mode"))
    return jax.shard_map(
        per_device, mesh=mesh, in_specs=in_specs, out_specs=out_specs, check_vma=False
    )
```

```python
import jax
import jax.numpy as jnp
from jax import lax
from jax.experimental import pallas as pl
from jax.experimental.pallas import tpu as pltpu
from jax.sharding import PartitionSpec as P


BLOCK = 128
REACH = 2
SLOTS = 5
C = 128
ATOMS = 1024
MODES = 1024
HALF = 512
SHARE = 64
RADIAL = 4
ATOM_DEV = 16
MODE_DEV = 8
HALO_ROWS = 272

F32 = jnp.float32
BF16 = jnp.bfloat16
MAGIC = 12582912.0
LIMIT = 24 * 1024 * 1024
VMEM = pltpu.VMEM

NT = (((1,), (1,)), ((), ()))
NN = (((1,), (0,)), ((), ()))


def dot(a, b, dims):
    return lax.dot_general(a, b, dims, preferred_element_type=F32)


def pieces(x):
    high = x.astype(BF16)
    low = (x - high.astype(F32)).astype(BF16)
    return high, low


def cos_sin_turns(t):
    r = t - ((t + MAGIC) - MAGIC)
    y = r * r
    s = r * (4.44287957 + y * (-7.30781668 + y * (3.59777418 + y * -0.79119939)))
    c = 1.4142135 + y * (
        -6.97885095 + y * (5.73946038 + y * (-1.88355791 + y * 0.31068803))
    )
    return 1.0 - s * s, s * c


ROWS = 32
TILE = 256
CHUNK = 4 * TILE
TILES = HALF // TILE


def columns_of(rows):
    rows = list(rows)
    rows = rows + [rows[0]] * (8 - len(rows))
    eight = jnp.concatenate(rows, axis=0)
    return jnp.concatenate([eight] * (BLOCK // 8), axis=0).T


def tables_tile(pos_ref, wave_ref, tab_ref, first, tile, leave):
    shard = lax.axis_index("atom")
    mid = (2 * shard + 1).astype(F32) * (1.0 / 32.0)
    for group in range(TILE // BLOCK):
        at = tile * TILE + group * BLOCK
        w = wave_ref[:, pl.ds(pl.multiple_of(first + at, BLOCK), BLOCK)]
        start = ((w[0:1] * (2 * shard + 1)) & 31).astype(F32) * (1.0 / 32.0)
        wf = w.astype(F32)
        columns = columns_of((wf[0:1], wf[1:2], wf[2:3], start))
        for chunk in range(BLOCK // ROWS):
            part = columns[chunk * ROWS : (chunk + 1) * ROWS]
            w0, w1, w2, c0 = (
                jnp.broadcast_to(part[:, d : d + 1], (ROWS, BLOCK)) for d in range(4)
            )
            row = tile * CHUNK + group * BLOCK + chunk * ROWS
            for k in range(ATOMS // BLOCK):
                lanes = pl.ds(k * BLOCK, BLOCK)
                p0 = pos_ref[0:1, lanes] - mid
                p1 = pos_ref[1:2, lanes]
                p2 = pos_ref[2:3, lanes]
                t = w0 * p0 + (w1 * p1 + (w2 * p2 + c0))
                cos, sin = cos_sin_turns(t)
                ch, cl = pieces(cos)
                sh, sl = pieces(sin)
                tab_ref[row : row + ROWS, lanes] = ch
                tab_ref[TILE + row : TILE + row + ROWS, lanes] = sh
                tab_ref[2 * TILE + row : 2 * TILE + row + ROWS, lanes] = cl
                tab_ref[3 * TILE + row : 3 * TILE + row + ROWS, lanes] = sl
        leave(tile * CHUNK + group * BLOCK)


def sums_tile(tab_ref, rhs_ref, out_ref, tile, wide, copies=()):
    at = tile * CHUNK
    for copy in copies:
        copy.wait()
    both = dot(tab_ref[at : at + 2 * TILE, :], rhs_ref[...], NT)
    rest = dot(tab_ref[at + 2 * TILE : at + CHUNK, :], rhs_ref[0:wide, :], NT)
    total = both[:, :wide] + both[:, wide:] + rest
    for trig in range(2):
        out_ref[tile * TILE : (tile + 1) * TILE, trig * wide : (trig + 1) * wide] = (
            total[trig * TILE : (trig + 1) * TILE]
        )


def cot_rows(cot_ref, rhs_ref, high_at, low_at):
    for k in range(MODE_DEV):
        high, low = pieces(cot_ref[k, 0:C, :])
        rhs_ref[high_at : high_at + C, k * BLOCK : (k + 1) * BLOCK] = high
        rhs_ref[low_at : low_at + C, k * BLOCK : (k + 1) * BLOCK] = low


def tables_kernel(own, feat_hbm, pos_ref, wave_ref, dep_ref, *rest):
    out_ref, tab_hbm, rhs_ref, tab_ref, feat_ref, sems = rest
    fetch = pltpu.make_async_copy(feat_hbm, feat_ref, sems.at[0])
    fetch.start()
    core = lax.axis_index("atom") % 2
    first = HALF * (core if own else 1 - core)
    copies = []

    def leave(row):
        for kind in range(4):
            rows = pl.ds(row + kind * TILE, BLOCK)
            sem = sems.at[1 + len(copies)]
            copies.append(
                pltpu.make_async_copy(tab_ref.at[rows], tab_hbm.at[rows], sem)
            )
            copies[-1].start()

    for tile in range(TILES):
        tables_tile(pos_ref, wave_ref, tab_ref, first, tile, leave)
        if tile == 0:
            fetch.wait()
            high, low = pieces(feat_ref[...])
            rhs_ref[0:C, :] = high
            rhs_ref[C:, :] = low
        sums_tile(tab_ref, rhs_ref, out_ref, tile, C)
    for copy in copies:
        copy.wait()


def spec():
    return pl.BlockSpec(memory_space=VMEM)


def call(body, ins, outs, scratch=(), flops=10**8, smem=(), far=(), far_outs=(), plain=(), args_in=(), any_in=()):
    args, in_specs = [], []
    for k, x in enumerate(ins):
        if k in smem:
            in_specs.append(pl.BlockSpec(memory_space=pltpu.SMEM))
        elif k in any_in:
            in_specs.append(pl.BlockSpec(memory_space=pl.ANY))
        elif k in far:
            in_specs.append(pl.BlockSpec(memory_space=pltpu.HBM))
            x = pltpu.with_memory_space_constraint(x, pltpu.HBM)
        else:
            in_specs.append(spec())
            if k not in args_in:
                x = pltpu.with_memory_space_constraint(x, VMEM)
        args.append(x)
    size = sum(x.size * x.dtype.itemsize for x in ins)
    return pl.pallas_call(
        body,
        out_shape=tuple(
            pltpu.HBM(shape, kind)
            if k in far_outs
            else (jax.ShapeDtypeStruct if k in plain else VMEM)(shape, kind)
            for k, (shape, kind) in enumerate(outs)
        ),
        in_specs=in_specs,
        out_specs=tuple(
            pl.BlockSpec(memory_space=pltpu.HBM) if k in far_outs else spec()
            for k in range(len(outs))
        ),
        scratch_shapes=list(scratch),
        compiler_params=pltpu.CompilerParams(vmem_limit_bytes=LIMIT),
        cost_estimate=pl.CostEstimate(
            flops=flops, bytes_accessed=size, transcendentals=0
        ),
    )(*args)


def tables_call(own, feat, pos, wave, dep):
    def body(*refs):
        tables_kernel(own, *refs)

    return call(
        body,
        (feat, pos, wave, dep),
        (((HALF, 2 * C), F32), ((4 * HALF, ATOMS), BF16)),
        [
            VMEM((2 * C, ATOMS), BF16),
            VMEM((4 * HALF, ATOMS), BF16),
            VMEM((C, ATOMS), F32),
            pltpu.SemaphoreType.DMA((1 + 4 * HALF // BLOCK,)),
        ],
        4 * 10**9,
        far=(0, 3),
        far_outs=(1,),
    )


def fetched(tab_hbm, tab_ref, sems, tiles):
    copies = []
    for tile in tiles:
        rows = pl.ds(tile * CHUNK, CHUNK)
        copy = pltpu.make_async_copy(tab_hbm.at[rows], tab_ref.at[rows], sems.at[tile])
        copy.start()
        copies.append(copy)
    return copies


def ahead(next_hbm, next_ref, sem):
    copy = pltpu.make_async_copy(next_hbm.at[pl.ds(0, CHUNK)], next_ref, sem)
    copy.start()
    return copy


def cot_kernel(first, cot_ref, tab_hbm, other_ref, *rest):
    if first:
        feat_hbm, pos_hbm, sums_ref, out_ref, next_ref, rim_ref = rest[:6]
        rhs_ref, tab_ref, sems, pos_ref = rest[6:]
        out_ref[:, 0 : 2 * C] = sums_ref[...]
        out_ref = out_ref.at[:, 2 * C :]
        copies = fetched(tab_hbm, tab_ref, sems, range(TILES))
        pad = REACH * BLOCK
        tail = lax.axis_index("mode") < MODE_DEV // 2
        block = jnp.where(tail, MODE_DEV - REACH, 0)
        lanes = pl.ds(pl.multiple_of(block * BLOCK, BLOCK), pad)
        later = [
            pltpu.make_async_copy(pos_hbm, pos_ref, sems.at[TILES + 1]),
            pltpu.make_async_copy(
                feat_hbm.at[:, lanes], rim_ref.at[pl.ds(0, C)], sems.at[TILES + 2]
            ),
        ]
        for copy in later:
            copy.start()
        later.append(ahead(other_ref, next_ref, sems.at[TILES]))
        for k in range(REACH):
            rim_ref[C + 8 :, k * BLOCK : (k + 1) * BLOCK] = cot_ref[block + k]
        rim_ref[C : C + 8, :] = jnp.zeros((8, pad), F32)
    else:
        out_ref, rhs_ref, tab_ref, sems = rest
        copies = [None] + fetched(tab_hbm, tab_ref, sems, range(1, TILES))
    cot_rows(cot_ref, rhs_ref, 0, C)
    for tile in range(TILES):
        if copies[tile] is None:
            sums_tile(other_ref, rhs_ref, out_ref, tile, C)
        else:
            copies[tile].wait()
            sums_tile(tab_ref, rhs_ref, out_ref, tile, C)
    if first:
        for copy in later:
            copy.wait()
        rim_ref[C : C + 3, :] = pos_ref[:, lanes]


def cot_call(first, cot, tab, other, *more):
    def body(*refs):
        cot_kernel(first, *refs)

    outs = [((HALF, 4 * C if first else 2 * C), F32)]
    scratch = [
        VMEM((2 * C, ATOMS), BF16),
        VMEM((4 * HALF, ATOMS), BF16),
        pltpu.SemaphoreType.DMA((TILES + 3,)),
    ]
    if first:
        outs += [((CHUNK, ATOMS), BF16), ((HALO_ROWS, REACH * BLOCK), F32)]
        scratch.append(VMEM((3, ATOMS), F32))
    return call(
        body,
        (cot, tab, other, *more),
        outs,
        scratch,
        2 * 10**9,
        far=(1, 2, 3, 4) if first else (1,),
    )


def merge_kernel(feat_ref, cot_ref, got_ref, out_hbm, out_ref, sems):
    copies = []
    for k in range(8):
        rows = slice(k * SHARE, (k + 1) * SHARE)
        for trig in range(2):
            for part in range(2):
                lanes = slice((2 * trig + part) * C, (2 * trig + part + 1) * C)
                here = slice(trig * C, (trig + 1) * C)
                there = slice((2 * part + trig) * C, (2 * part + trig + 1) * C)
                own = (feat_ref, cot_ref)[part]
                out_ref[k, :, lanes] = own[rows, here] + got_ref[rows, there]
        copies.append(pltpu.make_async_copy(out_ref.at[k], out_hbm.at[k], sems.at[k]))
        copies[-1].start()
    for copy in copies:
        copy.wait()


def give_back_kernel(own, sums_ref, filt_hbm, tab_hbm, other_ref, *rest):
    if own:
        acc_ref, next_ref, filt_ref, lhs_ref, tab_ref, sems = rest
    else:
        acc_ref, out_hbm, lhs_ref, tab_ref, sems, out_ref = rest
        filt_ref = filt_hbm
    core = lax.axis_index("atom") % 2
    at = pl.multiple_of(HALF * (core if own else 1 - core), HALF)
    if own:
        fetch = pltpu.make_async_copy(filt_hbm, filt_ref, sems.at[TILES])
        fetch.start()
        copies = fetched(tab_hbm, tab_ref, sems, range(TILES))
        later = ahead(other_ref, next_ref, sems.at[TILES + 1])
    else:
        copies = [None] + fetched(tab_hbm, tab_ref, sems, range(1, TILES))
    if own:
        fetch.wait()
    scale = 1.0 / (ATOM_DEV * ATOMS)
    for k in range(HALF // C):
        filt = filt_ref[:, pl.ds(pl.multiple_of(at + k * C, C), C)] * scale
        tile, part = divmod(k * C, TILE)
        for trig in range(2):
            lanes = pl.ds((tile * 2 + trig) * TILE + part, C)
            for row in range(2):
                sums = sums_ref[k * C : (k + 1) * C, pl.ds((2 * trig + row) * C, C)]
                high, low = pieces(filt * sums.T)
                lhs_ref[row * C : (row + 1) * C, lanes] = high
                lhs_ref[(2 + row) * C : (3 + row) * C, lanes] = low
    width = 2 * BLOCK
    stores = []
    for n in range(TILES):
        if copies[n] is not None:
            copies[n].wait()
        table = other_ref if copies[n] is None else tab_ref
        depth = slice(n * 2 * TILE, (n + 1) * 2 * TILE)
        for k in range(ATOMS // width):
            lanes = slice(k * width, (k + 1) * width)
            top = n * CHUNK
            both = dot(lhs_ref[:, depth], table[top : top + 2 * TILE, lanes], NN)
            more = dot(
                lhs_ref[0 : 2 * C, depth],
                table[top + 2 * TILE : top + CHUNK, lanes],
                NN,
            )
            part = both[: 2 * C] + both[2 * C :] + more
            if not own and n == 0:
                part = part + acc_ref[:, lanes]
            if own and n == 0:
                acc_ref[:, lanes] = part
            elif own:
                acc_ref[:, lanes] = acc_ref[:, lanes] + part
            else:
                for side in range(2):
                    half = part[:, side * BLOCK : (side + 1) * BLOCK]
                    if n:
                        half = half + out_ref[2 * k + side]
                    out_ref[2 * k + side] = half
                if n == TILES - 1:
                    pair = pl.ds(2 * k, 2)
                    stores.append(
                        pltpu.make_async_copy(
                            out_ref.at[pair], out_hbm.at[pair], sems.at[TILES + 2 + k]
                        )
                    )
                    stores[-1].start()
    for store in stores:
        store.wait()
    if own:
        later.wait()


def give_back_call(own, sums, filt, tab, other, acc=None):
    def body(*refs):
        give_back_kernel(own, *refs)

    args = [sums, filt, tab, other]
    if own:
        outs = [((2 * C, ATOMS), F32), ((CHUNK, ATOMS), BF16), ((C, MODES), F32)]
    else:
        args.append(acc)
        outs = [((MODE_DEV, 2 * C, BLOCK), F32)]
    return call(
        body,
        args,
        outs,
        [
            VMEM((4 * C, 2 * HALF), BF16),
            VMEM((4 * HALF, ATOMS), BF16),
            pltpu.SemaphoreType.DMA((TILES + 2 + ATOMS // (2 * BLOCK),)),
        ]
        + ([] if own else [VMEM(outs[0][0], F32)]),
        4 * 10**9,
        far=(1, 2, 3) if own else (2,),
        far_outs=() if own else (0,),
    )


def grad_kernel(own_ref, oth_ref, grad_ref):
    core = lax.axis_index("atom") % 2
    scale = 1.0 / (ATOM_DEV * ATOMS)
    for half in range(2):
        ref = (own_ref, oth_ref)[half]
        at = pl.multiple_of(HALF * (core if half == 0 else 1 - core), HALF)
        for k in range(HALF // C):
            rows = slice(k * C, (k + 1) * C)
            grad = (
                ref[rows, 0:C] * ref[rows, C : 2 * C]
                + ref[rows, 2 * C : 3 * C] * ref[rows, 3 * C :]
            )
            grad_ref[:, pl.ds(pl.multiple_of(at + k * C, C), C)] = grad.T * scale


def near_kernel(
    rim_ref,
    feat_ref,
    pos_ref,
    cot_ref,
    mix_hbm,
    rate_ref,
    out_ref,
    back_ref,
    ext_ref,
    rhs_ref,
    mix_ref,
    pos_vmem,
    sems,
):
    own = lax.axis_index("mode")
    pad = REACH * BLOCK
    middle = pl.ds(pad, ATOMS)
    rim_at = jnp.where(own < MODE_DEV // 2, 0, pad + ATOMS)
    moves = [
        (pos_ref, pos_vmem),
        (rim_ref, ext_ref.at[:, pl.ds(pl.multiple_of(rim_at, BLOCK), pad)]),
        (feat_ref, ext_ref.at[pl.ds(0, C), middle]),
        (mix_hbm, mix_ref),
    ]
    for k in range(MODE_DEV):
        lanes = pl.ds(pad + k * BLOCK, BLOCK)
        moves.append((cot_ref.at[k], ext_ref.at[pl.ds(C + 8, C + 8), lanes]))
    copies = [
        pltpu.make_async_copy(src, dst, sems.at[k]) for k, (src, dst) in enumerate(moves)
    ]
    for copy in copies:
        copy.start()
    for copy in copies:
        copy.wait()
    ext_ref[C : C + 3, pad : pad + ATOMS] = pos_vmem[...]
    shard = lax.axis_index("atom")
    total_blocks = ATOM_DEV * MODE_DEV

    def unit(block, row):
        return row * float(total_blocks) - block.astype(F32)

    def halves(row):
        q = row - 0.5
        y = q * q
        s = q * (
            3.14159265
            + y
            * (-5.16771276 + y * (2.55016332 + y * (-0.5992522 + y * (0.0820504 - 0.00702839 * y))))
        )
        c = 1.0 + y * (
            -4.93480214
            + y * (4.05870916 + y * (-1.335212 + y * (0.23493731 - 0.02439632 * y)))
        )
        return -s, c

    me = shard * MODE_DEV + own
    here = ext_ref[C : C + 8, pl.ds(pl.multiple_of(pad + own * BLOCK, BLOCK), BLOCK)]
    u_own = unit(me, here[0:1])
    c1, s1 = halves(here[1:2])
    c2, s2 = halves(here[2:3])
    columns = columns_of((u_own, c1, s1, c2, s2))
    wide = [jnp.broadcast_to(columns[:, k : k + 1], (BLOCK, BLOCK)) for k in range(5)]
    span = 2 * REACH + 1
    dist = []
    live = ext_ref[264:265, pl.ds(pl.multiple_of(pad + own * BLOCK, BLOCK), BLOCK)]
    for o in range(span):
        at = pl.ds(pl.multiple_of((own + o) * BLOCK, BLOCK), BLOCK)
        block = ext_ref[:, at]
        there = lax.rem(me + o - REACH + total_blocks, total_blocks)
        near = block[C : C + 8]
        x = wide[0] - (unit(there, near[0:1]) + float(o - REACH))
        d1c, d1s = halves(near[1:2])
        d2c, d2s = halves(near[2:3])
        y = x * x
        z = y * (3.14159265 / total_blocks) ** 2
        d = y * (1.0 + z * (-1.0 / 3.0 + z * (2.0 / 45.0)))
        e1 = wide[2] * d1c - wide[1] * d1s
        e2 = wide[4] * d2c - wide[3] * d2s
        d = d + (e1 * e1 + e2 * e2) * (2.0 / 3.14159265) ** 2
        dist.append(d)
        lanes = slice(o * BLOCK, (o + 1) * BLOCK)
        high, low = pieces(block[0:C] * live[0:1, o : o + 1])
        rhs_ref[0:C, lanes] = high
        rhs_ref[2 * C : 3 * C, lanes] = low
        lists_me = block[264:265, span - 1 - o : span - o]
        high, low = pieces(block[136 : 136 + C] * lists_me)
        rhs_ref[C : 2 * C, lanes] = high
        rhs_ref[3 * C :, lanes] = low
    out = ext_ref[0:C, pl.ds(pl.multiple_of(pad + own * BLOCK, BLOCK), BLOCK)]
    back = ext_ref[136 : 136 + C, pl.ds(pl.multiple_of(pad + own * BLOCK, BLOCK), BLOCK)]
    for r in range(RADIAL):
        rate = rate_ref[r]
        highs, lows = [], []
        for o in range(span):
            high, low = pieces(jnp.exp(dist[o] * -rate))
            highs.append(high)
            lows.append(low)
        weights_high = jnp.concatenate(highs, axis=1)
        weights_low = jnp.concatenate(lows, axis=1)
        both = dot(rhs_ref[...], weights_high, NT)
        got = (
            both[: 2 * C]
            + both[2 * C :]
            + dot(rhs_ref[0 : 2 * C, :], weights_low, NT)
        )
        high, low = pieces(got)
        mix = mix_ref[r]
        mh, ml = pieces(mix)
        th, tl = pieces(mix.T)
        out = out + (
            dot(th, high[:C], NN) + dot(th, low[:C], NN) + dot(tl, high[:C], NN)
        )
        back = back + (
            dot(mh, high[C:], NN) + dot(mh, low[C:], NN) + dot(ml, high[C:], NN)
        )
    out_ref[...] = out
    back_ref[...] = back


def near_call(rim, feat, pos, cot, mix, rates):
    return call(
        near_kernel,
        (rim, feat, pos, cot, mix, rates),
        (((C, BLOCK), F32), ((C, BLOCK), F32)),
        [
            VMEM((HALO_ROWS, ATOMS + 2 * REACH * BLOCK), F32),
            VMEM((4 * C, (2 * REACH + 1) * BLOCK), BF16),
            VMEM((RADIAL, C, C), F32),
            VMEM((3, ATOMS), F32),
            pltpu.SemaphoreType.DMA((4 + MODE_DEV,)),
        ],
        2 * 10**9,
        smem=(5,),
        any_in=(0, 1, 2, 3, 4),
    )


def pack_kernel(ids_hbm, live_ref, cot_hbm, pos_hbm, wave_hbm, *rest):
    out_hbm, pos_ref, wave_ref, ids_ref, pack_ref, sems = rest
    fetches = [
        pltpu.make_async_copy(cot_hbm, pack_ref.at[pl.ds(0, C)], sems.at[MODE_DEV]),
        pltpu.make_async_copy(ids_hbm, ids_ref, sems.at[MODE_DEV + 1]),
        pltpu.make_async_copy(pos_hbm, pos_ref, sems.at[MODE_DEV + 2]),
        pltpu.make_async_copy(wave_hbm, wave_ref, sems.at[MODE_DEV + 3]),
    ]
    for fetch in fetches:
        fetch.start()
    total_blocks = ATOM_DEV * MODE_DEV
    me = lax.axis_index("atom") * MODE_DEV + lax.axis_index("mode")
    lane = lax.broadcasted_iota(jnp.int32, (8, BLOCK), 1)
    live = jnp.zeros((8, BLOCK), F32)
    fetches[1].wait()
    for slot in range(SLOTS):
        offset = lax.rem(ids_ref[0, slot] - me + REACH + total_blocks, total_blocks)
        offset = jnp.where(slot < live_ref[0], offset, BLOCK)
        live = jnp.where(lane == offset, 1.0, live)
    pack_ref[C:, :] = live
    fetches[0].wait()
    copies = [
        pltpu.make_async_copy(pack_ref, out_hbm.at[k], sems.at[k]) for k in range(MODE_DEV)
    ]
    for copy in copies:
        copy.start()
    for copy in copies + fetches[2:]:
        copy.wait()


def share_kernel(parts_ref, out_ref):
    share = parts_ref[0]
    for k in range(1, ATOM_DEV // 2):
        share = share + parts_ref[k]
    for k in range(ATOM_DEV // 2):
        out_ref[k] = share


def finish_kernel(near_ref, back_ref, parts_ref, out_ref, grad_ref):
    out = near_ref[...]
    grad = back_ref[...]
    for k in range(MODE_DEV):
        out = out + parts_ref[k, 0:C]
        grad = grad + parts_ref[k, C:]
    out_ref[...] = out
    grad_ref[...] = grad


def per_device(
    features,
    positions,
    wavevectors,
    mode_filter,
    radial_mix,
    radial_rates,
    neighbour_ids,
    live_counts,
    cotangent,
):
    core_swap = [(i, i ^ 1) for i in range(ATOM_DEV)]
    chips = [[c + 2 * i for i in range(ATOM_DEV // 2)] for c in range(2)]
    rims = []
    for i in range(ATOM_DEV):
        for m in range(REACH):
            after = (i + 1) % ATOM_DEV
            rims.append((i * MODE_DEV + m, after * MODE_DEV + m))
            last = MODE_DEV - 1 - m
            rims.append((after * MODE_DEV + last, i * MODE_DEV + last))

    def exchange(x):
        return lax.all_to_all(x, "atom", 0, 0, axis_index_groups=chips, tiled=True)

    packed, pos_near, wave_near = call(
        pack_kernel,
        (neighbour_ids, live_counts, cotangent, positions, wavevectors),
        (
            ((MODE_DEV, C + 8, BLOCK), F32),
            (positions.shape, F32),
            (wavevectors.shape, jnp.int32),
        ),
        [
            pltpu.SMEM((1, SLOTS), jnp.int32),
            VMEM((C + 8, BLOCK), F32),
            pltpu.SemaphoreType.DMA((MODE_DEV + 4,)),
        ],
        smem=(1,),
        far=(0, 2, 3, 4),
        far_outs=(0,),
    )
    cot = lax.all_to_all(packed, "mode", 0, 0, tiled=True)

    f_own, tab_own = tables_call(True, features, pos_near, wave_near, packed)
    f_oth, tab_oth = tables_call(False, features, pos_near, wave_near, tab_own)
    cot, f_oth = lax.optimization_barrier((cot, f_oth))
    oth, tab_next, rim = cot_call(
        True, cot, tab_oth, tab_own, features, positions, f_oth
    )
    rim = lax.ppermute(rim, ("atom", "mode"), rims)
    got = lax.ppermute(oth, "atom", core_swap)
    cot, oth = lax.optimization_barrier((cot, oth))
    (c_own,) = cot_call(False, cot, tab_own, tab_next)
    (parts,) = call(
        merge_kernel,
        (f_own, c_own, got),
        (((8, SHARE, 4 * C), F32),),
        [VMEM((8, SHARE, 4 * C), F32), pltpu.SemaphoreType.DMA((8,))],
        far_outs=(0,),
    )
    parts = exchange(parts)
    (share,) = call(share_kernel, (parts,), ((parts.shape, F32),))
    own = exchange(share).reshape(HALF, 4 * C)
    oth = lax.ppermute(own, "atom", core_swap)
    acc, tab_next, filt = give_back_call(True, own, mode_filter, tab_own, tab_oth)
    (back,) = give_back_call(False, oth, filt, tab_oth, tab_next, acc)
    back, cot, rim = lax.optimization_barrier((back, cot, rim))
    near_out, near_back = near_call(
        rim, features, positions, cot, radial_mix, radial_rates
    )
    back = lax.all_to_all(back, "mode", 0, 0, tiled=True)
    (grad_filter,) = call(
        grad_kernel, (own, oth), (((C, MODES), F32),), plain=(0,), args_in=(0, 1)
    )
    layer_out, grad_features = call(
        finish_kernel,
        (near_out, near_back, back),
        (((C, BLOCK), F32), ((C, BLOCK), F32)),
        plain=(0, 1),
        args_in=(0, 1),
    )
    return (layer_out, grad_features, grad_filter)


def solution(mesh):
    in_specs = (
        P(None, "atom"),
        P(None, "atom"),
        P(None, "mode"),
        P(None, "mode"),
        P(),
        P(),
        P(("atom", "mode"), None),
        P(("atom", "mode")),
        P(None, ("atom", "mode")),
    )
    out_specs = (P(None, ("atom", "mode")), P(None, ("atom", "mode")), P(None, "mode"))
    return jax.shard_map(
        per_device, mesh=mesh, in_specs=in_specs, out_specs=out_specs, check_vma=False
    )
```

```python
import jax
import jax.numpy as jnp
from jax import lax
from jax.experimental import pallas as pl
from jax.experimental.pallas import tpu as pltpu
from jax.sharding import PartitionSpec as P


BLOCK = 128
REACH = 2
SLOTS = 5
C = 128
ATOMS = 1024
MODES = 1024
HALF = 512
SHARE = 64
RADIAL = 4
ATOM_DEV = 16
MODE_DEV = 8
HALO_ROWS = 272

F32 = jnp.float32
BF16 = jnp.bfloat16
MAGIC = 12582912.0
LIMIT = 24 * 1024 * 1024
VMEM = pltpu.VMEM

NT = (((1,), (1,)), ((), ()))
NN = (((1,), (0,)), ((), ()))


def dot(a, b, dims):
    return lax.dot_general(a, b, dims, preferred_element_type=F32)


def pieces(x):
    high = x.astype(BF16)
    low = (x - high.astype(F32)).astype(BF16)
    return high, low


def cos_sin_turns(t):
    r = t - ((t + MAGIC) - MAGIC)
    y = r * r
    s = r * (4.44287957 + y * (-7.30781668 + y * (3.59777418 + y * -0.79119939)))
    c = 1.4142135 + y * (
        -6.97885095 + y * (5.73946038 + y * (-1.88355791 + y * 0.31068803))
    )
    return 1.0 - s * s, s * c


ROWS = 32
TILE = 256
CHUNK = 4 * TILE
TILES = HALF // TILE


def columns_of(rows):
    rows = list(rows)
    rows = rows + [rows[0]] * (8 - len(rows))
    eight = jnp.concatenate(rows, axis=0)
    return jnp.concatenate([eight] * (BLOCK // 8), axis=0).T


def tables_tile(pos_ref, wave_ref, tab_ref, first, tile, leave):
    shard = lax.axis_index("atom")
    mid = (2 * shard + 1).astype(F32) * (1.0 / 32.0)
    for group in range(TILE // BLOCK):
        at = tile * TILE + group * BLOCK
        w = wave_ref[:, pl.ds(pl.multiple_of(first + at, BLOCK), BLOCK)]
        start = ((w[0:1] * (2 * shard + 1)) & 31).astype(F32) * (1.0 / 32.0)
        wf = w.astype(F32)
        columns = columns_of((wf[0:1], wf[1:2], wf[2:3], start))
        for chunk in range(BLOCK // ROWS):
            part = columns[chunk * ROWS : (chunk + 1) * ROWS]
            w0, w1, w2, c0 = (
                jnp.broadcast_to(part[:, d : d + 1], (ROWS, BLOCK)) for d in range(4)
            )
            row = tile * CHUNK + group * BLOCK + chunk * ROWS
            for k in range(ATOMS // BLOCK):
                lanes = pl.ds(k * BLOCK, BLOCK)
                p0 = pos_ref[0:1, lanes] - mid
                p1 = pos_ref[1:2, lanes]
                p2 = pos_ref[2:3, lanes]
                t = w0 * p0 + (w1 * p1 + (w2 * p2 + c0))
                cos, sin = cos_sin_turns(t)
                ch, cl = pieces(cos)
                sh, sl = pieces(sin)
                tab_ref[row : row + ROWS, lanes] = ch
                tab_ref[TILE + row : TILE + row + ROWS, lanes] = sh
                tab_ref[2 * TILE + row : 2 * TILE + row + ROWS, lanes] = cl
                tab_ref[3 * TILE + row : 3 * TILE + row + ROWS, lanes] = sl
        leave(tile * CHUNK + group * BLOCK)


def sums_tile(tab_ref, rhs_ref, out_ref, tile, wide, copies=()):
    at = tile * CHUNK
    for copy in copies:
        copy.wait()
    both = dot(tab_ref[at : at + 2 * TILE, :], rhs_ref[...], NT)
    rest = dot(tab_ref[at + 2 * TILE : at + CHUNK, :], rhs_ref[0:wide, :], NT)
    total = both[:, :wide] + both[:, wide:] + rest
    for trig in range(2):
        out_ref[tile * TILE : (tile + 1) * TILE, trig * wide : (trig + 1) * wide] = (
            total[trig * TILE : (trig + 1) * TILE]
        )


def cot_rows(cot_ref, rhs_ref, high_at, low_at):
    for k in range(MODE_DEV):
        high, low = pieces(cot_ref[k, 0:C, :])
        rhs_ref[high_at : high_at + C, k * BLOCK : (k + 1) * BLOCK] = high
        rhs_ref[low_at : low_at + C, k * BLOCK : (k + 1) * BLOCK] = low


def tables_kernel(own, feat_hbm, pos_ref, wave_ref, dep_ref, *rest):
    out_ref, tab_hbm, rhs_ref, tab_ref, feat_ref, sems = rest
    fetch = pltpu.make_async_copy(feat_hbm, feat_ref, sems.at[0])
    fetch.start()
    core = lax.axis_index("atom") % 2
    first = HALF * (core if own else 1 - core)
    copies = []

    def leave(row):
        for kind in range(4):
            rows = pl.ds(row + kind * TILE, BLOCK)
            sem = sems.at[1 + len(copies)]
            copies.append(
                pltpu.make_async_copy(tab_ref.at[rows], tab_hbm.at[rows], sem)
            )
            copies[-1].start()

    for tile in range(TILES):
        tables_tile(pos_ref, wave_ref, tab_ref, first, tile, leave)
        if tile == 0:
            fetch.wait()
            high, low = pieces(feat_ref[...])
            rhs_ref[0:C, :] = high
            rhs_ref[C:, :] = low
        sums_tile(tab_ref, rhs_ref, out_ref, tile, C)
    for copy in copies:
        copy.wait()


def spec():
    return pl.BlockSpec(memory_space=VMEM)


def call(body, ins, outs, scratch=(), flops=10**8, smem=(), far=(), far_outs=(), plain=(), args_in=(), any_in=()):
    args, in_specs = [], []
    for k, x in enumerate(ins):
        if k in smem:
            in_specs.append(pl.BlockSpec(memory_space=pltpu.SMEM))
        elif k in any_in:
            in_specs.append(pl.BlockSpec(memory_space=pl.ANY))
        elif k in far:
            in_specs.append(pl.BlockSpec(memory_space=pltpu.HBM))
            x = pltpu.with_memory_space_constraint(x, pltpu.HBM)
        else:
            in_specs.append(spec())
            if k not in args_in:
                x = pltpu.with_memory_space_constraint(x, VMEM)
        args.append(x)
    size = sum(x.size * x.dtype.itemsize for x in ins)
    return pl.pallas_call(
        body,
        out_shape=tuple(
            pltpu.HBM(shape, kind)
            if k in far_outs
            else (jax.ShapeDtypeStruct if k in plain else VMEM)(shape, kind)
            for k, (shape, kind) in enumerate(outs)
        ),
        in_specs=in_specs,
        out_specs=tuple(
            pl.BlockSpec(memory_space=pltpu.HBM) if k in far_outs else spec()
            for k in range(len(outs))
        ),
        scratch_shapes=list(scratch),
        compiler_params=pltpu.CompilerParams(vmem_limit_bytes=LIMIT),
        cost_estimate=pl.CostEstimate(
            flops=flops, bytes_accessed=size, transcendentals=0
        ),
    )(*args)


def tables_call(own, feat, pos, wave, dep):
    def body(*refs):
        tables_kernel(own, *refs)

    return call(
        body,
        (feat, pos, wave, dep),
        (((HALF, 2 * C), F32), ((4 * HALF, ATOMS), BF16)),
        [
            VMEM((2 * C, ATOMS), BF16),
            VMEM((4 * HALF, ATOMS), BF16),
            VMEM((C, ATOMS), F32),
            pltpu.SemaphoreType.DMA((1 + 4 * HALF // BLOCK,)),
        ],
        4 * 10**9,
        far=(0, 3),
        far_outs=(1,),
    )


def fetched(tab_hbm, tab_ref, sems, tiles):
    copies = []
    for tile in tiles:
        rows = pl.ds(tile * CHUNK, CHUNK)
        copy = pltpu.make_async_copy(tab_hbm.at[rows], tab_ref.at[rows], sems.at[tile])
        copy.start()
        copies.append(copy)
    return copies


def ahead(next_hbm, next_ref, sem):
    copy = pltpu.make_async_copy(next_hbm.at[pl.ds(0, CHUNK)], next_ref, sem)
    copy.start()
    return copy


def cot_kernel(first, cot_ref, tab_hbm, other_ref, *rest):
    if first:
        feat_hbm, pos_hbm, sums_ref, out_ref, next_ref, rim_ref = rest[:6]
        rhs_ref, tab_ref, sems, pos_ref = rest[6:]
        out_ref[:, 0 : 2 * C] = sums_ref[...]
        out_ref = out_ref.at[:, 2 * C :]
        copies = fetched(tab_hbm, tab_ref, sems, range(TILES))
        pad = REACH * BLOCK
        tail = lax.axis_index("mode") < MODE_DEV // 2
        block = jnp.where(tail, MODE_DEV - REACH, 0)
        lanes = pl.ds(pl.multiple_of(block * BLOCK, BLOCK), pad)
        later = [
            pltpu.make_async_copy(pos_hbm, pos_ref, sems.at[TILES + 1]),
            pltpu.make_async_copy(
                feat_hbm.at[:, lanes], rim_ref.at[pl.ds(0, C)], sems.at[TILES + 2]
            ),
        ]
        for copy in later:
            copy.start()
        later.append(ahead(other_ref, next_ref, sems.at[TILES]))
        for k in range(REACH):
            rim_ref[C + 8 :, k * BLOCK : (k + 1) * BLOCK] = cot_ref[block + k]
        rim_ref[C : C + 8, :] = jnp.zeros((8, pad), F32)
    else:
        out_ref, rhs_ref, tab_ref, sems = rest
        copies = [None] + fetched(tab_hbm, tab_ref, sems, range(1, TILES))
    cot_rows(cot_ref, rhs_ref, 0, C)
    for tile in range(TILES):
        if copies[tile] is None:
            sums_tile(other_ref, rhs_ref, out_ref, tile, C)
        else:
            copies[tile].wait()
            sums_tile(tab_ref, rhs_ref, out_ref, tile, C)
    if first:
        for copy in later:
            copy.wait()
        rim_ref[C : C + 3, :] = pos_ref[:, lanes]


def cot_call(first, cot, tab, other, *more):
    def body(*refs):
        cot_kernel(first, *refs)

    outs = [((HALF, 4 * C if first else 2 * C), F32)]
    scratch = [
        VMEM((2 * C, ATOMS), BF16),
        VMEM((4 * HALF, ATOMS), BF16),
        pltpu.SemaphoreType.DMA((TILES + 3,)),
    ]
    if first:
        outs += [((CHUNK, ATOMS), BF16), ((HALO_ROWS, REACH * BLOCK), F32)]
        scratch.append(VMEM((3, ATOMS), F32))
    return call(
        body,
        (cot, tab, other, *more),
        outs,
        scratch,
        2 * 10**9,
        far=(1, 2, 3, 4) if first else (1,),
    )


def merge_kernel(feat_ref, cot_ref, got_ref, out_hbm, out_ref, sems):
    copies = []
    for k in range(8):
        rows = slice(k * SHARE, (k + 1) * SHARE)
        for trig in range(2):
            for part in range(2):
                lanes = slice((2 * trig + part) * C, (2 * trig + part + 1) * C)
                here = slice(trig * C, (trig + 1) * C)
                there = slice((2 * part + trig) * C, (2 * part + trig + 1) * C)
                own = (feat_ref, cot_ref)[part]
                out_ref[k, :, lanes] = own[rows, here] + got_ref[rows, there]
        copies.append(pltpu.make_async_copy(out_ref.at[k], out_hbm.at[k], sems.at[k]))
        copies[-1].start()
    for copy in copies:
        copy.wait()


def give_back_kernel(own, sums_ref, filt_hbm, tab_hbm, other_ref, *rest):
    if own:
        acc_ref, next_ref, filt_ref, lhs_ref, tab_ref, sems = rest
    else:
        acc_ref, out_hbm, lhs_ref, tab_ref, sems, out_ref = rest
        filt_ref = filt_hbm
    core = lax.axis_index("atom") % 2
    at = pl.multiple_of(HALF * (core if own else 1 - core), HALF)
    if own:
        mine = pl.ds(at, HALF)
        fetch = pltpu.make_async_copy(
            filt_hbm.at[:, mine], filt_ref.at[:, mine], sems.at[TILES]
        )
        fetch.start()
        copies = fetched(tab_hbm, tab_ref, sems, range(TILES))
        theirs = pl.ds(pl.multiple_of(HALF - at, HALF), HALF)
        rest_fetch = pltpu.make_async_copy(
            filt_hbm.at[:, theirs], filt_ref.at[:, theirs], sems.at[TILES + 2]
        )
        rest_fetch.start()
        later = ahead(other_ref, next_ref, sems.at[TILES + 1])
    else:
        copies = [None] + fetched(tab_hbm, tab_ref, sems, range(1, TILES))
    if own:
        fetch.wait()
    scale = 1.0 / (ATOM_DEV * ATOMS)
    for k in range(HALF // C):
        filt = filt_ref[:, pl.ds(pl.multiple_of(at + k * C, C), C)] * scale
        tile, part = divmod(k * C, TILE)
        for trig in range(2):
            lanes = pl.ds((tile * 2 + trig) * TILE + part, C)
            for row in range(2):
                sums = sums_ref[k * C : (k + 1) * C, pl.ds((2 * trig + row) * C, C)]
                high, low = pieces(filt * sums.T)
                lhs_ref[row * C : (row + 1) * C, lanes] = high
                lhs_ref[(2 + row) * C : (3 + row) * C, lanes] = low
    width = 2 * BLOCK
    stores = []
    for n in range(TILES):
        if copies[n] is not None:
            copies[n].wait()
        table = other_ref if copies[n] is None else tab_ref
        depth = slice(n * 2 * TILE, (n + 1) * 2 * TILE)
        for k in range(ATOMS // width):
            lanes = slice(k * width, (k + 1) * width)
            top = n * CHUNK
            both = dot(lhs_ref[:, depth], table[top : top + 2 * TILE, lanes], NN)
            more = dot(
                lhs_ref[0 : 2 * C, depth],
                table[top + 2 * TILE : top + CHUNK, lanes],
                NN,
            )
            part = both[: 2 * C] + both[2 * C :] + more
            if not own and n == 0:
                part = part + acc_ref[:, lanes]
            if own and n == 0:
                acc_ref[:, lanes] = part
            elif own:
                acc_ref[:, lanes] = acc_ref[:, lanes] + part
            else:
                for side in range(2):
                    half = part[:, side * BLOCK : (side + 1) * BLOCK]
                    if n:
                        half = half + out_ref[2 * k + side]
                    out_ref[2 * k + side] = half
                if n == TILES - 1:
                    pair = pl.ds(2 * k, 2)
                    stores.append(
                        pltpu.make_async_copy(
                            out_ref.at[pair], out_hbm.at[pair], sems.at[TILES + 2 + k]
                        )
                    )
                    stores[-1].start()
    for store in stores:
        store.wait()
    if own:
        rest_fetch.wait()
        later.wait()


def give_back_call(own, sums, filt, tab, other, acc=None):
    def body(*refs):
        give_back_kernel(own, *refs)

    args = [sums, filt, tab, other]
    if own:
        outs = [((2 * C, ATOMS), F32), ((CHUNK, ATOMS), BF16), ((C, MODES), F32)]
    else:
        args.append(acc)
        outs = [((MODE_DEV, 2 * C, BLOCK), F32)]
    return call(
        body,
        args,
        outs,
        [
            VMEM((4 * C, 2 * HALF), BF16),
            VMEM((4 * HALF, ATOMS), BF16),
            pltpu.SemaphoreType.DMA((TILES + 2 + ATOMS // (2 * BLOCK),)),
        ]
        + ([] if own else [VMEM(outs[0][0], F32)]),
        4 * 10**9,
        far=(1, 2, 3) if own else (2,),
        far_outs=() if own else (0,),
    )


def grad_kernel(own_ref, oth_ref, grad_ref):
    core = lax.axis_index("atom") % 2
    scale = 1.0 / (ATOM_DEV * ATOMS)
    for half in range(2):
        ref = (own_ref, oth_ref)[half]
        at = pl.multiple_of(HALF * (core if half == 0 else 1 - core), HALF)
        for k in range(HALF // C):
            rows = slice(k * C, (k + 1) * C)
            grad = (
                ref[rows, 0:C] * ref[rows, C : 2 * C]
                + ref[rows, 2 * C : 3 * C] * ref[rows, 3 * C :]
            )
            grad_ref[:, pl.ds(pl.multiple_of(at + k * C, C), C)] = grad.T * scale


def near_kernel(
    rim_ref,
    feat_ref,
    pos_ref,
    cot_ref,
    mix_hbm,
    rate_ref,
    out_ref,
    back_ref,
    ext_ref,
    rhs_ref,
    mix_ref,
    pos_vmem,
    sems,
):
    own = lax.axis_index("mode")
    pad = REACH * BLOCK
    middle = pl.ds(pad, ATOMS)
    rim_at = jnp.where(own < MODE_DEV // 2, 0, pad + ATOMS)
    moves = [
        (pos_ref, pos_vmem),
        (rim_ref, ext_ref.at[:, pl.ds(pl.multiple_of(rim_at, BLOCK), pad)]),
        (feat_ref, ext_ref.at[pl.ds(0, C), middle]),
        (mix_hbm, mix_ref),
    ]
    for k in range(MODE_DEV):
        lanes = pl.ds(pad + k * BLOCK, BLOCK)
        moves.append((cot_ref.at[k], ext_ref.at[pl.ds(C + 8, C + 8), lanes]))
    copies = [
        pltpu.make_async_copy(src, dst, sems.at[k]) for k, (src, dst) in enumerate(moves)
    ]
    for copy in copies:
        copy.start()
    for copy in copies:
        copy.wait()
    ext_ref[C : C + 3, pad : pad + ATOMS] = pos_vmem[...]
    shard = lax.axis_index("atom")
    total_blocks = ATOM_DEV * MODE_DEV

    def unit(block, row):
        return row * float(total_blocks) - block.astype(F32)

    def halves(row):
        q = row - 0.5
        y = q * q
        s = q * (
            3.14159265
            + y
            * (-5.16771276 + y * (2.55016332 + y * (-0.5992522 + y * (0.0820504 - 0.00702839 * y))))
        )
        c = 1.0 + y * (
            -4.93480214
            + y * (4.05870916 + y * (-1.335212 + y * (0.23493731 - 0.02439632 * y)))
        )
        return -s, c

    me = shard * MODE_DEV + own
    here = ext_ref[C : C + 8, pl.ds(pl.multiple_of(pad + own * BLOCK, BLOCK), BLOCK)]
    u_own = unit(me, here[0:1])
    c1, s1 = halves(here[1:2])
    c2, s2 = halves(here[2:3])
    columns = columns_of((u_own, c1, s1, c2, s2))
    wide = [jnp.broadcast_to(columns[:, k : k + 1], (BLOCK, BLOCK)) for k in range(5)]
    span = 2 * REACH + 1
    dist = []
    live = ext_ref[264:265, pl.ds(pl.multiple_of(pad + own * BLOCK, BLOCK), BLOCK)]
    for o in range(span):
        at = pl.ds(pl.multiple_of((own + o) * BLOCK, BLOCK), BLOCK)
        block = ext_ref[:, at]
        there = lax.rem(me + o - REACH + total_blocks, total_blocks)
        near = block[C : C + 8]
        x = wide[0] - (unit(there, near[0:1]) + float(o - REACH))
        d1c, d1s = halves(near[1:2])
        d2c, d2s = halves(near[2:3])
        y = x * x
        z = y * (3.14159265 / total_blocks) ** 2
        d = y * (1.0 + z * (-1.0 / 3.0 + z * (2.0 / 45.0)))
        e1 = wide[2] * d1c - wide[1] * d1s
        e2 = wide[4] * d2c - wide[3] * d2s
        d = d + (e1 * e1 + e2 * e2) * (2.0 / 3.14159265) ** 2
        dist.append(d)
        lanes = slice(o * BLOCK, (o + 1) * BLOCK)
        high, low = pieces(block[0:C] * live[0:1, o : o + 1])
        rhs_ref[0:C, lanes] = high
        rhs_ref[2 * C : 3 * C, lanes] = low
        lists_me = block[264:265, span - 1 - o : span - o]
        high, low = pieces(block[136 : 136 + C] * lists_me)
        rhs_ref[C : 2 * C, lanes] = high
        rhs_ref[3 * C :, lanes] = low
    out = ext_ref[0:C, pl.ds(pl.multiple_of(pad + own * BLOCK, BLOCK), BLOCK)]
    back = ext_ref[136 : 136 + C, pl.ds(pl.multiple_of(pad + own * BLOCK, BLOCK), BLOCK)]
    for r in range(RADIAL):
        rate = rate_ref[r]
        highs, lows = [], []
        for o in range(span):
            high, low = pieces(jnp.exp(dist[o] * -rate))
            highs.append(high)
            lows.append(low)
        weights_high = jnp.concatenate(highs, axis=1)
        weights_low = jnp.concatenate(lows, axis=1)
        both = dot(rhs_ref[...], weights_high, NT)
        got = (
            both[: 2 * C]
            + both[2 * C :]
            + dot(rhs_ref[0 : 2 * C, :], weights_low, NT)
        )
        high, low = pieces(got)
        mix = mix_ref[r]
        mh, ml = pieces(mix)
        th, tl = pieces(mix.T)
        out = out + (
            dot(th, high[:C], NN) + dot(th, low[:C], NN) + dot(tl, high[:C], NN)
        )
        back = back + (
            dot(mh, high[C:], NN) + dot(mh, low[C:], NN) + dot(ml, high[C:], NN)
        )
    out_ref[...] = out
    back_ref[...] = back


def near_call(rim, feat, pos, cot, mix, rates):
    return call(
        near_kernel,
        (rim, feat, pos, cot, mix, rates),
        (((C, BLOCK), F32), ((C, BLOCK), F32)),
        [
            VMEM((HALO_ROWS, ATOMS + 2 * REACH * BLOCK), F32),
            VMEM((4 * C, (2 * REACH + 1) * BLOCK), BF16),
            VMEM((RADIAL, C, C), F32),
            VMEM((3, ATOMS), F32),
            pltpu.SemaphoreType.DMA((4 + MODE_DEV,)),
        ],
        2 * 10**9,
        smem=(5,),
        any_in=(0, 1, 2, 3, 4),
    )


def pack_kernel(ids_hbm, live_ref, cot_hbm, pos_hbm, wave_hbm, *rest):
    out_hbm, pos_ref, wave_ref, ids_ref, pack_ref, sems = rest
    fetches = [
        pltpu.make_async_copy(cot_hbm, pack_ref.at[pl.ds(0, C)], sems.at[MODE_DEV]),
        pltpu.make_async_copy(ids_hbm, ids_ref, sems.at[MODE_DEV + 1]),
        pltpu.make_async_copy(pos_hbm, pos_ref, sems.at[MODE_DEV + 2]),
        pltpu.make_async_copy(wave_hbm, wave_ref, sems.at[MODE_DEV + 3]),
    ]
    for fetch in fetches:
        fetch.start()
    total_blocks = ATOM_DEV * MODE_DEV
    me = lax.axis_index("atom") * MODE_DEV + lax.axis_index("mode")
    lane = lax.broadcasted_iota(jnp.int32, (8, BLOCK), 1)
    live = jnp.zeros((8, BLOCK), F32)
    fetches[1].wait()
    for slot in range(SLOTS):
        offset = lax.rem(ids_ref[0, slot] - me + REACH + total_blocks, total_blocks)
        offset = jnp.where(slot < live_ref[0], offset, BLOCK)
        live = jnp.where(lane == offset, 1.0, live)
    pack_ref[C:, :] = live
    fetches[0].wait()
    copies = [
        pltpu.make_async_copy(pack_ref, out_hbm.at[k], sems.at[k]) for k in range(MODE_DEV)
    ]
    for copy in copies:
        copy.start()
    for copy in copies + fetches[2:]:
        copy.wait()


def share_kernel(parts_ref, out_ref):
    share = parts_ref[0]
    for k in range(1, ATOM_DEV // 2):
        share = share + parts_ref[k]
    for k in range(ATOM_DEV // 2):
        out_ref[k] = share


def finish_kernel(near_ref, back_ref, parts_ref, out_ref, grad_ref):
    out = near_ref[...]
    grad = back_ref[...]
    for k in range(MODE_DEV):
        out = out + parts_ref[k, 0:C]
        grad = grad + parts_ref[k, C:]
    out_ref[...] = out
    grad_ref[...] = grad


def per_device(
    features,
    positions,
    wavevectors,
    mode_filter,
    radial_mix,
    radial_rates,
    neighbour_ids,
    live_counts,
    cotangent,
):
    core_swap = [(i, i ^ 1) for i in range(ATOM_DEV)]
    chips = [[c + 2 * i for i in range(ATOM_DEV // 2)] for c in range(2)]
    rims = []
    for i in range(ATOM_DEV):
        for m in range(REACH):
            after = (i + 1) % ATOM_DEV
            rims.append((i * MODE_DEV + m, after * MODE_DEV + m))
            last = MODE_DEV - 1 - m
            rims.append((after * MODE_DEV + last, i * MODE_DEV + last))

    def exchange(x):
        return lax.all_to_all(x, "atom", 0, 0, axis_index_groups=chips, tiled=True)

    packed, pos_near, wave_near = call(
        pack_kernel,
        (neighbour_ids, live_counts, cotangent, positions, wavevectors),
        (
            ((MODE_DEV, C + 8, BLOCK), F32),
            (positions.shape, F32),
            (wavevectors.shape, jnp.int32),
        ),
        [
            pltpu.SMEM((1, SLOTS), jnp.int32),
            VMEM((C + 8, BLOCK), F32),
            pltpu.SemaphoreType.DMA((MODE_DEV + 4,)),
        ],
        smem=(1,),
        far=(0, 2, 3, 4),
        far_outs=(0,),
    )
    cot = lax.all_to_all(packed, "mode", 0, 0, tiled=True)

    f_own, tab_own = tables_call(True, features, pos_near, wave_near, packed)
    f_oth, tab_oth = tables_call(False, features, pos_near, wave_near, tab_own)
    cot, f_oth = lax.optimization_barrier((cot, f_oth))
    oth, tab_next, rim = cot_call(
        True, cot, tab_oth, tab_own, features, positions, f_oth
    )
    rim = lax.ppermute(rim, ("atom", "mode"), rims)
    got = lax.ppermute(oth, "atom", core_swap)
    cot, oth = lax.optimization_barrier((cot, oth))
    (c_own,) = cot_call(False, cot, tab_own, tab_next)
    (parts,) = call(
        merge_kernel,
        (f_own, c_own, got),
        (((8, SHARE, 4 * C), F32),),
        [VMEM((8, SHARE, 4 * C), F32), pltpu.SemaphoreType.DMA((8,))],
        far_outs=(0,),
    )
    parts = exchange(parts)
    (share,) = call(share_kernel, (parts,), ((parts.shape, F32),))
    own = exchange(share).reshape(HALF, 4 * C)
    oth = lax.ppermute(own, "atom", core_swap)
    acc, tab_next, filt = give_back_call(True, own, mode_filter, tab_own, tab_oth)
    (back,) = give_back_call(False, oth, filt, tab_oth, tab_next, acc)
    back, cot, rim = lax.optimization_barrier((back, cot, rim))
    near_out, near_back = near_call(
        rim, features, positions, cot, radial_mix, radial_rates
    )
    back = lax.all_to_all(back, "mode", 0, 0, tiled=True)
    (grad_filter,) = call(
        grad_kernel, (own, oth), (((C, MODES), F32),), plain=(0,), args_in=(0, 1)
    )
    layer_out, grad_features = call(
        finish_kernel,
        (near_out, near_back, back),
        (((C, BLOCK), F32), ((C, BLOCK), F32)),
        plain=(0, 1),
        args_in=(0, 1),
    )
    return (layer_out, grad_features, grad_filter)


def solution(mesh):
    in_specs = (
        P(None, "atom"),
        P(None, "atom"),
        P(None, "mode"),
        P(None, "mode"),
        P(),
        P(),
        P(("atom", "mode"), None),
        P(("atom", "mode")),
        P(None, ("atom", "mode")),
    )
    out_specs = (P(None, ("atom", "mode")), P(None, ("atom", "mode")), P(None, "mode"))
    return jax.shard_map(
        per_device, mesh=mesh, in_specs=in_specs, out_specs=out_specs, check_vma=False
    )
```
